256 devices in a mesh: frame: 16 (over y_hi, x, core), head: 16 (over y_lo, z).
Axes of the slice: x: 4, y: 4 (y_hi: 2, y_lo: 2; y = y_hi * 2 + y_lo), z: 8, core: 2. Of those that a mesh axis runs over, the one named last changes fastest.
Arguments:
- queries: bfloat16 [32768, 2048], P('frame', 'head'), may hold values from -64 to 64
- keys: bfloat16 [32768, 2048], P('frame', 'head'), may hold values from -4 to 4
- values: bfloat16 [32768, 2048], P('frame', 'head'), may hold values from -6 to 6
- block_mask: int32 [16, 16, 32, 45], P('head', 'frame'), may hold values 0 or 1
- out_weight: bfloat16 [2048, 3072], P('head'), may hold values from -1 to 1
Outputs:
- projected: bfloat16 [32768, 3072], P(('frame', 'head'))
The draws below stay inside these ranges and needn't reach their ends.
All inputs are finite; a program needn't handle non-finite values. No bound on the sum of `block_mask` on one device may be relied on, other than what follows from the above.
Results may differ from the reference program's by a relative error of at most 0.018.
Values may be sent and summed in bfloat16 or wider, within the bound.
A program may use at most 128 MiB of HBM per device.

```python
import math
import jax
import jax.numpy as jnp
from jax import lax

D = 3072
HEAD_DIM = 128
HEADS = 16
TROWS = 4
TCOLS = 8
WIN = 45
TILE = 64
FRAMES = 16
TOKENS = 32768


def shared_pair(key):
    width = HEADS * HEAD_DIM
    key_base = jnp.clip(jax.random.normal(jax.random.fold_in(key, 11), (TOKENS, width), jnp.float32), -4.0, 4.0)
    query_base = jnp.clip(2.0 * jax.random.normal(jax.random.fold_in(key, 12), (TOKENS, width), jnp.float32), -8.0, 8.0)
    return (query_base, key_base)


def draw_queries(key, part):
    query_base, key_base = shared_pair(key)
    return query_base.astype(jnp.bfloat16)


def draw_keys(key, part):
    query_base, key_base = shared_pair(key)
    return key_base.astype(jnp.bfloat16)


def plant(values, stream_key, smallest, high):
    longest = values.shape.index(max(values.shape))
    spots = []
    for shift in (0, 1):
        where = [jax.random.randint(jax.random.fold_in(stream_key, axis), (), 0, length) for axis, length in enumerate(values.shape)]
        where[longest] = (where[longest] + shift) % values.shape[longest]
        spots.append(tuple(where))
    return values.at[spots[0]].set(smallest).at[spots[1]].set(high)


def levels(rng, extent, pieces, smallest, largest):
    loudness, own = 1.0, jax.random.fold_in(rng, 6)
    for position, shards_of in pieces:
        draws = jnp.exp(jax.random.uniform(jax.random.fold_in(own, position), (shards_of,), jnp.float32, smallest / len(pieces), largest / len(pieces)))
        loudness = loudness * jnp.repeat(draws, extent[position] // shards_of).reshape([-1 if axis == position else 1 for axis in range(len(extent))])
    return loudness


def centred(key, dims, spread, reach, split=(), held_as=jnp.bfloat16):
    gain = levels(key, dims, split, -0.22, 0.18) if split else 1.0
    array = jax.random.normal(key, dims, jnp.float32) * spread * gain
    return jnp.minimum(jnp.maximum(array, -reach), reach).astype(held_as)


def setup_inputs(seed: int = 0) -> dict:
    arg_keys = jax.random.split(jax.random.key(seed), 6)
    queries = draw_queries(jax.random.fold_in(arg_keys[5], 71), 0)
    keys = draw_keys(jax.random.fold_in(arg_keys[5], 71), 0)
    values = centred(arg_keys[2], (TOKENS, HEADS * HEAD_DIM), 1.0, 6.0, ((0, 16), (1, 16)))
    block_mask = plant((jax.random.randint(arg_keys[3], (HEADS, FRAMES, TROWS * TCOLS, WIN), 0, 4) < 3).astype(jnp.int32), jax.random.fold_in(arg_keys[3], 1), 0, 1)
    out_weight = centred(arg_keys[4], (HEADS * HEAD_DIM, D), (HEADS * HEAD_DIM // 64) ** -0.5, 1.0, ((0, 16),))
    return dict(queries=queries, keys=keys, values=values, block_mask=block_mask, out_weight=out_weight)


def tile_allowed(mask_rows, frame, row, frames_total):
    frame_step = jnp.arange(3, dtype=jnp.int32)[None, :, None, None]
    row_step = jnp.arange(3, dtype=jnp.int32)[None, None, :, None]
    query_col = jnp.arange(TCOLS, dtype=jnp.int32)[:, None, None, None]
    key_col = jnp.arange(TCOLS, dtype=jnp.int32)[None, None, None, :]
    col_step = key_col - query_col
    offset = frame_step * 15 + row_step * 5 + col_step + 2
    picked = offset[..., None] == jnp.arange(WIN, dtype=jnp.int32)
    chosen = lax.optimization_barrier(jnp.sum(jnp.where(picked, mask_rows[:, None, None, None, :], 0), axis=-1)) > 0
    centre = (frame_step == 1) & (row_step == 1) & (col_step == 0)
    key_frame = frame + frame_step - 1
    key_row = row + row_step - 1
    inside = (key_frame >= 0) & (key_frame < frames_total) & (key_row >= 0) & (key_row < TROWS)
    nearby = jnp.abs(col_step) <= 2
    allowed = (chosen | centre) & nearby & inside
    expanded = jnp.broadcast_to(allowed[:, None, :, :, :, None], (TCOLS, TILE, 3, 3, TCOLS, TILE))
    return expanded.reshape(TCOLS * TILE, 9 * TCOLS * TILE)

def attend_block(query_block, key_block, value_block, allowed):
    scale = 1.0 / math.sqrt(HEAD_DIM)
    scores = jnp.dot(query_block, key_block.T, preferred_element_type=jnp.float32) * scale
    scores = jnp.where(allowed, scores, -jnp.inf)
    peak = lax.optimization_barrier(jnp.max(scores, axis=1, keepdims=True))
    expos = jnp.exp(scores - peak)
    weights = (expos / lax.optimization_barrier(jnp.sum(expos, axis=1, keepdims=True))).astype(jnp.bfloat16)
    return jnp.dot(weights, value_block, preferred_element_type=jnp.float32).astype(jnp.bfloat16)

def reference(queries, keys, values, block_mask, out_weight):
    span = TCOLS * TILE
    query_grid = queries.reshape(FRAMES, TROWS, span, HEADS, HEAD_DIM)
    pair = jnp.stack([keys, values]).reshape(2, FRAMES, TROWS, span, HEADS, HEAD_DIM)
    padded = jnp.pad(pair, ((0, 0), (1, 1), (1, 1), (0, 0), (0, 0), (0, 0)))
    mask_grid = block_mask.reshape(HEADS, FRAMES, TROWS, TCOLS, WIN)

    def one_block(which):
        head = (which // (FRAMES * TROWS)).astype(jnp.int32)
        frame = (which // TROWS % FRAMES).astype(jnp.int32)
        row = (which % TROWS).astype(jnp.int32)
        zero = jnp.zeros((), jnp.int32)
        query_block = lax.dynamic_slice(query_grid, (frame, row, zero, head, zero), (1, 1, span, 1, HEAD_DIM)).reshape(span, HEAD_DIM)
        pair_block = lax.dynamic_slice(padded, (zero, frame, row, zero, head, zero), (2, 3, 3, span, 1, HEAD_DIM)).reshape(2, 9 * span, HEAD_DIM)
        mask_rows = lax.dynamic_slice(mask_grid, (head, frame, row, zero, zero), (1, 1, 1, TCOLS, WIN)).reshape(TCOLS, WIN)
        allowed = tile_allowed(mask_rows, frame, row, FRAMES)
        return attend_block(query_block, pair_block[0], pair_block[1], allowed)
    blocks = lax.map(one_block, jnp.arange(HEADS * FRAMES * TROWS, dtype=jnp.int32))
    attention = blocks.reshape(HEADS, FRAMES, TROWS, span, HEAD_DIM).transpose(1, 2, 3, 0, 4).reshape(TOKENS, HEADS * HEAD_DIM)
    return jnp.dot(attention, out_weight, preferred_element_type=jnp.float32).astype(jnp.bfloat16)
```

```python
import math

import jax
import jax.numpy as jnp
from jax import lax
from jax.sharding import PartitionSpec as P

HEAD_DIM = 128
TROWS = 4
TCOLS = 8
WIN = 45
TILE = 64


def padded_2(block, sides, width):
    for axis, dim in sides:
        count = lax.axis_size(axis)
        forward = [(i, i + 1) for i in range(count - 1)]
        backward = [(target, source) for source, target in forward]
        low = lax.ppermute(
            lax.slice_in_dim(block, block.shape[dim] - width, None, axis=dim), axis, forward
        )
        high = lax.ppermute(lax.slice_in_dim(block, 0, width, axis=dim), axis, backward)
        block = jnp.concatenate([low, block, high], axis=dim)
    return block


def tile_allowed(mask_rows, frame, row, frames_total):
    frame_step = jnp.arange(3, dtype=jnp.int32)[None, :, None, None]
    row_step = jnp.arange(3, dtype=jnp.int32)[None, None, :, None]
    query_col = jnp.arange(TCOLS, dtype=jnp.int32)[:, None, None, None]
    key_col = jnp.arange(TCOLS, dtype=jnp.int32)[None, None, None, :]
    col_step = key_col - query_col
    offset = frame_step * 15 + row_step * 5 + col_step + 2
    picked = offset[..., None] == jnp.arange(WIN, dtype=jnp.int32)
    chosen = jnp.sum(jnp.where(picked, mask_rows[:, None, None, None, :], 0), axis=-1) > 0
    centre = (frame_step == 1) & (row_step == 1) & (col_step == 0)
    key_frame = frame + frame_step - 1
    key_row = row + row_step - 1
    inside = (key_frame >= 0) & (key_frame < frames_total) & (key_row >= 0) & (key_row < TROWS)
    nearby = jnp.abs(col_step) <= 2
    allowed = (chosen | centre) & nearby & inside
    expanded = jnp.broadcast_to(allowed[:, None, :, :, :, None], (TCOLS, TILE, 3, 3, TCOLS, TILE))
    return expanded.reshape(TCOLS * TILE, 9 * TCOLS * TILE)


def attend_block(query_block, key_block, value_block, allowed):
    scale = 1.0 / math.sqrt(HEAD_DIM)
    scores = jnp.dot(query_block, key_block.T, preferred_element_type=jnp.float32) * scale
    scores = jnp.where(allowed, scores, -jnp.inf)
    peak = jnp.max(scores, axis=1, keepdims=True)
    expos = jnp.exp(scores - peak)
    weights = (expos / jnp.sum(expos, axis=1, keepdims=True)).astype(jnp.bfloat16)
    return jnp.dot(weights, value_block, preferred_element_type=jnp.float32).astype(jnp.bfloat16)


def on_device(queries, keys, values, block_mask, out_weight):
    span = TCOLS * TILE
    tok_dev = queries.shape[0]
    width = queries.shape[1]
    heads_here = width // HEAD_DIM
    frames_here = tok_dev // (TROWS * span)
    frames_total = frames_here * lax.axis_size("frame")
    first_frame = lax.axis_index("frame") * frames_here
    pair = jnp.stack([keys, values]).reshape(2, frames_here, TROWS, span, width)
    padded = padded_2(pair, (("frame", 1),), 1)
    padded = jnp.pad(padded, ((0, 0), (0, 0), (1, 1), (0, 0), (0, 0)))
    query_grid = queries.reshape(frames_here, TROWS, span, width)
    mask_grid = block_mask.reshape(heads_here, frames_here, TROWS, TCOLS, WIN)

    def one_block(which):
        head = which // (frames_here * TROWS)
        frame = which // TROWS % frames_here
        row = which % TROWS
        zero = jnp.zeros((), jnp.int32)
        column = head * HEAD_DIM
        query_block = lax.dynamic_slice(
            query_grid, (frame, row, zero, column), (1, 1, span, HEAD_DIM)
        ).reshape(span, HEAD_DIM)
        pair_block = lax.dynamic_slice(
            padded, (zero, frame, row, zero, column), (2, 3, 3, span, HEAD_DIM)
        ).reshape(2, 9 * span, HEAD_DIM)
        mask_rows = lax.dynamic_slice(
            mask_grid, (head, frame, row, zero, zero), (1, 1, 1, TCOLS, WIN)
        ).reshape(TCOLS, WIN)
        allowed = tile_allowed(mask_rows, first_frame + frame, row, frames_total)
        return attend_block(query_block, pair_block[0], pair_block[1], allowed)

    blocks = lax.map(one_block, jnp.arange(heads_here * frames_here * TROWS, dtype=jnp.int32))
    attention = (
        blocks.reshape(heads_here, frames_here, TROWS, span, HEAD_DIM)
        .transpose(1, 2, 3, 0, 4)
        .reshape(tok_dev, width)
    )
    full_weight = lax.all_gather(out_weight, "head", axis=0, tiled=True)
    gathered = lax.all_to_all(attention, "head", 0, 1, tiled=True)
    return jnp.dot(gathered, full_weight, preferred_element_type=jnp.float32).astype(jnp.bfloat16)


def solution(mesh):
    return jax.shard_map(
        on_device,
        mesh=mesh,
        in_specs=(
            P("frame", "head"),
            P("frame", "head"),
            P("frame", "head"),
            P("head", "frame", None, None),
            P("head", None),
        ),
        out_specs=P(("frame", "head"), None),
        check_vma=False,
    )
```

```python
import math

import numpy as np
import jax
import jax.numpy as jnp
from jax import lax
from jax.experimental import pallas as pl
from jax.experimental.pallas import tpu as pltpu
from jax.sharding import PartitionSpec as P

HEAD_DIM = 128
TROWS = 4
TCOLS = 8
WIN = 45
TILE = 64
QTILES = 2
KCOLS = 6
SEGS = 9
BLOCK_Q = QTILES * TILE
SEG_K = KCOLS * TILE
ROW_K = SEGS * SEG_K
GROUPS = TCOLS // QTILES


def window_tables():
    shape = (TROWS * GROUPS, QTILES, SEGS, KCOLS)
    qtile = np.zeros(shape, np.int32)
    offset = np.zeros(shape, np.int32)
    static_ok = np.zeros(shape, bool)
    centre = np.zeros(shape, bool)
    frame_step = np.zeros(shape, np.int32)
    for row in range(TROWS):
        for group in range(GROUPS):
            start = min(max(QTILES * group - 2, 0), TCOLS - KCOLS)
            for a in range(QTILES):
                col = QTILES * group + a
                for seg in range(SEGS):
                    df, dr = divmod(seg, 3)
                    for j in range(KCOLS):
                        dc = start + j - col
                        b = row * GROUPS + group
                        qtile[b, a, seg, j] = row * TCOLS + col
                        ok = abs(dc) <= 2 and 0 <= row + dr - 1 < TROWS
                        static_ok[b, a, seg, j] = ok
                        offset[b, a, seg, j] = 15 * df + 5 * dr + dc + 2 if ok else 0
                        centre[b, a, seg, j] = df == 1 and dr == 1 and dc == 0
                        frame_step[b, a, seg, j] = df - 1
    return qtile, offset, static_ok, centre, frame_step


def window_bias(mask_rows, frame, frames_total):
    qtile, offset, static_ok, centre, frame_step = window_tables()
    chosen = mask_rows[qtile, offset] > 0
    key_frame = frame + frame_step
    inside = (key_frame >= 0) & (key_frame < frames_total)
    allowed = (chosen | centre) & static_ok & inside
    bias = jnp.where(allowed, 0.0, -jnp.inf).astype(jnp.float32)
    bias = jnp.broadcast_to(bias[..., None], bias.shape + (TILE,))
    return bias.reshape(TROWS * GROUPS, QTILES, ROW_K)


def attention_kernel(q_ref, kp_ref, k_ref, kn_ref, vp_ref, v_ref, vn_ref, bias_ref, o_ref,
                     s_ref, p_ref):
    row = pl.program_id(0)
    group = pl.program_id(1)
    start = jnp.clip(QTILES * group - 2, 0, TCOLS - KCOLS) * TILE
    key_refs = (kp_ref, k_ref, kn_ref)
    value_refs = (vp_ref, v_ref, vn_ref)
    q = q_ref[...]
    bases = []
    for seg in range(SEGS):
        df, dr = divmod(seg, 3)
        key_row = jnp.clip(row + dr - 1, 0, TROWS - 1)
        base = pl.multiple_of(key_row * (TCOLS * TILE) + start, TILE)
        bases.append(base)
        k = key_refs[df][pl.ds(base, SEG_K), :]
        s_ref[:, seg * SEG_K:(seg + 1) * SEG_K] = lax.dot_general(
            q, k, (((1,), (1,)), ((), ())), preferred_element_type=jnp.float32
        )
    scale = 1.0 / math.sqrt(HEAD_DIM)
    for a in range(QTILES):
        rows = slice(a * TILE, (a + 1) * TILE)
        scores = s_ref[rows, :] * scale + bias_ref[0, a:a + 1, :]
        peak = jnp.max(scores, axis=1, keepdims=True)
        expos = jnp.exp(scores - peak)
        total = jnp.sum(expos, axis=1, keepdims=True)
        p_ref[rows, :] = (expos * (1.0 / total)).astype(jnp.bfloat16)
    acc = jnp.zeros((BLOCK_Q, HEAD_DIM), jnp.float32)
    for seg in range(SEGS):
        df, dr = divmod(seg, 3)
        v = value_refs[df][pl.ds(bases[seg], SEG_K), :]
        acc += jnp.dot(p_ref[:, seg * SEG_K:(seg + 1) * SEG_K], v,
                       preferred_element_type=jnp.float32)
    o_ref[...] = acc.astype(o_ref.dtype)


def attend(q, kp, k, kn, vp, v, vn, bias):
    tokens = q.shape[0]
    full = pl.BlockSpec((tokens, HEAD_DIM), lambda r, g: (0, 0))
    return pl.pallas_call(
        attention_kernel,
        grid=(TROWS, GROUPS),
        in_specs=[pl.BlockSpec((BLOCK_Q, HEAD_DIM), lambda r, g: (r * GROUPS + g, 0))]
        + [full] * 6
        + [pl.BlockSpec((1, QTILES, ROW_K), lambda r, g: (r * GROUPS + g, 0, 0))],
        out_specs=pl.BlockSpec((BLOCK_Q, HEAD_DIM), lambda r, g: (r * GROUPS + g, 0)),
        out_shape=jax.ShapeDtypeStruct((tokens, HEAD_DIM), jnp.bfloat16),
        scratch_shapes=[
            pltpu.VMEM((BLOCK_Q, ROW_K), jnp.float32),
            pltpu.VMEM((BLOCK_Q, ROW_K), jnp.bfloat16),
        ],
    )(q, kp, k, kn, vp, v, vn, bias)


def on_device(queries, keys, values, block_mask, out_weight):
    tok_dev = queries.shape[0]
    frames_here = tok_dev // (TROWS * TCOLS * TILE)
    assert frames_here == 1 and queries.shape[1] == HEAD_DIM
    count = lax.axis_size("frame")
    frames_total = frames_here * count
    frame = lax.axis_index("frame") * frames_here
    forward = [(i, i + 1) for i in range(count - 1)]
    backward = [(t, s) for s, t in forward]
    pair = jnp.stack([keys, values])
    prev = lax.ppermute(pair, "frame", forward)
    nxt = lax.ppermute(pair, "frame", backward)
    mask_rows = block_mask.reshape(TROWS * TCOLS, WIN)
    bias = window_bias(mask_rows, frame, frames_total)
    attention = attend(queries, prev[0], keys, nxt[0], prev[1], values, nxt[1], bias)
    full_weight = lax.all_gather(out_weight, "head", axis=0, tiled=True)
    gathered = lax.all_to_all(attention, "head", 0, 1, tiled=True)
    return jnp.dot(gathered, full_weight, preferred_element_type=jnp.float32).astype(jnp.bfloat16)


def solution(mesh):
    return jax.shard_map(
        on_device,
        mesh=mesh,
        in_specs=(
            P("frame", "head"),
            P("frame", "head"),
            P("frame", "head"),
            P("head", "frame", None, None),
            P("head", None),
        ),
        out_specs=P(("frame", "head"), None),
        check_vma=False,
    )
```

```python
import math

import numpy as np
import jax
import jax.numpy as jnp
from jax import lax
from jax.experimental import pallas as pl
from jax.experimental.pallas import tpu as pltpu
from jax.sharding import PartitionSpec as P

HEAD_DIM = 128
TROWS = 4
TCOLS = 8
WIN = 45
TILE = 64
QTILES = 2
KCOLS = 6
SEGS = 9
BLOCK_Q = QTILES * TILE
SEG_K = KCOLS * TILE
ROW_K = SEGS * SEG_K
GROUPS = TCOLS // QTILES


def window_tables():
    shape = (TROWS * GROUPS, QTILES, SEGS, KCOLS)
    qtile = np.zeros(shape, np.int32)
    offset = np.zeros(shape, np.int32)
    static_ok = np.zeros(shape, bool)
    centre = np.zeros(shape, bool)
    frame_step = np.zeros(shape, np.int32)
    for row in range(TROWS):
        for group in range(GROUPS):
            start = min(max(QTILES * group - 2, 0), TCOLS - KCOLS)
            for a in range(QTILES):
                col = QTILES * group + a
                for seg in range(SEGS):
                    df, dr = divmod(seg, 3)
                    for j in range(KCOLS):
                        dc = start + j - col
                        b = row * GROUPS + group
                        qtile[b, a, seg, j] = row * TCOLS + col
                        ok = abs(dc) <= 2 and 0 <= row + dr - 1 < TROWS
                        static_ok[b, a, seg, j] = ok
                        offset[b, a, seg, j] = 15 * df + 5 * dr + dc + 2 if ok else 0
                        centre[b, a, seg, j] = df == 1 and dr == 1 and dc == 0
                        frame_step[b, a, seg, j] = df - 1
    return qtile, offset, static_ok, centre, frame_step


def window_bias(mask_rows, frame, frames_total):
    qtile, offset, static_ok, centre, frame_step = window_tables()
    chosen = mask_rows[qtile, offset] > 0
    key_frame = frame + frame_step
    inside = (key_frame >= 0) & (key_frame < frames_total)
    allowed = (chosen | centre) & static_ok & inside
    bias = jnp.where(allowed, 0.0, -jnp.inf).astype(jnp.float32)
    bias = jnp.broadcast_to(bias[..., None], bias.shape + (TILE,))
    return bias.reshape(TROWS * GROUPS, QTILES, ROW_K)


def attention_kernel(q_ref, kp_ref, k_ref, kn_ref, vp_ref, v_ref, vn_ref, bias_ref, o_ref,
                     s_ref, p_ref):
    row = pl.program_id(0)
    group = pl.program_id(1)
    start = jnp.clip(QTILES * group - 2, 0, TCOLS - KCOLS) * TILE
    key_refs = (kp_ref, k_ref, kn_ref)
    value_refs = (vp_ref, v_ref, vn_ref)
    q = q_ref[...]
    bases = []
    for seg in range(SEGS):
        df, dr = divmod(seg, 3)
        key_row = jnp.clip(row + dr - 1, 0, TROWS - 1)
        base = pl.multiple_of(key_row * (TCOLS * TILE) + start, TILE)
        bases.append(base)
        k = key_refs[df][pl.ds(base, SEG_K), :]
        s_ref[:, seg * SEG_K:(seg + 1) * SEG_K] = lax.dot_general(
            q, k, (((1,), (1,)), ((), ())), preferred_element_type=jnp.float32
        )
    scale = 1.0 / math.sqrt(HEAD_DIM)
    for a in range(QTILES):
        rows = slice(a * TILE, (a + 1) * TILE)
        scores = s_ref[rows, :] * scale + bias_ref[0, a:a + 1, :]
        peak = jnp.max(scores, axis=1, keepdims=True)
        expos = jnp.exp(scores - peak)
        total = jnp.sum(expos, axis=1, keepdims=True)
        p_ref[rows, :] = (expos * (1.0 / total)).astype(jnp.bfloat16)
    acc = jnp.zeros((BLOCK_Q, HEAD_DIM), jnp.float32)
    for seg in range(SEGS):
        df, dr = divmod(seg, 3)
        v = value_refs[df][pl.ds(bases[seg], SEG_K), :]
        acc += jnp.dot(p_ref[:, seg * SEG_K:(seg + 1) * SEG_K], v,
                       preferred_element_type=jnp.float32)
    o_ref[...] = acc.astype(o_ref.dtype)


def attend(q, kp, k, kn, vp, v, vn, bias):
    tokens = q.shape[0]
    full = pl.BlockSpec((tokens, HEAD_DIM), lambda r, g: (0, 0))
    return pl.pallas_call(
        attention_kernel,
        grid=(TROWS, GROUPS),
        in_specs=[pl.BlockSpec((BLOCK_Q, HEAD_DIM), lambda r, g: (r * GROUPS + g, 0))]
        + [full] * 6
        + [pl.BlockSpec((1, QTILES, ROW_K), lambda r, g: (r * GROUPS + g, 0, 0))],
        out_specs=pl.BlockSpec((BLOCK_Q, HEAD_DIM), lambda r, g: (r * GROUPS + g, 0)),
        out_shape=jax.ShapeDtypeStruct((tokens, HEAD_DIM), jnp.bfloat16),
        scratch_shapes=[
            pltpu.VMEM((BLOCK_Q, ROW_K), jnp.float32),
            pltpu.VMEM((BLOCK_Q, ROW_K), jnp.bfloat16),
        ],
    )(q, kp, k, kn, vp, v, vn, bias)


def on_device(queries, keys, values, block_mask, out_weight):
    tok_dev = queries.shape[0]
    frames_here = tok_dev // (TROWS * TCOLS * TILE)
    assert frames_here == 1 and queries.shape[1] == HEAD_DIM
    count = lax.axis_size("frame")
    frames_total = frames_here * count
    frame = lax.axis_index("frame") * frames_here
    forward = [(i, i + 1) for i in range(count - 1)]
    backward = [(t, s) for s, t in forward]
    pair = jnp.stack([keys, values])
    prev = lax.ppermute(pair, "frame", forward)
    nxt = lax.ppermute(pair, "frame", backward)
    mask_rows = block_mask.reshape(TROWS * TCOLS, WIN)
    bias = window_bias(mask_rows, frame, frames_total)
    attention = attend(queries, prev[0], keys, nxt[0], prev[1], values, nxt[1], bias)
    core = lax.axis_index("frame") % 2
    half = out_weight.shape[1] // 2
    partners = [(i, i ^ 1) for i in range(count)]
    weight_half = lax.dynamic_slice_in_dim(out_weight, core * half, half, axis=1)
    weight_half = lax.all_gather(weight_half, "head", axis=0, tiled=True)
    mine = lax.all_to_all(attention, "head", 0, 1, tiled=True)
    theirs = lax.ppermute(mine, "frame", partners)
    project = lambda x: jnp.dot(x, weight_half, preferred_element_type=jnp.float32).astype(jnp.bfloat16)
    own_half = project(mine)
    other_half = lax.ppermute(project(theirs), "frame", partners)
    return jnp.where(
        core == 0,
        jnp.concatenate([own_half, other_half], axis=1),
        jnp.concatenate([other_half, own_half], axis=1),
    )


def solution(mesh):
    return jax.shard_map(
        on_device,
        mesh=mesh,
        in_specs=(
            P("frame", "head"),
            P("frame", "head"),
            P("frame", "head"),
            P("head", "frame", None, None),
            P("head", None),
        ),
        out_specs=P(("frame", "head"), None),
        check_vma=False,
    )
```

```python
import math

import numpy as np
import jax
import jax.numpy as jnp
from jax import lax
from jax.experimental import pallas as pl
from jax.experimental.pallas import tpu as pltpu
from jax.sharding import PartitionSpec as P

HEAD_DIM = 128
TROWS = 4
TCOLS = 8
WIN = 45
TILE = 64
QTILES = 2
KCOLS = 6
SEGS = 9
BLOCK_Q = QTILES * TILE
SEG_K = KCOLS * TILE
ROW_K = SEGS * SEG_K
GROUPS = TCOLS // QTILES


def window_tables():
    shape = (TROWS * GROUPS, QTILES, SEGS, KCOLS)
    qtile = np.zeros(shape, np.int32)
    offset = np.zeros(shape, np.int32)
    static_ok = np.zeros(shape, bool)
    centre = np.zeros(shape, bool)
    frame_step = np.zeros(shape, np.int32)
    for row in range(TROWS):
        for group in range(GROUPS):
            start = min(max(QTILES * group - 2, 0), TCOLS - KCOLS)
            for a in range(QTILES):
                col = QTILES * group + a
                for seg in range(SEGS):
                    df, dr = divmod(seg, 3)
                    for j in range(KCOLS):
                        dc = start + j - col
                        b = row * GROUPS + group
                        qtile[b, a, seg, j] = row * TCOLS + col
                        ok = abs(dc) <= 2 and 0 <= row + dr - 1 < TROWS
                        static_ok[b, a, seg, j] = ok
                        offset[b, a, seg, j] = 15 * df + 5 * dr + dc + 2 if ok else 0
                        centre[b, a, seg, j] = df == 1 and dr == 1 and dc == 0
                        frame_step[b, a, seg, j] = df - 1
    return qtile, offset, static_ok, centre, frame_step


def window_bias(mask_rows, frame, frames_total):
    qtile, offset, static_ok, centre, frame_step = window_tables()
    chosen = mask_rows[qtile, offset] > 0
    key_frame = frame + frame_step
    inside = (key_frame >= 0) & (key_frame < frames_total)
    allowed = (chosen | centre) & static_ok & inside
    bias = jnp.where(allowed, 0.0, -jnp.inf).astype(jnp.float32)
    bias = jnp.broadcast_to(bias[..., None], bias.shape + (TILE,))
    return bias.reshape(TROWS * GROUPS, QTILES, ROW_K)


def attention_kernel(q_ref, kp_ref, k_ref, kn_ref, vp_ref, v_ref, vn_ref, bias_ref, o_ref,
                     s_ref, p_ref):
    row = pl.program_id(0)
    group = pl.program_id(1)
    start = jnp.clip(QTILES * group - 2, 0, TCOLS - KCOLS) * TILE
    key_refs = (kp_ref, k_ref, kn_ref)
    value_refs = (vp_ref, v_ref, vn_ref)
    q = q_ref[...]
    bases = []
    for seg in range(SEGS):
        df, dr = divmod(seg, 3)
        key_row = jnp.clip(row + dr - 1, 0, TROWS - 1)
        base = pl.multiple_of(key_row * (TCOLS * TILE) + start, TILE)
        bases.append(base)
        k = key_refs[df][pl.ds(base, SEG_K), :]
        s_ref[:, seg * SEG_K:(seg + 1) * SEG_K] = lax.dot_general(
            q, k, (((1,), (1,)), ((), ())), preferred_element_type=jnp.float32
        )
    scale = 1.0 / math.sqrt(HEAD_DIM)
    for a in range(QTILES):
        rows = slice(a * TILE, (a + 1) * TILE)
        scores = s_ref[rows, :] * scale + bias_ref[0, a:a + 1, :]
        peak = jnp.max(scores, axis=1, keepdims=True)
        expos = jnp.exp(scores - peak)
        total = jnp.sum(expos, axis=1, keepdims=True)
        p_ref[rows, :] = (expos * (1.0 / total)).astype(jnp.bfloat16)
    acc = jnp.zeros((BLOCK_Q, HEAD_DIM), jnp.float32)
    for seg in range(SEGS):
        df, dr = divmod(seg, 3)
        v = value_refs[df][pl.ds(bases[seg], SEG_K), :]
        acc += jnp.dot(p_ref[:, seg * SEG_K:(seg + 1) * SEG_K], v,
                       preferred_element_type=jnp.float32)
    o_ref[...] = acc.astype(o_ref.dtype)


def attend(q, kp, k, kn, vp, v, vn, bias):
    tokens = q.shape[0]
    full = pl.BlockSpec((tokens, HEAD_DIM), lambda r, g: (0, 0))
    return pl.pallas_call(
        attention_kernel,
        grid=(TROWS, GROUPS),
        in_specs=[pl.BlockSpec((BLOCK_Q, HEAD_DIM), lambda r, g: (r * GROUPS + g, 0))]
        + [full] * 6
        + [pl.BlockSpec((1, QTILES, ROW_K), lambda r, g: (r * GROUPS + g, 0, 0))],
        out_specs=pl.BlockSpec((BLOCK_Q, HEAD_DIM), lambda r, g: (r * GROUPS + g, 0)),
        out_shape=jax.ShapeDtypeStruct((tokens, HEAD_DIM), jnp.bfloat16),
        scratch_shapes=[
            pltpu.VMEM((BLOCK_Q, ROW_K), jnp.float32),
            pltpu.VMEM((BLOCK_Q, ROW_K), jnp.bfloat16),
        ],
    )(q, kp, k, kn, vp, v, vn, bias)


def on_device(queries, keys, values, block_mask, out_weight):
    tok_dev = queries.shape[0]
    frames_here = tok_dev // (TROWS * TCOLS * TILE)
    assert frames_here == 1 and queries.shape[1] == HEAD_DIM
    count = lax.axis_size("frame")
    frames_total = frames_here * count
    frame = lax.axis_index("frame") * frames_here
    forward = [(i, i + 1) for i in range(count - 1)]
    backward = [(t, s) for s, t in forward]
    pair = jnp.stack([keys, values])
    prev = lax.ppermute(pair, "frame", forward)
    nxt = lax.ppermute(pair, "frame", backward)
    mask_rows = block_mask.reshape(TROWS * TCOLS, WIN)
    bias = window_bias(mask_rows, frame, frames_total)
    attention = attend(queries, prev[0], keys, nxt[0], prev[1], values, nxt[1], bias)
    core = lax.axis_index("frame") % 2
    side = lax.axis_index("hy")
    sides = lax.axis_size("hy")
    half = out_weight.shape[1] // 2
    partners = [(i, i ^ 1) for i in range(count)]
    weight_half = lax.dynamic_slice_in_dim(out_weight, core * half, half, axis=1)
    weight_half = lax.all_gather(weight_half, "hz", axis=0, tiled=True)
    chunks = attention.reshape(sides, -1, tok_dev // (sides * lax.axis_size("hz")), HEAD_DIM)
    chunks = chunks.transpose(1, 0, 2, 3).reshape(tok_dev, HEAD_DIM)
    mine = lax.all_to_all(chunks, "hz", 0, 1, tiled=True)
    theirs = lax.ppermute(mine, "frame", partners)
    block = mine.shape[0] // sides

    def project(x, which):
        rows = lax.dynamic_slice_in_dim(x, which * block, block, axis=0)
        return jnp.dot(rows, weight_half, preferred_element_type=jnp.float32)

    flip = [(0, 1), (1, 0)]
    sent = lax.ppermute(jnp.stack([project(mine, 1 - side), project(theirs, 1 - side)]), "hy", flip)
    own_half = (project(mine, side) + sent[0]).astype(jnp.bfloat16)
    other_half = lax.ppermute((project(theirs, side) + sent[1]).astype(jnp.bfloat16), "frame", partners)
    return jnp.where(
        core == 0,
        jnp.concatenate([own_half, other_half], axis=1),
        jnp.concatenate([other_half, own_half], axis=1),
    )


def solution(mesh):
    frames, heads = mesh.devices.shape
    grid = mesh.devices.reshape(frames, 2, heads // 2)
    split = jax.sharding.Mesh(grid, ("frame", "hy", "hz"))
    head = ("hy", "hz")
    return jax.shard_map(
        on_device,
        mesh=split,
        in_specs=(
            P("frame", head),
            P("frame", head),
            P("frame", head),
            P(head, "frame", None, None),
            P(head, None),
        ),
        out_specs=P(("frame",) + head, None),
        check_vma=False,
    )
```

```python
import math

import numpy as np
import jax
import jax.numpy as jnp
from jax import lax
from jax.experimental import pallas as pl
from jax.experimental.pallas import tpu as pltpu
from jax.sharding import PartitionSpec as P

HEAD_DIM = 128
TROWS = 4
TCOLS = 8
WIN = 45
TILE = 64
QTILES = 2
KCOLS = 6
SEGS = 9
BLOCK_Q = QTILES * TILE
SEG_K = KCOLS * TILE
ROW_K = SEGS * SEG_K
GROUPS = TCOLS // QTILES


def window_tables():
    shape = (TROWS * GROUPS, QTILES, SEGS, KCOLS)
    qtile = np.zeros(shape, np.int32)
    offset = np.zeros(shape, np.int32)
    static_ok = np.zeros(shape, bool)
    centre = np.zeros(shape, bool)
    frame_step = np.zeros(shape, np.int32)
    for row in range(TROWS):
        for group in range(GROUPS):
            start = min(max(QTILES * group - 2, 0), TCOLS - KCOLS)
            for a in range(QTILES):
                col = QTILES * group + a
                for seg in range(SEGS):
                    df, dr = divmod(seg, 3)
                    for j in range(KCOLS):
                        dc = start + j - col
                        b = row * GROUPS + group
                        qtile[b, a, seg, j] = row * TCOLS + col
                        ok = abs(dc) <= 2 and 0 <= row + dr - 1 < TROWS
                        static_ok[b, a, seg, j] = ok
                        offset[b, a, seg, j] = 15 * df + 5 * dr + dc + 2 if ok else 0
                        centre[b, a, seg, j] = df == 1 and dr == 1 and dc == 0
                        frame_step[b, a, seg, j] = df - 1
    return qtile, offset, static_ok, centre, frame_step


def window_picks():
    picks = np.zeros((TCOLS, WIN, SEGS, KCOLS), np.float32)
    for col in range(TCOLS):
        start = min(max(QTILES * (col // QTILES) - 2, 0), TCOLS - KCOLS)
        for seg in range(SEGS):
            df, dr = divmod(seg, 3)
            for j in range(KCOLS):
                dc = start + j - col
                if abs(dc) <= 2:
                    picks[col, 15 * df + 5 * dr + dc + 2, seg, j] = 1.0
    return picks


def window_bias(mask_rows, frame, frames_total):
    qtile, offset, static_ok, centre, frame_step = window_tables()
    grid = mask_rows.astype(jnp.float32).reshape(TROWS, TCOLS, WIN)
    chosen = jnp.einsum("rcw,cwk->rck", grid, window_picks().reshape(TCOLS, WIN, SEGS * KCOLS))
    chosen = chosen.reshape(static_ok.shape) > 0.5
    key_frame = frame + frame_step
    inside = (key_frame >= 0) & (key_frame < frames_total)
    allowed = (chosen | centre) & static_ok & inside
    bias = jnp.where(allowed, 0.0, -jnp.inf).astype(jnp.float32)
    bias = jnp.broadcast_to(bias[..., None], bias.shape + (TILE,))
    return bias.reshape(TROWS * GROUPS, QTILES, ROW_K)


def attention_kernel(q_ref, kp_ref, k_ref, kn_ref, vp_ref, v_ref, vn_ref, bias_ref, o_ref,
                     s_ref, p_ref):
    row = pl.program_id(0)
    group = pl.program_id(1)
    start = jnp.clip(QTILES * group - 2, 0, TCOLS - KCOLS) * TILE
    key_refs = (kp_ref, k_ref, kn_ref)
    value_refs = (vp_ref, v_ref, vn_ref)
    q = q_ref[...]
    bases = []
    for seg in range(SEGS):
        df, dr = divmod(seg, 3)
        key_row = jnp.clip(row + dr - 1, 0, TROWS - 1)
        base = pl.multiple_of(key_row * (TCOLS * TILE) + start, TILE)
        bases.append(base)
        k = key_refs[df][pl.ds(base, SEG_K), :]
        s_ref[:, seg * SEG_K:(seg + 1) * SEG_K] = lax.dot_general(
            q, k, (((1,), (1,)), ((), ())), preferred_element_type=jnp.float32
        )
    scale = 1.0 / math.sqrt(HEAD_DIM)
    for a in range(QTILES):
        rows = slice(a * TILE, (a + 1) * TILE)
        scores = s_ref[rows, :] * scale + bias_ref[0, a:a + 1, :]
        peak = jnp.max(scores, axis=1, keepdims=True)
        expos = jnp.exp(scores - peak)
        total = jnp.sum(expos, axis=1, keepdims=True)
        p_ref[rows, :] = (expos * (1.0 / total)).astype(jnp.bfloat16)
    acc = jnp.zeros((BLOCK_Q, HEAD_DIM), jnp.float32)
    for seg in range(SEGS):
        df, dr = divmod(seg, 3)
        v = value_refs[df][pl.ds(bases[seg], SEG_K), :]
        acc += jnp.dot(p_ref[:, seg * SEG_K:(seg + 1) * SEG_K], v,
                       preferred_element_type=jnp.float32)
    o_ref[...] = acc.astype(o_ref.dtype)


def attend(q, kp, k, kn, vp, v, vn, bias):
    tokens = q.shape[0]
    full = pl.BlockSpec((tokens, HEAD_DIM), lambda r, g: (0, 0))
    return pl.pallas_call(
        attention_kernel,
        grid=(TROWS, GROUPS),
        in_specs=[pl.BlockSpec((BLOCK_Q, HEAD_DIM), lambda r, g: (r * GROUPS + g, 0))]
        + [full] * 6
        + [pl.BlockSpec((1, QTILES, ROW_K), lambda r, g: (r * GROUPS + g, 0, 0))],
        out_specs=pl.BlockSpec((BLOCK_Q, HEAD_DIM), lambda r, g: (r * GROUPS + g, 0)),
        out_shape=jax.ShapeDtypeStruct((tokens, HEAD_DIM), jnp.bfloat16),
        scratch_shapes=[
            pltpu.VMEM((BLOCK_Q, ROW_K), jnp.float32),
            pltpu.VMEM((BLOCK_Q, ROW_K), jnp.bfloat16),
        ],
    )(q, kp, k, kn, vp, v, vn, bias)


def on_device(queries, keys, values, block_mask, out_weight):
    tok_dev = queries.shape[0]
    frames_here = tok_dev // (TROWS * TCOLS * TILE)
    assert frames_here == 1 and queries.shape[1] == HEAD_DIM
    count = lax.axis_size("frame")
    frames_total = frames_here * count
    frame = lax.axis_index("frame") * frames_here
    forward = [(i, i + 1) for i in range(count - 1)]
    backward = [(t, s) for s, t in forward]
    pair = jnp.stack([keys, values])
    prev = lax.ppermute(pair, "frame", forward)
    nxt = lax.ppermute(pair, "frame", backward)
    mask_rows = block_mask.reshape(TROWS * TCOLS, WIN)
    bias = window_bias(mask_rows, frame, frames_total)
    attention = attend(queries, prev[0], keys, nxt[0], prev[1], values, nxt[1], bias)
    core = lax.axis_index("frame") % 2
    side = lax.axis_index("hy")
    sides = lax.axis_size("hy")
    half = out_weight.shape[1] // 2
    partners = [(i, i ^ 1) for i in range(count)]
    weight_half = lax.dynamic_slice_in_dim(out_weight, core * half, half, axis=1)
    weight_half = lax.all_gather(weight_half, "hz", axis=0, tiled=True)
    chunks = attention.reshape(sides, -1, tok_dev // (sides * lax.axis_size("hz")), HEAD_DIM)
    chunks = chunks.transpose(1, 0, 2, 3).reshape(tok_dev, HEAD_DIM)
    mine = lax.all_to_all(chunks, "hz", 0, 1, tiled=True)
    theirs = lax.ppermute(mine, "frame", partners)
    block = mine.shape[0] // sides

    def project(x, which):
        rows = lax.dynamic_slice_in_dim(x, which * block, block, axis=0)
        return jnp.dot(rows, weight_half, preferred_element_type=jnp.float32)

    flip = [(0, 1), (1, 0)]
    sent_mine = lax.ppermute(project(mine, 1 - side).astype(jnp.bfloat16), "hy", flip)
    sent_theirs = lax.ppermute(project(theirs, 1 - side).astype(jnp.bfloat16), "hy", flip)
    other = (project(theirs, side) + sent_theirs.astype(jnp.float32)).astype(jnp.bfloat16)
    other_half = lax.ppermute(other, "frame", partners)
    own_half = (project(mine, side) + sent_mine.astype(jnp.float32)).astype(jnp.bfloat16)
    return jnp.where(
        core == 0,
        jnp.concatenate([own_half, other_half], axis=1),
        jnp.concatenate([other_half, own_half], axis=1),
    )


def solution(mesh):
    frames, heads = mesh.devices.shape
    grid = mesh.devices.reshape(frames, 2, heads // 2)
    split = jax.sharding.Mesh(grid, ("frame", "hy", "hz"))
    head = ("hy", "hz")
    return jax.shard_map(
        on_device,
        mesh=split,
        in_specs=(
            P("frame", head),
            P("frame", head),
            P("frame", head),
            P(head, "frame", None, None),
            P(head, None),
        ),
        out_specs=P(("frame",) + head, None),
        check_vma=False,
    )
```

```python
import math

import numpy as np
import jax
import jax.numpy as jnp
from jax import lax
from jax.experimental import pallas as pl
from jax.experimental.pallas import tpu as pltpu
from jax.sharding import PartitionSpec as P

HEAD_DIM = 128
TROWS = 4
TCOLS = 8
WIN = 45
TILE = 64
QTILES = 2
KCOLS = 6
SEGS = 9
BLOCK_Q = QTILES * TILE
SEG_K = KCOLS * TILE
ROW_K = SEGS * SEG_K
GROUPS = TCOLS // QTILES


def window_tables():
    shape = (TROWS * GROUPS, QTILES, SEGS, KCOLS)
    qtile = np.zeros(shape, np.int32)
    offset = np.zeros(shape, np.int32)
    static_ok = np.zeros(shape, bool)
    centre = np.zeros(shape, bool)
    frame_step = np.zeros(shape, np.int32)
    for row in range(TROWS):
        for group in range(GROUPS):
            start = min(max(QTILES * group - 2, 0), TCOLS - KCOLS)
            for a in range(QTILES):
                col = QTILES * group + a
                for seg in range(SEGS):
                    df, dr = divmod(seg, 3)
                    for j in range(KCOLS):
                        dc = start + j - col
                        b = row * GROUPS + group
                        qtile[b, a, seg, j] = row * TCOLS + col
                        ok = abs(dc) <= 2 and 0 <= row + dr - 1 < TROWS
                        static_ok[b, a, seg, j] = ok
                        offset[b, a, seg, j] = 15 * df + 5 * dr + dc + 2 if ok else 0
                        centre[b, a, seg, j] = df == 1 and dr == 1 and dc == 0
                        frame_step[b, a, seg, j] = df - 1
    return qtile, offset, static_ok, centre, frame_step


def window_picks():
    picks = np.zeros((TCOLS, WIN, SEGS, KCOLS), np.float32)
    for col in range(TCOLS):
        start = min(max(QTILES * (col // QTILES) - 2, 0), TCOLS - KCOLS)
        for seg in range(SEGS):
            df, dr = divmod(seg, 3)
            for j in range(KCOLS):
                dc = start + j - col
                if abs(dc) <= 2:
                    picks[col, 15 * df + 5 * dr + dc + 2, seg, j] = 1.0
    return picks


def window_bias(mask_rows, frame, frames_total):
    qtile, offset, static_ok, centre, frame_step = window_tables()
    grid = mask_rows.astype(jnp.float32).reshape(TROWS, TCOLS, WIN)
    chosen = jnp.einsum("rcw,cwk->rck", grid, window_picks().reshape(TCOLS, WIN, SEGS * KCOLS))
    chosen = chosen.reshape(static_ok.shape) > 0.5
    key_frame = frame + frame_step
    inside = (key_frame >= 0) & (key_frame < frames_total)
    allowed = (chosen | centre) & static_ok & inside
    bias = jnp.where(allowed, 0.0, -jnp.inf).astype(jnp.float32)
    bias = jnp.broadcast_to(bias[..., None], bias.shape + (TILE,))
    return bias.reshape(TROWS * GROUPS, QTILES, ROW_K)


def attention_kernel(q_ref, kp_ref, k_ref, kn_ref, vp_ref, v_ref, vn_ref, bias_ref, o_ref,
                     s_ref, p_ref):
    row = pl.program_id(0)
    group = pl.program_id(1)
    start = jnp.clip(QTILES * group - 2, 0, TCOLS - KCOLS) * TILE
    key_refs = (kp_ref, k_ref, kn_ref)
    value_refs = (vp_ref, v_ref, vn_ref)
    q = q_ref[...]
    bases = []
    for seg in range(SEGS):
        df, dr = divmod(seg, 3)
        key_row = jnp.clip(row + dr - 1, 0, TROWS - 1)
        base = pl.multiple_of(key_row * (TCOLS * TILE) + start, TILE)
        bases.append(base)
        k = key_refs[df][pl.ds(base, SEG_K), :]
        s_ref[:, seg * SEG_K:(seg + 1) * SEG_K] = lax.dot_general(
            q, k, (((1,), (1,)), ((), ())), preferred_element_type=jnp.float32
        )
    scale = 1.0 / math.sqrt(HEAD_DIM)
    for a in range(QTILES):
        rows = slice(a * TILE, (a + 1) * TILE)
        scores = s_ref[rows, :] * scale + bias_ref[0, a:a + 1, :]
        peak = jnp.max(scores, axis=1, keepdims=True)
        expos = jnp.exp(scores - peak)
        total = jnp.sum(expos, axis=1, keepdims=True)
        p_ref[rows, :] = (expos * (1.0 / total)).astype(jnp.bfloat16)
    acc = jnp.zeros((BLOCK_Q, HEAD_DIM), jnp.float32)
    for seg in range(SEGS):
        df, dr = divmod(seg, 3)
        v = value_refs[df][pl.ds(bases[seg], SEG_K), :]
        acc += jnp.dot(p_ref[:, seg * SEG_K:(seg + 1) * SEG_K], v,
                       preferred_element_type=jnp.float32)
    o_ref[...] = acc.astype(o_ref.dtype)


def attend(q, kp, k, kn, vp, v, vn, bias):
    tokens = q.shape[0]
    full = pl.BlockSpec((tokens, HEAD_DIM), lambda r, g: (0, 0))
    return pl.pallas_call(
        attention_kernel,
        grid=(TROWS, GROUPS),
        in_specs=[pl.BlockSpec((BLOCK_Q, HEAD_DIM), lambda r, g: (r * GROUPS + g, 0))]
        + [full] * 6
        + [pl.BlockSpec((1, QTILES, ROW_K), lambda r, g: (r * GROUPS + g, 0, 0))],
        out_specs=pl.BlockSpec((BLOCK_Q, HEAD_DIM), lambda r, g: (r * GROUPS + g, 0)),
        out_shape=jax.ShapeDtypeStruct((tokens, HEAD_DIM), jnp.bfloat16),
        scratch_shapes=[
            pltpu.VMEM((BLOCK_Q, ROW_K), jnp.float32),
            pltpu.VMEM((BLOCK_Q, ROW_K), jnp.bfloat16),
        ],
    )(q, kp, k, kn, vp, v, vn, bias)


def exchange_kernel(x_ref, o_ref, send_sem, recv_sem):
    me = lax.axis_index("hz")
    peers = lax.axis_size("hz")
    frame = lax.axis_index("frame")
    side = lax.axis_index("hy")
    mesh = pl.DeviceIdType.MESH
    barrier = pltpu.get_barrier_semaphore()
    for i in range(1, peers):
        peer = lax.rem(me + i, peers)
        pl.semaphore_signal(barrier, inc=1, device_id=(frame, side, peer), device_id_type=mesh)
    pl.semaphore_wait(barrier, peers - 1)
    copies = []
    for i in range(1, peers):
        peer = lax.rem(me + i, peers)
        copy = pltpu.make_async_remote_copy(
            src_ref=x_ref.at[peer],
            dst_ref=o_ref.at[me],
            send_sem=send_sem.at[i],
            recv_sem=recv_sem.at[i],
            device_id=(frame, side, peer),
            device_id_type=mesh,
        )
        copy.start()
        copies.append(copy)
    o_ref[me] = x_ref[me]
    for copy in copies:
        copy.wait()


def exchange(x):
    peers = x.shape[0]
    return pl.pallas_call(
        exchange_kernel,
        out_shape=jax.ShapeDtypeStruct(x.shape, x.dtype),
        in_specs=[pl.BlockSpec(memory_space=pltpu.VMEM)],
        out_specs=pl.BlockSpec(memory_space=pltpu.VMEM),
        scratch_shapes=[pltpu.SemaphoreType.DMA((peers,)), pltpu.SemaphoreType.DMA((peers,))],
        compiler_params=pltpu.CompilerParams(collective_id=0, has_side_effects=True),
    )(x)


def on_device(queries, keys, values, block_mask, out_weight):
    tok_dev = queries.shape[0]
    frames_here = tok_dev // (TROWS * TCOLS * TILE)
    assert frames_here == 1 and queries.shape[1] == HEAD_DIM
    count = lax.axis_size("frame")
    frames_total = frames_here * count
    frame = lax.axis_index("frame") * frames_here
    forward = [(i, i + 1) for i in range(count - 1)]
    backward = [(t, s) for s, t in forward]
    pair = jnp.stack([keys, values])
    prev = lax.ppermute(pair, "frame", forward)
    nxt = lax.ppermute(pair, "frame", backward)
    mask_rows = block_mask.reshape(TROWS * TCOLS, WIN)
    bias = window_bias(mask_rows, frame, frames_total)
    attention = attend(queries, prev[0], keys, nxt[0], prev[1], values, nxt[1], bias)
    core = lax.axis_index("frame") % 2
    side = lax.axis_index("hy")
    sides = lax.axis_size("hy")
    half = out_weight.shape[1] // 2
    partners = [(i, i ^ 1) for i in range(count)]
    weight_half = lax.dynamic_slice_in_dim(out_weight, core * half, half, axis=1)
    weight_half = lax.all_gather(weight_half, "hz", axis=0, tiled=True)
    chunks = attention.reshape(sides, -1, tok_dev // (sides * lax.axis_size("hz")), HEAD_DIM)
    peers = lax.axis_size("hz")
    chunks = chunks.transpose(1, 0, 2, 3).reshape(peers, tok_dev // peers, HEAD_DIM)
    mine = exchange(chunks).transpose(1, 0, 2).reshape(tok_dev // peers, peers * HEAD_DIM)
    theirs = lax.ppermute(mine, "frame", partners)
    block = mine.shape[0] // sides

    def project(x, which):
        rows = lax.dynamic_slice_in_dim(x, which * block, block, axis=0)
        return jnp.dot(rows, weight_half, preferred_element_type=jnp.float32)

    flip = [(0, 1), (1, 0)]
    sent_mine = lax.ppermute(project(mine, 1 - side).astype(jnp.bfloat16), "hy", flip)
    sent_theirs = lax.ppermute(project(theirs, 1 - side).astype(jnp.bfloat16), "hy", flip)
    other = (project(theirs, side) + sent_theirs.astype(jnp.float32)).astype(jnp.bfloat16)
    other_half = lax.ppermute(other, "frame", partners)
    own_half = (project(mine, side) + sent_mine.astype(jnp.float32)).astype(jnp.bfloat16)
    return jnp.where(
        core == 0,
        jnp.concatenate([own_half, other_half], axis=1),
        jnp.concatenate([other_half, own_half], axis=1),
    )


def solution(mesh):
    frames, heads = mesh.devices.shape
    grid = mesh.devices.reshape(frames, 2, heads // 2)
    split = jax.sharding.Mesh(grid, ("frame", "hy", "hz"))
    head = ("hy", "hz")
    return jax.shard_map(
        on_device,
        mesh=split,
        in_specs=(
            P("frame", head),
            P("frame", head),
            P("frame", head),
            P(head, "frame", None, None),
            P(head, None),
        ),
        out_specs=P(("frame",) + head, None),
        check_vma=False,
    )
```

```python
import math

import numpy as np
import jax
import jax.numpy as jnp
from jax import lax
from jax.experimental import pallas as pl
from jax.experimental.pallas import tpu as pltpu
from jax.sharding import PartitionSpec as P

HEAD_DIM = 128
TROWS = 4
TCOLS = 8
WIN = 45
TILE = 64
QTILES = 2
KCOLS = 6
SEGS = 9
BLOCK_Q = QTILES * TILE
SEG_K = KCOLS * TILE
ROW_K = SEGS * SEG_K
GROUPS = TCOLS // QTILES


def window_tables():
    shape = (TROWS * GROUPS, QTILES, SEGS, KCOLS)
    qtile = np.zeros(shape, np.int32)
    offset = np.zeros(shape, np.int32)
    static_ok = np.zeros(shape, bool)
    centre = np.zeros(shape, bool)
    frame_step = np.zeros(shape, np.int32)
    for row in range(TROWS):
        for group in range(GROUPS):
            start = min(max(QTILES * group - 2, 0), TCOLS - KCOLS)
            for a in range(QTILES):
                col = QTILES * group + a
                for seg in range(SEGS):
                    df, dr = divmod(seg, 3)
                    for j in range(KCOLS):
                        dc = start + j - col
                        b = row * GROUPS + group
                        qtile[b, a, seg, j] = row * TCOLS + col
                        ok = abs(dc) <= 2 and 0 <= row + dr - 1 < TROWS
                        static_ok[b, a, seg, j] = ok
                        offset[b, a, seg, j] = 15 * df + 5 * dr + dc + 2 if ok else 0
                        centre[b, a, seg, j] = df == 1 and dr == 1 and dc == 0
                        frame_step[b, a, seg, j] = df - 1
    return qtile, offset, static_ok, centre, frame_step


def window_picks():
    picks = np.zeros((TCOLS, WIN, SEGS, KCOLS), np.float32)
    for col in range(TCOLS):
        start = min(max(QTILES * (col // QTILES) - 2, 0), TCOLS - KCOLS)
        for seg in range(SEGS):
            df, dr = divmod(seg, 3)
            for j in range(KCOLS):
                dc = start + j - col
                if abs(dc) <= 2:
                    picks[col, 15 * df + 5 * dr + dc + 2, seg, j] = 1.0
    return picks


def window_bias(mask_rows, frame, frames_total):
    qtile, offset, static_ok, centre, frame_step = window_tables()
    grid = mask_rows.astype(jnp.float32).reshape(TROWS, TCOLS, WIN)
    chosen = jnp.einsum("rcw,cwk->rck", grid, window_picks().reshape(TCOLS, WIN, SEGS * KCOLS))
    chosen = chosen.reshape(static_ok.shape) > 0.5
    key_frame = frame + frame_step
    inside = (key_frame >= 0) & (key_frame < frames_total)
    allowed = (chosen | centre) & static_ok & inside
    bias = jnp.where(allowed, 0.0, -jnp.inf).astype(jnp.float32)
    bias = jnp.broadcast_to(bias[..., None], bias.shape + (TILE,))
    return bias.reshape(TROWS * GROUPS, QTILES, ROW_K)


def attention_kernel(q_ref, kp_ref, k_ref, kn_ref, vp_ref, v_ref, vn_ref, bias_ref, o_ref,
                     s_ref, p_ref):
    row = pl.program_id(0)
    group = pl.program_id(1)
    start = jnp.clip(QTILES * group - 2, 0, TCOLS - KCOLS) * TILE
    key_refs = (kp_ref, k_ref, kn_ref)
    value_refs = (vp_ref, v_ref, vn_ref)
    q = q_ref[...]
    bases = []
    for seg in range(SEGS):
        df, dr = divmod(seg, 3)
        key_row = jnp.clip(row + dr - 1, 0, TROWS - 1)
        base = pl.multiple_of(key_row * (TCOLS * TILE) + start, TILE)
        bases.append(base)
        k = key_refs[df][pl.ds(base, SEG_K), :]
        s_ref[:, seg * SEG_K:(seg + 1) * SEG_K] = lax.dot_general(
            q, k, (((1,), (1,)), ((), ())), preferred_element_type=jnp.float32
        )
    scale = 1.0 / math.sqrt(HEAD_DIM)
    for a in range(QTILES):
        rows = slice(a * TILE, (a + 1) * TILE)
        scores = s_ref[rows, :] * scale + bias_ref[0, a:a + 1, :]
        peak = jnp.max(scores, axis=1, keepdims=True)
        expos = jnp.exp(scores - peak)
        total = jnp.sum(expos, axis=1, keepdims=True)
        p_ref[rows, :] = (expos * (1.0 / total)).astype(jnp.bfloat16)
    acc = jnp.zeros((BLOCK_Q, HEAD_DIM), jnp.float32)
    for seg in range(SEGS):
        df, dr = divmod(seg, 3)
        v = value_refs[df][pl.ds(bases[seg], SEG_K), :]
        acc += jnp.dot(p_ref[:, seg * SEG_K:(seg + 1) * SEG_K], v,
                       preferred_element_type=jnp.float32)
    o_ref[...] = acc.astype(o_ref.dtype)


def attend(q, kp, k, kn, vp, v, vn, bias):
    tokens = q.shape[0]
    full = pl.BlockSpec((tokens, HEAD_DIM), lambda r, g: (0, 0))
    return pl.pallas_call(
        attention_kernel,
        grid=(TROWS, GROUPS),
        in_specs=[pl.BlockSpec((BLOCK_Q, HEAD_DIM), lambda r, g: (r * GROUPS + g, 0))]
        + [full] * 6
        + [pl.BlockSpec((1, QTILES, ROW_K), lambda r, g: (r * GROUPS + g, 0, 0))],
        out_specs=pl.BlockSpec((BLOCK_Q, HEAD_DIM), lambda r, g: (r * GROUPS + g, 0)),
        out_shape=jax.ShapeDtypeStruct((tokens, HEAD_DIM), jnp.bfloat16),
        scratch_shapes=[
            pltpu.VMEM((BLOCK_Q, ROW_K), jnp.float32),
            pltpu.VMEM((BLOCK_Q, ROW_K), jnp.bfloat16),
        ],
    )(q, kp, k, kn, vp, v, vn, bias)


def exchange_kernel(x_ref, o_ref, send_sem, recv_sem):
    me = lax.axis_index("hz")
    peers = lax.axis_size("hz")
    frame = lax.axis_index("frame")
    side = lax.axis_index("hy")
    mesh = pl.DeviceIdType.MESH
    barrier = pltpu.get_barrier_semaphore()
    for i in range(1, peers):
        peer = lax.rem(me + i, peers)
        pl.semaphore_signal(barrier, inc=1, device_id=(frame, side, peer), device_id_type=mesh)
    pl.semaphore_wait(barrier, peers - 1)
    copies = []
    for i in range(1, peers):
        peer = lax.rem(me + i, peers)
        copy = pltpu.make_async_remote_copy(
            src_ref=x_ref.at[peer],
            dst_ref=o_ref.at[me],
            send_sem=send_sem.at[i],
            recv_sem=recv_sem.at[i],
            device_id=(frame, side, peer),
            device_id_type=mesh,
        )
        copy.start()
        copies.append(copy)
    o_ref[me] = x_ref[me]
    for copy in copies:
        copy.wait()


def exchange(x):
    peers = x.shape[0]
    return pl.pallas_call(
        exchange_kernel,
        out_shape=jax.ShapeDtypeStruct(x.shape, x.dtype),
        in_specs=[pl.BlockSpec(memory_space=pltpu.VMEM)],
        out_specs=pl.BlockSpec(memory_space=pltpu.VMEM),
        scratch_shapes=[pltpu.SemaphoreType.DMA((peers,)), pltpu.SemaphoreType.DMA((peers,))],
        compiler_params=pltpu.CompilerParams(collective_id=0, has_side_effects=True),
    )(x)


def on_device(queries, keys, values, block_mask, out_weight):
    tok_dev = queries.shape[0]
    frames_here = tok_dev // (TROWS * TCOLS * TILE)
    assert frames_here == 1 and queries.shape[1] == HEAD_DIM
    count = lax.axis_size("frame")
    frames_total = frames_here * count
    frame = lax.axis_index("frame") * frames_here
    forward = [(i, i + 1) for i in range(count - 1)]
    backward = [(t, s) for s, t in forward]
    prev = [lax.ppermute(x, "frame", forward) for x in (keys, values)]
    nxt = [lax.ppermute(x, "frame", backward) for x in (keys, values)]
    mask_rows = block_mask.reshape(TROWS * TCOLS, WIN)
    bias = window_bias(mask_rows, frame, frames_total)
    attention = attend(queries, prev[0], keys, nxt[0], prev[1], values, nxt[1], bias)
    core = lax.axis_index("frame") % 2
    side = lax.axis_index("hy")
    sides = lax.axis_size("hy")
    half = out_weight.shape[1] // 2
    partners = [(i, i ^ 1) for i in range(count)]
    weight_half = lax.dynamic_slice_in_dim(out_weight, core * half, half, axis=1)
    weight_half = lax.all_gather(weight_half, "hz", axis=0, tiled=True)
    chunks = attention.reshape(sides, -1, tok_dev // (sides * lax.axis_size("hz")), HEAD_DIM)
    peers = lax.axis_size("hz")
    chunks = chunks.transpose(1, 0, 2, 3).reshape(peers, tok_dev // peers, HEAD_DIM)
    mine = exchange(chunks).transpose(1, 0, 2).reshape(tok_dev // peers, peers * HEAD_DIM)
    theirs = lax.ppermute(mine, "frame", partners)
    block = mine.shape[0] // sides

    def project(x, which):
        rows = lax.dynamic_slice_in_dim(x, which * block, block, axis=0)
        return jnp.dot(rows, weight_half, preferred_element_type=jnp.float32)

    flip = [(0, 1), (1, 0)]
    sent_mine = lax.ppermute(project(mine, 1 - side).astype(jnp.bfloat16), "hy", flip)
    sent_theirs = lax.ppermute(project(theirs, 1 - side).astype(jnp.bfloat16), "hy", flip)
    other = (project(theirs, side) + sent_theirs.astype(jnp.float32)).astype(jnp.bfloat16)
    other_half = lax.ppermute(other, "frame", partners)
    own_half = (project(mine, side) + sent_mine.astype(jnp.float32)).astype(jnp.bfloat16)
    return jnp.where(
        core == 0,
        jnp.concatenate([own_half, other_half], axis=1),
        jnp.concatenate([other_half, own_half], axis=1),
    )


def solution(mesh):
    frames, heads = mesh.devices.shape
    grid = mesh.devices.reshape(frames, 2, heads // 2)
    split = jax.sharding.Mesh(grid, ("frame", "hy", "hz"))
    head = ("hy", "hz")
    return jax.shard_map(
        on_device,
        mesh=split,
        in_specs=(
            P("frame", head),
            P("frame", head),
            P("frame", head),
            P(head, "frame", None, None),
            P(head, None),
        ),
        out_specs=P(("frame",) + head, None),
        check_vma=False,
    )
```

```python
import functools
import math

import numpy as np
import jax
import jax.numpy as jnp
from jax import lax
from jax.experimental import pallas as pl
from jax.experimental.pallas import tpu as pltpu
from jax.sharding import PartitionSpec as P

HEAD_DIM = 128
TROWS = 4
TCOLS = 8
WIN = 45
TILE = 64
QTILES = 2
KCOLS = 6
SEGS = 9
BLOCK_Q = QTILES * TILE
SEG_K = KCOLS * TILE
ROW_K = SEGS * SEG_K
GROUPS = TCOLS // QTILES


def window_tables():
    shape = (TROWS * GROUPS, QTILES, SEGS, KCOLS)
    qtile = np.zeros(shape, np.int32)
    offset = np.zeros(shape, np.int32)
    static_ok = np.zeros(shape, bool)
    centre = np.zeros(shape, bool)
    frame_step = np.zeros(shape, np.int32)
    for row in range(TROWS):
        for group in range(GROUPS):
            start = min(max(QTILES * group - 2, 0), TCOLS - KCOLS)
            for a in range(QTILES):
                col = QTILES * group + a
                for seg in range(SEGS):
                    df, dr = divmod(seg, 3)
                    for j in range(KCOLS):
                        dc = start + j - col
                        b = row * GROUPS + group
                        qtile[b, a, seg, j] = row * TCOLS + col
                        ok = abs(dc) <= 2 and 0 <= row + dr - 1 < TROWS
                        static_ok[b, a, seg, j] = ok
                        offset[b, a, seg, j] = 15 * df + 5 * dr + dc + 2 if ok else 0
                        centre[b, a, seg, j] = df == 1 and dr == 1 and dc == 0
                        frame_step[b, a, seg, j] = df - 1
    return qtile, offset, static_ok, centre, frame_step


def window_picks():
    picks = np.zeros((TCOLS, WIN, SEGS, KCOLS), np.float32)
    for col in range(TCOLS):
        start = min(max(QTILES * (col // QTILES) - 2, 0), TCOLS - KCOLS)
        for seg in range(SEGS):
            df, dr = divmod(seg, 3)
            for j in range(KCOLS):
                dc = start + j - col
                if abs(dc) <= 2:
                    picks[col, 15 * df + 5 * dr + dc + 2, seg, j] = 1.0
    return picks


def window_bias(mask_rows, frame, frames_total):
    qtile, offset, static_ok, centre, frame_step = window_tables()
    grid = mask_rows.astype(jnp.float32).reshape(TROWS, TCOLS, WIN)
    chosen = jnp.einsum("rcw,cwk->rck", grid, window_picks().reshape(TCOLS, WIN, SEGS * KCOLS))
    chosen = chosen.reshape(static_ok.shape) > 0.5
    key_frame = frame + frame_step
    inside = (key_frame >= 0) & (key_frame < frames_total)
    allowed = (chosen | centre) & static_ok & inside
    bias = jnp.where(allowed, 0.0, -jnp.inf).astype(jnp.float32)
    bias = jnp.broadcast_to(bias[..., None], bias.shape + (TILE,))
    return bias.reshape(TROWS * GROUPS, QTILES, ROW_K)


def attention_kernel(first, q_ref, kp_ref, k_ref, kn_ref, vp_ref, v_ref, vn_ref, bias_ref, o_ref,
                     s_ref, p_ref):
    row = half_base(first) + pl.program_id(0)
    group = pl.program_id(1)
    start = jnp.clip(QTILES * group - 2, 0, TCOLS - KCOLS) * TILE
    key_refs = (kp_ref, k_ref, kn_ref)
    value_refs = (vp_ref, v_ref, vn_ref)
    q = q_ref[...]
    bases = []
    for seg in range(SEGS):
        df, dr = divmod(seg, 3)
        key_row = jnp.clip(row + dr - 1, 0, TROWS - 1)
        base = pl.multiple_of(key_row * (TCOLS * TILE) + start, TILE)
        bases.append(base)
        k = key_refs[df][pl.ds(base, SEG_K), :]
        s_ref[:, seg * SEG_K:(seg + 1) * SEG_K] = lax.dot_general(
            q, k, (((1,), (1,)), ((), ())), preferred_element_type=jnp.float32
        )
    scale = 1.0 / math.sqrt(HEAD_DIM)
    for a in range(QTILES):
        rows = slice(a * TILE, (a + 1) * TILE)
        scores = s_ref[rows, :] * scale + bias_ref[0, a:a + 1, :]
        peak = jnp.max(scores, axis=1, keepdims=True)
        expos = jnp.exp(scores - peak)
        total = jnp.sum(expos, axis=1, keepdims=True)
        p_ref[rows, :] = (expos * (1.0 / total)).astype(jnp.bfloat16)
    acc = jnp.zeros((BLOCK_Q, HEAD_DIM), jnp.float32)
    for seg in range(SEGS):
        df, dr = divmod(seg, 3)
        v = value_refs[df][pl.ds(bases[seg], SEG_K), :]
        acc += jnp.dot(p_ref[:, seg * SEG_K:(seg + 1) * SEG_K], v,
                       preferred_element_type=jnp.float32)
    o_ref[...] = acc.astype(o_ref.dtype)


def half_base(first):
    side = lax.axis_index("hy")
    owner = 1 - side if first else side
    return owner * (TROWS // 2)


def attend(first, q, kp, k, kn, vp, v, vn, bias):
    tokens = k.shape[0]
    full = pl.BlockSpec((tokens, HEAD_DIM), lambda r, g: (0, 0))
    return pl.pallas_call(
        functools.partial(attention_kernel, first),
        grid=(TROWS // 2, GROUPS),
        in_specs=[pl.BlockSpec((BLOCK_Q, HEAD_DIM), lambda r, g: (r * GROUPS + g, 0))]
        + [full] * 6
        + [pl.BlockSpec((1, QTILES, ROW_K), lambda r, g: (r * GROUPS + g, 0, 0))],
        out_specs=pl.BlockSpec((BLOCK_Q, HEAD_DIM), lambda r, g: (r * GROUPS + g, 0)),
        out_shape=jax.ShapeDtypeStruct((tokens // 2, HEAD_DIM), jnp.bfloat16),
        scratch_shapes=[
            pltpu.VMEM((BLOCK_Q, ROW_K), jnp.float32),
            pltpu.VMEM((BLOCK_Q, ROW_K), jnp.bfloat16),
        ],
    )(q, kp, k, kn, vp, v, vn, bias)


def exchange_kernel(x_ref, o_ref, send_sem, recv_sem):
    me = lax.axis_index("hz")
    peers = lax.axis_size("hz")
    frame = lax.axis_index("frame")
    side = lax.axis_index("hy")
    mesh = pl.DeviceIdType.MESH
    barrier = pltpu.get_barrier_semaphore()
    for i in range(1, peers):
        peer = lax.rem(me + i, peers)
        pl.semaphore_signal(barrier, inc=1, device_id=(frame, side, peer), device_id_type=mesh)
    pl.semaphore_wait(barrier, peers - 1)
    copies = []
    for i in range(1, peers):
        peer = lax.rem(me + i, peers)
        copy = pltpu.make_async_remote_copy(
            src_ref=x_ref.at[peer],
            dst_ref=o_ref.at[me],
            send_sem=send_sem.at[i],
            recv_sem=recv_sem.at[i],
            device_id=(frame, side, peer),
            device_id_type=mesh,
        )
        copy.start()
        copies.append(copy)
    o_ref[me] = x_ref[me]
    for copy in copies:
        copy.wait()


def exchange(x, channel):
    peers = x.shape[0]
    return pl.pallas_call(
        exchange_kernel,
        out_shape=jax.ShapeDtypeStruct(x.shape, x.dtype),
        in_specs=[pl.BlockSpec(memory_space=pltpu.VMEM)],
        out_specs=pl.BlockSpec(memory_space=pltpu.VMEM),
        scratch_shapes=[pltpu.SemaphoreType.DMA((peers,)), pltpu.SemaphoreType.DMA((peers,))],
        compiler_params=pltpu.CompilerParams(collective_id=channel, has_side_effects=True),
    )(x)


def on_device(queries, keys, values, block_mask, out_weight):
    tok_dev = queries.shape[0]
    frames_here = tok_dev // (TROWS * TCOLS * TILE)
    assert frames_here == 1 and queries.shape[1] == HEAD_DIM
    count = lax.axis_size("frame")
    frames_total = frames_here * count
    frame = lax.axis_index("frame") * frames_here
    forward = [(i, i + 1) for i in range(count - 1)]
    backward = [(t, s) for s, t in forward]
    prev = [lax.ppermute(x, "frame", forward) for x in (keys, values)]
    nxt = [lax.ppermute(x, "frame", backward) for x in (keys, values)]
    mask_rows = block_mask.reshape(TROWS * TCOLS, WIN)
    bias = window_bias(mask_rows, frame, frames_total)
    core = lax.axis_index("frame") % 2
    side = lax.axis_index("hy")
    half = out_weight.shape[1] // 2
    partners = [(i, i ^ 1) for i in range(count)]
    flip = [(0, 1), (1, 0)]
    weight_half = lax.dynamic_slice_in_dim(out_weight, core * half, half, axis=1)
    weight_half = lax.all_gather(weight_half, "hz", axis=0, tiled=True)
    peers = lax.axis_size("hz")
    rows = tok_dev // 2
    bias_rows = bias.shape[0] // 2

    def half_attention(first):
        base = half_base(first)
        q = lax.dynamic_slice_in_dim(queries, base * (rows // 2), rows, axis=0)
        b = lax.dynamic_slice_in_dim(bias, base * (bias_rows // 2), bias_rows, axis=0)
        out = attend(first, q, prev[0], keys, nxt[0], prev[1], values, nxt[1], b)
        got = exchange(out.reshape(peers, rows // peers, HEAD_DIM), 1 if first else 2)
        mine = got.transpose(1, 0, 2).reshape(rows // peers, peers * HEAD_DIM)
        theirs = lax.ppermute(mine, "frame", partners)
        return mine, theirs

    project = lambda x: jnp.dot(x, weight_half, preferred_element_type=jnp.float32)
    mine, theirs = half_attention(True)
    partials = jnp.stack([project(mine), project(theirs)]).astype(jnp.bfloat16)
    partials, queries = lax.optimization_barrier((partials, queries))
    sent_mine, sent_theirs = lax.ppermute(partials, "hy", flip)
    mine, theirs = half_attention(False)
    other = (project(theirs) + sent_theirs.astype(jnp.float32)).astype(jnp.bfloat16)
    other_half = lax.ppermute(other, "frame", partners)
    own_half = (project(mine) + sent_mine.astype(jnp.float32)).astype(jnp.bfloat16)
    return jnp.where(
        core == 0,
        jnp.concatenate([own_half, other_half], axis=1),
        jnp.concatenate([other_half, own_half], axis=1),
    )


def solution(mesh):
    frames, heads = mesh.devices.shape
    grid = mesh.devices.reshape(frames, 2, heads // 2)
    split = jax.sharding.Mesh(grid, ("frame", "hy", "hz"))
    head = ("hy", "hz")
    return jax.shard_map(
        on_device,
        mesh=split,
        in_specs=(
            P("frame", head),
            P("frame", head),
            P("frame", head),
            P(head, "frame", None, None),
            P(head, None),
        ),
        out_specs=P(("frame",) + head, None),
        check_vma=False,
    )
```

```python
import math

import numpy as np
import jax
import jax.numpy as jnp
from jax import lax
from jax.experimental import pallas as pl
from jax.experimental.pallas import tpu as pltpu
from jax.sharding import PartitionSpec as P

HEAD_DIM = 128
TROWS = 4
TCOLS = 8
WIN = 45
TILE = 64
QTILES = 2
KCOLS = 6
SEGS = 9
BLOCK_Q = QTILES * TILE
SEG_K = KCOLS * TILE
ROW_K = SEGS * SEG_K
GROUPS = TCOLS // QTILES


def window_tables():
    shape = (TROWS * GROUPS, QTILES, SEGS, KCOLS)
    qtile = np.zeros(shape, np.int32)
    offset = np.zeros(shape, np.int32)
    static_ok = np.zeros(shape, bool)
    centre = np.zeros(shape, bool)
    frame_step = np.zeros(shape, np.int32)
    for row in range(TROWS):
        for group in range(GROUPS):
            start = min(max(QTILES * group - 2, 0), TCOLS - KCOLS)
            for a in range(QTILES):
                col = QTILES * group + a
                for seg in range(SEGS):
                    df, dr = divmod(seg, 3)
                    for j in range(KCOLS):
                        dc = start + j - col
                        b = row * GROUPS + group
                        qtile[b, a, seg, j] = row * TCOLS + col
                        ok = abs(dc) <= 2 and 0 <= row + dr - 1 < TROWS
                        static_ok[b, a, seg, j] = ok
                        offset[b, a, seg, j] = 15 * df + 5 * dr + dc + 2 if ok else 0
                        centre[b, a, seg, j] = df == 1 and dr == 1 and dc == 0
                        frame_step[b, a, seg, j] = df - 1
    return qtile, offset, static_ok, centre, frame_step


def window_picks():
    picks = np.zeros((TCOLS, WIN, SEGS, KCOLS), np.float32)
    for col in range(TCOLS):
        start = min(max(QTILES * (col // QTILES) - 2, 0), TCOLS - KCOLS)
        for seg in range(SEGS):
            df, dr = divmod(seg, 3)
            for j in range(KCOLS):
                dc = start + j - col
                if abs(dc) <= 2:
                    picks[col, 15 * df + 5 * dr + dc + 2, seg, j] = 1.0
    return picks


def window_bias(mask_rows, frame, frames_total):
    qtile, offset, static_ok, centre, frame_step = window_tables()
    grid = mask_rows.astype(jnp.float32).reshape(TROWS, TCOLS, WIN)
    chosen = jnp.einsum("rcw,cwk->rck", grid, window_picks().reshape(TCOLS, WIN, SEGS * KCOLS))
    chosen = chosen.reshape(static_ok.shape) > 0.5
    key_frame = frame + frame_step
    inside = (key_frame >= 0) & (key_frame < frames_total)
    allowed = (chosen | centre) & static_ok & inside
    bias = jnp.where(allowed, 0.0, -jnp.inf).astype(jnp.float32)
    bias = jnp.broadcast_to(bias[..., None], bias.shape + (TILE,))
    return bias.reshape(TROWS * GROUPS, QTILES, ROW_K)


def attention_kernel(q_ref, k_ref, v_ref, bias_ref, o_ref,
                     kp_ref, kn_ref, vp_ref, vn_ref, s_ref, p_ref, send_sem, recv_sem):
    row = pl.program_id(0)
    group = pl.program_id(1)

    @pl.when((row == 0) & (group == 0))
    def _():
        frame = lax.axis_index("frame")
        count = lax.axis_size("frame")
        side = lax.axis_index("hy")
        peer = lax.axis_index("hz")
        mesh = pl.DeviceIdType.MESH
        has_prev = frame > 0
        has_next = frame < count - 1
        prev_dev = (frame - 1, side, peer)
        next_dev = (frame + 1, side, peer)
        barrier = pltpu.get_barrier_semaphore()

        @pl.when(has_prev)
        def _():
            pl.semaphore_signal(barrier, inc=1, device_id=prev_dev, device_id_type=mesh)

        @pl.when(has_next)
        def _():
            pl.semaphore_signal(barrier, inc=1, device_id=next_dev, device_id_type=mesh)

        @pl.when(has_prev & has_next)
        def _():
            pl.semaphore_wait(barrier, 2)

        @pl.when(has_prev != has_next)
        def _():
            pl.semaphore_wait(barrier, 1)

        def push(src, dst, slot, device):
            return pltpu.make_async_remote_copy(
                src_ref=src, dst_ref=dst, send_sem=send_sem.at[slot], recv_sem=recv_sem.at[slot],
                device_id=device, device_id_type=mesh,
            )

        to_next = [push(k_ref, kp_ref, 0, next_dev), push(v_ref, vp_ref, 1, next_dev)]
        to_prev = [push(k_ref, kn_ref, 2, prev_dev), push(v_ref, vn_ref, 3, prev_dev)]

        @pl.when(has_next)
        def _():
            for copy in to_next:
                copy.start()

        @pl.when(has_prev)
        def _():
            for copy in to_prev:
                copy.start()

        @pl.when(has_prev)
        def _():
            for copy in to_prev:
                copy.wait_send()
            for copy in to_next:
                copy.wait_recv()

        @pl.when(has_next)
        def _():
            for copy in to_next:
                copy.wait_send()
            for copy in to_prev:
                copy.wait_recv()

        @pl.when(jnp.logical_not(has_prev))
        def _():
            kp_ref[...] = jnp.zeros_like(kp_ref)
            vp_ref[...] = jnp.zeros_like(vp_ref)

        @pl.when(jnp.logical_not(has_next))
        def _():
            kn_ref[...] = jnp.zeros_like(kn_ref)
            vn_ref[...] = jnp.zeros_like(vn_ref)

    start = jnp.clip(QTILES * group - 2, 0, TCOLS - KCOLS) * TILE
    key_refs = (kp_ref, k_ref, kn_ref)
    value_refs = (vp_ref, v_ref, vn_ref)
    q = q_ref[...]
    bases = []
    for seg in range(SEGS):
        df, dr = divmod(seg, 3)
        key_row = jnp.clip(row + dr - 1, 0, TROWS - 1)
        base = pl.multiple_of(key_row * (TCOLS * TILE) + start, TILE)
        bases.append(base)
        k = key_refs[df][pl.ds(base, SEG_K), :]
        s_ref[:, seg * SEG_K:(seg + 1) * SEG_K] = lax.dot_general(
            q, k, (((1,), (1,)), ((), ())), preferred_element_type=jnp.float32
        )
    scale = 1.0 / math.sqrt(HEAD_DIM)
    for a in range(QTILES):
        rows = slice(a * TILE, (a + 1) * TILE)
        scores = s_ref[rows, :] * scale + bias_ref[0, a:a + 1, :]
        peak = jnp.max(scores, axis=1, keepdims=True)
        expos = jnp.exp(scores - peak)
        total = jnp.sum(expos, axis=1, keepdims=True)
        p_ref[rows, :] = (expos * (1.0 / total)).astype(jnp.bfloat16)
    acc = jnp.zeros((BLOCK_Q, HEAD_DIM), jnp.float32)
    for seg in range(SEGS):
        df, dr = divmod(seg, 3)
        v = value_refs[df][pl.ds(bases[seg], SEG_K), :]
        acc += jnp.dot(p_ref[:, seg * SEG_K:(seg + 1) * SEG_K], v,
                       preferred_element_type=jnp.float32)
    o_ref[...] = acc.astype(o_ref.dtype)


def attend(q, k, v, bias):
    tokens = q.shape[0]
    full = pl.BlockSpec((tokens, HEAD_DIM), lambda r, g: (0, 0))
    frame_kv = pltpu.VMEM((tokens, HEAD_DIM), jnp.bfloat16)
    return pl.pallas_call(
        attention_kernel,
        grid=(TROWS, GROUPS),
        in_specs=[pl.BlockSpec((BLOCK_Q, HEAD_DIM), lambda r, g: (r * GROUPS + g, 0))]
        + [full] * 2
        + [pl.BlockSpec((1, QTILES, ROW_K), lambda r, g: (r * GROUPS + g, 0, 0))],
        out_specs=pl.BlockSpec((BLOCK_Q, HEAD_DIM), lambda r, g: (r * GROUPS + g, 0)),
        out_shape=jax.ShapeDtypeStruct((tokens, HEAD_DIM), jnp.bfloat16),
        scratch_shapes=[frame_kv] * 4 + [
            pltpu.VMEM((BLOCK_Q, ROW_K), jnp.float32),
            pltpu.VMEM((BLOCK_Q, ROW_K), jnp.bfloat16),
            pltpu.SemaphoreType.DMA((4,)),
            pltpu.SemaphoreType.DMA((4,)),
        ],
        compiler_params=pltpu.CompilerParams(collective_id=1, has_side_effects=True),
    )(q, k, v, bias)


def exchange_kernel(x_ref, o_ref, send_sem, recv_sem):
    me = lax.axis_index("hz")
    peers = lax.axis_size("hz")
    frame = lax.axis_index("frame")
    side = lax.axis_index("hy")
    mesh = pl.DeviceIdType.MESH
    barrier = pltpu.get_barrier_semaphore()
    for i in range(1, peers):
        peer = lax.rem(me + i, peers)
        pl.semaphore_signal(barrier, inc=1, device_id=(frame, side, peer), device_id_type=mesh)
    pl.semaphore_wait(barrier, peers - 1)
    copies = []
    for i in range(1, peers):
        peer = lax.rem(me + i, peers)
        copy = pltpu.make_async_remote_copy(
            src_ref=x_ref.at[peer],
            dst_ref=o_ref.at[me],
            send_sem=send_sem.at[i],
            recv_sem=recv_sem.at[i],
            device_id=(frame, side, peer),
            device_id_type=mesh,
        )
        copy.start()
        copies.append(copy)
    o_ref[me] = x_ref[me]
    for copy in copies:
        copy.wait()


def exchange(x):
    peers = x.shape[0]
    return pl.pallas_call(
        exchange_kernel,
        out_shape=jax.ShapeDtypeStruct(x.shape, x.dtype),
        in_specs=[pl.BlockSpec(memory_space=pltpu.VMEM)],
        out_specs=pl.BlockSpec(memory_space=pltpu.VMEM),
        scratch_shapes=[pltpu.SemaphoreType.DMA((peers,)), pltpu.SemaphoreType.DMA((peers,))],
        compiler_params=pltpu.CompilerParams(collective_id=0, has_side_effects=True),
    )(x)


def on_device(queries, keys, values, block_mask, out_weight):
    tok_dev = queries.shape[0]
    frames_here = tok_dev // (TROWS * TCOLS * TILE)
    assert frames_here == 1 and queries.shape[1] == HEAD_DIM
    count = lax.axis_size("frame")
    frames_total = frames_here * count
    frame = lax.axis_index("frame") * frames_here
    mask_rows = block_mask.reshape(TROWS * TCOLS, WIN)
    bias = window_bias(mask_rows, frame, frames_total)
    attention = attend(queries, keys, values, bias)
    core = lax.axis_index("frame") % 2
    side = lax.axis_index("hy")
    sides = lax.axis_size("hy")
    half = out_weight.shape[1] // 2
    partners = [(i, i ^ 1) for i in range(count)]
    weight_half = lax.dynamic_slice_in_dim(out_weight, core * half, half, axis=1)
    weight_half = lax.all_gather(weight_half, "hz", axis=0, tiled=True)
    chunks = attention.reshape(sides, -1, tok_dev // (sides * lax.axis_size("hz")), HEAD_DIM)
    peers = lax.axis_size("hz")
    chunks = chunks.transpose(1, 0, 2, 3).reshape(peers, tok_dev // peers, HEAD_DIM)
    mine = exchange(chunks).transpose(1, 0, 2).reshape(tok_dev // peers, peers * HEAD_DIM)
    theirs = lax.ppermute(mine, "frame", partners)
    block = mine.shape[0] // sides

    def project(x, which):
        rows = lax.dynamic_slice_in_dim(x, which * block, block, axis=0)
        return jnp.dot(rows, weight_half, preferred_element_type=jnp.float32)

    flip = [(0, 1), (1, 0)]
    sent_mine = lax.ppermute(project(mine, 1 - side).astype(jnp.bfloat16), "hy", flip)
    sent_theirs = lax.ppermute(project(theirs, 1 - side).astype(jnp.bfloat16), "hy", flip)
    other = (project(theirs, side) + sent_theirs.astype(jnp.float32)).astype(jnp.bfloat16)
    other_half = lax.ppermute(other, "frame", partners)
    own_half = (project(mine, side) + sent_mine.astype(jnp.float32)).astype(jnp.bfloat16)
    return jnp.where(
        core == 0,
        jnp.concatenate([own_half, other_half], axis=1),
        jnp.concatenate([other_half, own_half], axis=1),
    )


def solution(mesh):
    frames, heads = mesh.devices.shape
    grid = mesh.devices.reshape(frames, 2, heads // 2)
    split = jax.sharding.Mesh(grid, ("frame", "hy", "hz"))
    head = ("hy", "hz")
    return jax.shard_map(
        on_device,
        mesh=split,
        in_specs=(
            P("frame", head),
            P("frame", head),
            P("frame", head),
            P(head, "frame", None, None),
            P(head, None),
        ),
        out_specs=P(("frame",) + head, None),
        check_vma=False,
    )
```

```python
import math

import numpy as np
import jax
import jax.numpy as jnp
from jax import lax
from jax.experimental import pallas as pl
from jax.experimental.pallas import tpu as pltpu
from jax.sharding import PartitionSpec as P

HEAD_DIM = 128
TROWS = 4
TCOLS = 8
WIN = 45
TILE = 64
QTILES = 2
KCOLS = 6
SEGS = 9
BLOCK_Q = QTILES * TILE
SEG_K = KCOLS * TILE
ROW_K = SEGS * SEG_K
GROUPS = TCOLS // QTILES


def window_tables():
    shape = (TROWS * GROUPS, QTILES, SEGS, KCOLS)
    qtile = np.zeros(shape, np.int32)
    offset = np.zeros(shape, np.int32)
    static_ok = np.zeros(shape, bool)
    centre = np.zeros(shape, bool)
    frame_step = np.zeros(shape, np.int32)
    for row in range(TROWS):
        for group in range(GROUPS):
            start = min(max(QTILES * group - 2, 0), TCOLS - KCOLS)
            for a in range(QTILES):
                col = QTILES * group + a
                for seg in range(SEGS):
                    df, dr = divmod(seg, 3)
                    for j in range(KCOLS):
                        dc = start + j - col
                        b = row * GROUPS + group
                        qtile[b, a, seg, j] = row * TCOLS + col
                        ok = abs(dc) <= 2 and 0 <= row + dr - 1 < TROWS
                        static_ok[b, a, seg, j] = ok
                        offset[b, a, seg, j] = 15 * df + 5 * dr + dc + 2 if ok else 0
                        centre[b, a, seg, j] = df == 1 and dr == 1 and dc == 0
                        frame_step[b, a, seg, j] = df - 1
    return qtile, offset, static_ok, centre, frame_step


def window_picks():
    picks = np.zeros((TCOLS, WIN, SEGS, KCOLS), np.float32)
    for col in range(TCOLS):
        start = min(max(QTILES * (col // QTILES) - 2, 0), TCOLS - KCOLS)
        for seg in range(SEGS):
            df, dr = divmod(seg, 3)
            for j in range(KCOLS):
                dc = start + j - col
                if abs(dc) <= 2:
                    picks[col, 15 * df + 5 * dr + dc + 2, seg, j] = 1.0
    return picks


def window_bias(mask_rows, frame, frames_total):
    qtile, offset, static_ok, centre, frame_step = window_tables()
    grid = mask_rows.astype(jnp.float32).reshape(TROWS, TCOLS, WIN)
    chosen = jnp.einsum("rcw,cwk->rck", grid, window_picks().reshape(TCOLS, WIN, SEGS * KCOLS))
    chosen = chosen.reshape(static_ok.shape) > 0.5
    key_frame = frame + frame_step
    inside = (key_frame >= 0) & (key_frame < frames_total)
    allowed = (chosen | centre) & static_ok & inside
    bias = jnp.where(allowed, 0.0, -jnp.inf).astype(jnp.float32)
    bias = jnp.broadcast_to(bias[..., None], bias.shape + (TILE,))
    return bias.reshape(TROWS * GROUPS, QTILES, ROW_K)


def attention_kernel(q_ref, k_ref, v_ref, bias_ref, o_ref,
                     kp_ref, kn_ref, vp_ref, vn_ref, s_ref, p_ref, att_ref, got_ref,
                     send_sem, recv_sem, out_send, out_recv):
    row = pl.program_id(0)
    group = pl.program_id(1)
    frame = lax.axis_index("frame")
    side = lax.axis_index("hy")
    me = lax.axis_index("hz")
    peers = lax.axis_size("hz")
    mesh = pl.DeviceIdType.MESH

    @pl.when((row == 0) & (group == 0))
    def _():
        count = lax.axis_size("frame")
        peer = me
        has_prev = frame > 0
        has_next = frame < count - 1
        prev_dev = (frame - 1, side, peer)
        next_dev = (frame + 1, side, peer)
        barrier = pltpu.get_barrier_semaphore()

        @pl.when(has_prev)
        def _():
            pl.semaphore_signal(barrier, inc=1, device_id=prev_dev, device_id_type=mesh)

        @pl.when(has_next)
        def _():
            pl.semaphore_signal(barrier, inc=1, device_id=next_dev, device_id_type=mesh)

        for i in range(1, peers):
            other = (frame, side, lax.rem(me + i, peers))
            pl.semaphore_signal(barrier, inc=1, device_id=other, device_id_type=mesh)

        @pl.when(has_prev & has_next)
        def _():
            pl.semaphore_wait(barrier, peers + 1)

        @pl.when(has_prev != has_next)
        def _():
            pl.semaphore_wait(barrier, peers)

        def push(src, dst, slot, device):
            return pltpu.make_async_remote_copy(
                src_ref=src, dst_ref=dst, send_sem=send_sem.at[slot], recv_sem=recv_sem.at[slot],
                device_id=device, device_id_type=mesh,
            )

        to_next = [push(k_ref, kp_ref, 0, next_dev), push(v_ref, vp_ref, 1, next_dev)]
        to_prev = [push(k_ref, kn_ref, 2, prev_dev), push(v_ref, vn_ref, 3, prev_dev)]

        @pl.when(has_next)
        def _():
            for copy in to_next:
                copy.start()

        @pl.when(has_prev)
        def _():
            for copy in to_prev:
                copy.start()

        @pl.when(has_prev)
        def _():
            for copy in to_prev:
                copy.wait_send()
            for copy in to_next:
                copy.wait_recv()

        @pl.when(has_next)
        def _():
            for copy in to_next:
                copy.wait_send()
            for copy in to_prev:
                copy.wait_recv()

        @pl.when(jnp.logical_not(has_prev))
        def _():
            kp_ref[...] = jnp.zeros_like(kp_ref)
            vp_ref[...] = jnp.zeros_like(vp_ref)

        @pl.when(jnp.logical_not(has_next))
        def _():
            kn_ref[...] = jnp.zeros_like(kn_ref)
            vn_ref[...] = jnp.zeros_like(vn_ref)

    start = jnp.clip(QTILES * group - 2, 0, TCOLS - KCOLS) * TILE
    key_refs = (kp_ref, k_ref, kn_ref)
    value_refs = (vp_ref, v_ref, vn_ref)
    q = q_ref[...]
    bases = []
    for seg in range(SEGS):
        df, dr = divmod(seg, 3)
        key_row = jnp.clip(row + dr - 1, 0, TROWS - 1)
        base = pl.multiple_of(key_row * (TCOLS * TILE) + start, TILE)
        bases.append(base)
        k = key_refs[df][pl.ds(base, SEG_K), :]
        s_ref[:, seg * SEG_K:(seg + 1) * SEG_K] = lax.dot_general(
            q, k, (((1,), (1,)), ((), ())), preferred_element_type=jnp.float32
        )
    scale = 1.0 / math.sqrt(HEAD_DIM)
    for a in range(QTILES):
        rows = slice(a * TILE, (a + 1) * TILE)
        scores = s_ref[rows, :] * scale + bias_ref[0, a:a + 1, :]
        peak = jnp.max(scores, axis=1, keepdims=True)
        expos = jnp.exp(scores - peak)
        total = jnp.sum(expos, axis=1, keepdims=True)
        p_ref[rows, :] = (expos * (1.0 / total)).astype(jnp.bfloat16)
    acc = jnp.zeros((BLOCK_Q, HEAD_DIM), jnp.float32)
    for seg in range(SEGS):
        df, dr = divmod(seg, 3)
        v = value_refs[df][pl.ds(bases[seg], SEG_K), :]
        acc += jnp.dot(p_ref[:, seg * SEG_K:(seg + 1) * SEG_K], v,
                       preferred_element_type=jnp.float32)
    att_ref[pl.ds(pl.multiple_of((row * GROUPS + group) * BLOCK_Q, BLOCK_Q), BLOCK_Q), :] = (
        acc.astype(att_ref.dtype))

    @pl.when((row == TROWS - 1) & (group == GROUPS - 1))
    def _():
        chunk = got_ref.shape[1] // 2
        copies = []
        for i in range(1, peers):
            peer = lax.rem(me + i, peers)
            for part in range(2):
                src = pl.multiple_of((part * peers + peer) * chunk, chunk)
                copy = pltpu.make_async_remote_copy(
                    src_ref=att_ref.at[pl.ds(src, chunk)],
                    dst_ref=got_ref.at[me, pl.ds(part * chunk, chunk)],
                    send_sem=out_send.at[2 * i + part],
                    recv_sem=out_recv.at[2 * i + part],
                    device_id=(frame, side, peer),
                    device_id_type=mesh,
                )
                copy.start()
                copies.append(copy)
        for part in range(2):
            src = pl.multiple_of((part * peers + me) * chunk, chunk)
            got_ref[me, pl.ds(part * chunk, chunk), :] = att_ref[pl.ds(src, chunk), :]
        for copy in copies:
            copy.wait()
        o_ref[...] = got_ref[...]


def attend(q, k, v, bias):
    tokens = q.shape[0]
    full = pl.BlockSpec((tokens, HEAD_DIM), lambda r, g: (0, 0))
    frame_kv = pltpu.VMEM((tokens, HEAD_DIM), jnp.bfloat16)
    peers = lax.axis_size("hz")
    got_shape = (peers, tokens // peers, HEAD_DIM)
    got = pltpu.VMEM(got_shape, jnp.bfloat16)
    return pl.pallas_call(
        attention_kernel,
        grid=(TROWS, GROUPS),
        in_specs=[pl.BlockSpec((BLOCK_Q, HEAD_DIM), lambda r, g: (r * GROUPS + g, 0))]
        + [full] * 2
        + [pl.BlockSpec((1, QTILES, ROW_K), lambda r, g: (r * GROUPS + g, 0, 0))],
        out_specs=pl.BlockSpec(got_shape, lambda r, g: (0, 0, 0)),
        out_shape=jax.ShapeDtypeStruct(got_shape, jnp.bfloat16),
        scratch_shapes=[frame_kv] * 4 + [
            pltpu.VMEM((BLOCK_Q, ROW_K), jnp.float32),
            pltpu.VMEM((BLOCK_Q, ROW_K), jnp.bfloat16),
            frame_kv,
            got,
            pltpu.SemaphoreType.DMA((4,)),
            pltpu.SemaphoreType.DMA((4,)),
            pltpu.SemaphoreType.DMA((2 * peers,)),
            pltpu.SemaphoreType.DMA((2 * peers,)),
        ],
        compiler_params=pltpu.CompilerParams(collective_id=1, has_side_effects=True),
    )(q, k, v, bias)


def on_device(queries, keys, values, block_mask, out_weight):
    tok_dev = queries.shape[0]
    frames_here = tok_dev // (TROWS * TCOLS * TILE)
    assert frames_here == 1 and queries.shape[1] == HEAD_DIM
    count = lax.axis_size("frame")
    frames_total = frames_here * count
    frame = lax.axis_index("frame") * frames_here
    mask_rows = block_mask.reshape(TROWS * TCOLS, WIN)
    bias = window_bias(mask_rows, frame, frames_total)
    got = attend(queries, keys, values, bias)
    core = lax.axis_index("frame") % 2
    side = lax.axis_index("hy")
    sides = lax.axis_size("hy")
    half = out_weight.shape[1] // 2
    partners = [(i, i ^ 1) for i in range(count)]
    weight_half = lax.dynamic_slice_in_dim(out_weight, core * half, half, axis=1)
    weight_half = lax.all_gather(weight_half, "hz", axis=0, tiled=True)
    peers = lax.axis_size("hz")
    mine = got.transpose(1, 0, 2).reshape(tok_dev // peers, peers * HEAD_DIM)
    theirs = lax.ppermute(mine, "frame", partners)
    block = mine.shape[0] // sides

    def project(x, which):
        rows = lax.dynamic_slice_in_dim(x, which * block, block, axis=0)
        return jnp.dot(rows, weight_half, preferred_element_type=jnp.float32)

    flip = [(0, 1), (1, 0)]
    sent_mine = lax.ppermute(project(mine, 1 - side).astype(jnp.bfloat16), "hy", flip)
    sent_theirs = lax.ppermute(project(theirs, 1 - side).astype(jnp.bfloat16), "hy", flip)
    other = (project(theirs, side) + sent_theirs.astype(jnp.float32)).astype(jnp.bfloat16)
    other_half = lax.ppermute(other, "frame", partners)
    own_half = (project(mine, side) + sent_mine.astype(jnp.float32)).astype(jnp.bfloat16)
    return jnp.where(
        core == 0,
        jnp.concatenate([own_half, other_half], axis=1),
        jnp.concatenate([other_half, own_half], axis=1),
    )


def solution(mesh):
    frames, heads = mesh.devices.shape
    grid = mesh.devices.reshape(frames, 2, heads // 2)
    split = jax.sharding.Mesh(grid, ("frame", "hy", "hz"))
    head = ("hy", "hz")
    return jax.shard_map(
        on_device,
        mesh=split,
        in_specs=(
            P("frame", head),
            P("frame", head),
            P("frame", head),
            P(head, "frame", None, None),
            P(head, None),
        ),
        out_specs=P(("frame",) + head, None),
        check_vma=False,
    )
```

```python
import math

import numpy as np
import jax
import jax.numpy as jnp
from jax import lax
from jax.experimental import pallas as pl
from jax.experimental.pallas import tpu as pltpu
from jax.sharding import PartitionSpec as P

HEAD_DIM = 128
TROWS = 4
TCOLS = 8
WIN = 45
TILE = 64
QTILES = 2
KCOLS = 6
SEGS = 9
BLOCK_Q = QTILES * TILE
SEG_K = KCOLS * TILE
ROW_K = SEGS * SEG_K
GROUPS = TCOLS // QTILES


def window_tables():
    shape = (TROWS * GROUPS, QTILES, SEGS, KCOLS)
    qtile = np.zeros(shape, np.int32)
    offset = np.zeros(shape, np.int32)
    static_ok = np.zeros(shape, bool)
    centre = np.zeros(shape, bool)
    frame_step = np.zeros(shape, np.int32)
    for row in range(TROWS):
        for group in range(GROUPS):
            start = min(max(QTILES * group - 2, 0), TCOLS - KCOLS)
            for a in range(QTILES):
                col = QTILES * group + a
                for seg in range(SEGS):
                    df, dr = divmod(seg, 3)
                    for j in range(KCOLS):
                        dc = start + j - col
                        b = row * GROUPS + group
                        qtile[b, a, seg, j] = row * TCOLS + col
                        ok = abs(dc) <= 2 and 0 <= row + dr - 1 < TROWS
                        static_ok[b, a, seg, j] = ok
                        offset[b, a, seg, j] = 15 * df + 5 * dr + dc + 2 if ok else 0
                        centre[b, a, seg, j] = df == 1 and dr == 1 and dc == 0
                        frame_step[b, a, seg, j] = df - 1
    return qtile, offset, static_ok, centre, frame_step


def window_picks():
    picks = np.zeros((TCOLS, WIN, SEGS, KCOLS), np.float32)
    for col in range(TCOLS):
        start = min(max(QTILES * (col // QTILES) - 2, 0), TCOLS - KCOLS)
        for seg in range(SEGS):
            df, dr = divmod(seg, 3)
            for j in range(KCOLS):
                dc = start + j - col
                if abs(dc) <= 2:
                    picks[col, 15 * df + 5 * dr + dc + 2, seg, j] = 1.0
    return picks


def window_bias(mask_rows, frame, frames_total):
    qtile, offset, static_ok, centre, frame_step = window_tables()
    grid = mask_rows.astype(jnp.float32).reshape(TROWS, TCOLS, WIN)
    chosen = jnp.einsum("rcw,cwk->rck", grid, window_picks().reshape(TCOLS, WIN, SEGS * KCOLS))
    chosen = chosen.reshape(static_ok.shape) > 0.5
    key_frame = frame + frame_step
    inside = (key_frame >= 0) & (key_frame < frames_total)
    allowed = (chosen | centre) & static_ok & inside
    bias = jnp.where(allowed, 0.0, -jnp.inf).astype(jnp.float32)
    bias = jnp.broadcast_to(bias[..., None], bias.shape + (TILE,))
    return bias.reshape(TROWS * GROUPS, QTILES, ROW_K)


def attention_kernel(q_ref, k_ref, v_ref, bias_ref, o_ref,
                     kp_ref, kn_ref, vp_ref, vn_ref, s_ref, p_ref, att_ref, got_ref,
                     send_sem, recv_sem, out_send, out_recv):
    row = pl.program_id(0)
    group = pl.program_id(1)
    frame = lax.axis_index("frame")
    side = lax.axis_index("hy")
    me = lax.axis_index("hz")
    peers = lax.axis_size("hz")
    mesh = pl.DeviceIdType.MESH

    @pl.when((row == 0) & (group == 0))
    def _():
        count = lax.axis_size("frame")
        peer = me
        has_prev = frame > 0
        has_next = frame < count - 1
        prev_dev = (frame - 1, side, peer)
        next_dev = (frame + 1, side, peer)
        barrier = pltpu.get_barrier_semaphore()

        @pl.when(has_prev)
        def _():
            pl.semaphore_signal(barrier, inc=1, device_id=prev_dev, device_id_type=mesh)

        @pl.when(has_next)
        def _():
            pl.semaphore_signal(barrier, inc=1, device_id=next_dev, device_id_type=mesh)

        for i in range(1, peers):
            other = (frame, side, lax.rem(me + i, peers))
            pl.semaphore_signal(barrier, inc=1, device_id=other, device_id_type=mesh)

        @pl.when(has_prev & has_next)
        def _():
            pl.semaphore_wait(barrier, peers + 1)

        @pl.when(has_prev != has_next)
        def _():
            pl.semaphore_wait(barrier, peers)

        def push(src, dst, slot, device):
            return pltpu.make_async_remote_copy(
                src_ref=src, dst_ref=dst, send_sem=send_sem.at[slot], recv_sem=recv_sem.at[slot],
                device_id=device, device_id_type=mesh,
            )

        to_next = [push(k_ref, kp_ref, 0, next_dev), push(v_ref, vp_ref, 1, next_dev)]
        to_prev = [push(k_ref, kn_ref, 2, prev_dev), push(v_ref, vn_ref, 3, prev_dev)]

        @pl.when(has_next)
        def _():
            for copy in to_next:
                copy.start()

        @pl.when(has_prev)
        def _():
            for copy in to_prev:
                copy.start()

        @pl.when(has_prev)
        def _():
            for copy in to_prev:
                copy.wait_send()
            for copy in to_next:
                copy.wait_recv()

        @pl.when(has_next)
        def _():
            for copy in to_next:
                copy.wait_send()
            for copy in to_prev:
                copy.wait_recv()

        @pl.when(jnp.logical_not(has_prev))
        def _():
            kp_ref[...] = jnp.zeros_like(kp_ref)
            vp_ref[...] = jnp.zeros_like(vp_ref)

        @pl.when(jnp.logical_not(has_next))
        def _():
            kn_ref[...] = jnp.zeros_like(kn_ref)
            vn_ref[...] = jnp.zeros_like(vn_ref)

    start = jnp.clip(QTILES * group - 2, 0, TCOLS - KCOLS) * TILE
    key_refs = (kp_ref, k_ref, kn_ref)
    value_refs = (vp_ref, v_ref, vn_ref)
    q = q_ref[...]
    bases = []
    for seg in range(SEGS):
        df, dr = divmod(seg, 3)
        key_row = jnp.clip(row + dr - 1, 0, TROWS - 1)
        base = pl.multiple_of(key_row * (TCOLS * TILE) + start, TILE)
        bases.append(base)
        k = key_refs[df][pl.ds(base, SEG_K), :]
        s_ref[:, seg * SEG_K:(seg + 1) * SEG_K] = lax.dot_general(
            q, k, (((1,), (1,)), ((), ())), preferred_element_type=jnp.float32
        )
    scale = 1.0 / math.sqrt(HEAD_DIM)
    for a in range(QTILES):
        rows = slice(a * TILE, (a + 1) * TILE)
        scores = s_ref[rows, :] * scale + bias_ref[0, a:a + 1, :]
        peak = jnp.max(scores, axis=1, keepdims=True)
        expos = jnp.exp(scores - peak)
        total = jnp.sum(expos, axis=1, keepdims=True)
        p_ref[rows, :] = (expos * (1.0 / total)).astype(jnp.bfloat16)
    acc = jnp.zeros((BLOCK_Q, HEAD_DIM), jnp.float32)
    for seg in range(SEGS):
        df, dr = divmod(seg, 3)
        v = value_refs[df][pl.ds(bases[seg], SEG_K), :]
        acc += jnp.dot(p_ref[:, seg * SEG_K:(seg + 1) * SEG_K], v,
                       preferred_element_type=jnp.float32)
    att_ref[pl.ds(pl.multiple_of((row * GROUPS + group) * BLOCK_Q, BLOCK_Q), BLOCK_Q), :] = (
        acc.astype(att_ref.dtype))

    @pl.when((row == TROWS - 1) & (group == GROUPS - 1))
    def _():
        chunk = got_ref.shape[1] // 2
        copies = []
        for i in range(1, peers):
            peer = lax.rem(me + i, peers)
            for part in range(2):
                src = pl.multiple_of((part * peers + peer) * chunk, chunk)
                copy = pltpu.make_async_remote_copy(
                    src_ref=att_ref.at[pl.ds(src, chunk)],
                    dst_ref=got_ref.at[me, pl.ds(part * chunk, chunk)],
                    send_sem=out_send.at[2 * i + part],
                    recv_sem=out_recv.at[2 * i + part],
                    device_id=(frame, side, peer),
                    device_id_type=mesh,
                )
                copy.start()
                copies.append(copy)
        for part in range(2):
            src = pl.multiple_of((part * peers + me) * chunk, chunk)
            got_ref[me, pl.ds(part * chunk, chunk), :] = att_ref[pl.ds(src, chunk), :]
        for copy in copies:
            copy.wait()
        o_ref[...] = got_ref[...]


def attend(q, k, v, bias):
    tokens = q.shape[0]
    full = pl.BlockSpec((tokens, HEAD_DIM), lambda r, g: (0, 0))
    frame_kv = pltpu.VMEM((tokens, HEAD_DIM), jnp.bfloat16)
    peers = lax.axis_size("hz")
    got_shape = (peers, tokens // peers, HEAD_DIM)
    got = pltpu.VMEM(got_shape, jnp.bfloat16)
    return pl.pallas_call(
        attention_kernel,
        grid=(TROWS, GROUPS),
        in_specs=[pl.BlockSpec((BLOCK_Q, HEAD_DIM), lambda r, g: (r * GROUPS + g, 0))]
        + [full] * 2
        + [pl.BlockSpec((1, QTILES, ROW_K), lambda r, g: (r * GROUPS + g, 0, 0))],
        out_specs=pl.BlockSpec(got_shape, lambda r, g: (0, 0, 0)),
        out_shape=jax.ShapeDtypeStruct(got_shape, jnp.bfloat16),
        scratch_shapes=[frame_kv] * 4 + [
            pltpu.VMEM((BLOCK_Q, ROW_K), jnp.float32),
            pltpu.VMEM((BLOCK_Q, ROW_K), jnp.bfloat16),
            frame_kv,
            got,
            pltpu.SemaphoreType.DMA((4,)),
            pltpu.SemaphoreType.DMA((4,)),
            pltpu.SemaphoreType.DMA((2 * peers,)),
            pltpu.SemaphoreType.DMA((2 * peers,)),
        ],
        compiler_params=pltpu.CompilerParams(collective_id=1, has_side_effects=True),
    )(q, k, v, bias)


def on_device(queries, keys, values, block_mask, out_weight):
    tok_dev = queries.shape[0]
    frames_here = tok_dev // (TROWS * TCOLS * TILE)
    assert frames_here == 1 and queries.shape[1] == HEAD_DIM
    count = lax.axis_size("frame")
    frames_total = frames_here * count
    frame = lax.axis_index("frame") * frames_here
    mask_rows = block_mask.reshape(TROWS * TCOLS, WIN)
    bias = window_bias(mask_rows, frame, frames_total)
    got = attend(queries, keys, values, bias)
    core = lax.axis_index("frame") % 2
    side = lax.axis_index("hy")
    sides = lax.axis_size("hy")
    half = out_weight.shape[1] // 2
    partners = [(i, i ^ 1) for i in range(count)]
    weight_half = lax.dynamic_slice_in_dim(out_weight, core * half, half, axis=1)
    weight_half = lax.all_gather(weight_half, "hz", axis=0, tiled=True)
    peers = lax.axis_size("hz")
    mine = got.transpose(1, 0, 2).reshape(tok_dev // peers, peers * HEAD_DIM)
    block = mine.shape[0] // sides

    def project(x, which):
        rows = lax.dynamic_slice_in_dim(x, which * block, block, axis=0)
        return jnp.dot(rows, weight_half, preferred_element_type=jnp.float32)

    flip = [(0, 1), (1, 0)]
    partial_mine = project(mine, 1 - side).astype(jnp.bfloat16)
    partial_mine, mine = lax.optimization_barrier((partial_mine, mine))
    sent_mine = lax.ppermute(partial_mine, "hy", flip)
    theirs = lax.ppermute(mine, "frame", partners)
    sent_theirs = lax.ppermute(project(theirs, 1 - side).astype(jnp.bfloat16), "hy", flip)
    own_mine = lax.optimization_barrier(project(mine, side))
    own_theirs = lax.optimization_barrier(project(theirs, side))
    other = (own_theirs + sent_theirs.astype(jnp.float32)).astype(jnp.bfloat16)
    other_half = lax.ppermute(other, "frame", partners)
    own_half = (own_mine + sent_mine.astype(jnp.float32)).astype(jnp.bfloat16)
    return jnp.where(
        core == 0,
        jnp.concatenate([own_half, other_half], axis=1),
        jnp.concatenate([other_half, own_half], axis=1),
    )


def solution(mesh):
    frames, heads = mesh.devices.shape
    grid = mesh.devices.reshape(frames, 2, heads // 2)
    split = jax.sharding.Mesh(grid, ("frame", "hy", "hz"))
    head = ("hy", "hz")
    return jax.shard_map(
        on_device,
        mesh=split,
        in_specs=(
            P("frame", head),
            P("frame", head),
            P("frame", head),
            P(head, "frame", None, None),
            P(head, None),
        ),
        out_specs=P(("frame",) + head, None),
        check_vma=False,
    )
```

```python
import math

import numpy as np
import jax
import jax.numpy as jnp
from jax import lax
from jax.experimental import pallas as pl
from jax.experimental.pallas import tpu as pltpu
from jax.sharding import PartitionSpec as P

HEAD_DIM = 128
TROWS = 4
TCOLS = 8
WIN = 45
TILE = 64
QTILES = 2
KCOLS = 6
SEGS = 9
BLOCK_Q = QTILES * TILE
SEG_K = KCOLS * TILE
ROW_K = SEGS * SEG_K
GROUPS = TCOLS // QTILES


def window_tables():
    shape = (TROWS * GROUPS, QTILES, SEGS, KCOLS)
    qtile = np.zeros(shape, np.int32)
    offset = np.zeros(shape, np.int32)
    static_ok = np.zeros(shape, bool)
    centre = np.zeros(shape, bool)
    frame_step = np.zeros(shape, np.int32)
    for row in range(TROWS):
        for group in range(GROUPS):
            start = min(max(QTILES * group - 2, 0), TCOLS - KCOLS)
            for a in range(QTILES):
                col = QTILES * group + a
                for seg in range(SEGS):
                    df, dr = divmod(seg, 3)
                    for j in range(KCOLS):
                        dc = start + j - col
                        b = row * GROUPS + group
                        qtile[b, a, seg, j] = row * TCOLS + col
                        ok = abs(dc) <= 2 and 0 <= row + dr - 1 < TROWS
                        static_ok[b, a, seg, j] = ok
                        offset[b, a, seg, j] = 15 * df + 5 * dr + dc + 2 if ok else 0
                        centre[b, a, seg, j] = df == 1 and dr == 1 and dc == 0
                        frame_step[b, a, seg, j] = df - 1
    return qtile, offset, static_ok, centre, frame_step


def window_picks():
    picks = np.zeros((TCOLS, WIN, SEGS, KCOLS), np.float32)
    for col in range(TCOLS):
        start = min(max(QTILES * (col // QTILES) - 2, 0), TCOLS - KCOLS)
        for seg in range(SEGS):
            df, dr = divmod(seg, 3)
            for j in range(KCOLS):
                dc = start + j - col
                if abs(dc) <= 2:
                    picks[col, 15 * df + 5 * dr + dc + 2, seg, j] = 1.0
    return picks


def window_bias(mask_rows, frame, frames_total):
    qtile, offset, static_ok, centre, frame_step = window_tables()
    grid = mask_rows.astype(jnp.float32).reshape(TROWS, TCOLS, WIN)
    chosen = jnp.einsum("rcw,cwk->rck", grid, window_picks().reshape(TCOLS, WIN, SEGS * KCOLS))
    chosen = chosen.reshape(static_ok.shape) > 0.5
    key_frame = frame + frame_step
    inside = (key_frame >= 0) & (key_frame < frames_total)
    allowed = (chosen | centre) & static_ok & inside
    bias = jnp.where(allowed, 0.0, -jnp.inf).astype(jnp.float32)
    bias = jnp.broadcast_to(bias[..., None], bias.shape + (TILE,))
    return bias.reshape(TROWS * GROUPS, QTILES, ROW_K)


def attention_kernel(q_ref, k_ref, v_ref, bias_ref, o_ref, o2_ref,
                     kp_ref, kn_ref, vp_ref, vn_ref, s_ref, p_ref, att_ref, got_ref, their_ref,
                     send_sem, recv_sem, out_send, out_recv, pair_send, pair_recv):
    row = pl.program_id(0)
    group = pl.program_id(1)
    frame = lax.axis_index("frame")
    side = lax.axis_index("hy")
    me = lax.axis_index("hz")
    peers = lax.axis_size("hz")
    mesh = pl.DeviceIdType.MESH
    partner = frame + 1 - 2 * (frame % 2)

    @pl.when((row == 0) & (group == 0))
    def _():
        count = lax.axis_size("frame")
        peer = me
        has_prev = frame > 0
        has_next = frame < count - 1
        prev_dev = (frame - 1, side, peer)
        next_dev = (frame + 1, side, peer)
        barrier = pltpu.get_barrier_semaphore()

        @pl.when(has_prev)
        def _():
            pl.semaphore_signal(barrier, inc=1, device_id=prev_dev, device_id_type=mesh)

        @pl.when(has_next)
        def _():
            pl.semaphore_signal(barrier, inc=1, device_id=next_dev, device_id_type=mesh)

        for i in range(1, peers):
            other = (frame, side, lax.rem(me + i, peers))
            pl.semaphore_signal(barrier, inc=1, device_id=other, device_id_type=mesh)
        for j in range(peers):
            other = (partner, side, j)
            pl.semaphore_signal(barrier, inc=1, device_id=other, device_id_type=mesh)

        @pl.when(has_prev & has_next)
        def _():
            pl.semaphore_wait(barrier, 2 * peers + 1)

        @pl.when(has_prev != has_next)
        def _():
            pl.semaphore_wait(barrier, 2 * peers)

        def push(src, dst, slot, device):
            return pltpu.make_async_remote_copy(
                src_ref=src, dst_ref=dst, send_sem=send_sem.at[slot], recv_sem=recv_sem.at[slot],
                device_id=device, device_id_type=mesh,
            )

        to_next = [push(k_ref, kp_ref, 0, next_dev), push(v_ref, vp_ref, 1, next_dev)]
        to_prev = [push(k_ref, kn_ref, 2, prev_dev), push(v_ref, vn_ref, 3, prev_dev)]

        @pl.when(has_next)
        def _():
            for copy in to_next:
                copy.start()

        @pl.when(has_prev)
        def _():
            for copy in to_prev:
                copy.start()

        @pl.when(has_prev)
        def _():
            for copy in to_prev:
                copy.wait_send()
            for copy in to_next:
                copy.wait_recv()

        @pl.when(has_next)
        def _():
            for copy in to_next:
                copy.wait_send()
            for copy in to_prev:
                copy.wait_recv()

        @pl.when(jnp.logical_not(has_prev))
        def _():
            kp_ref[...] = jnp.zeros_like(kp_ref)
            vp_ref[...] = jnp.zeros_like(vp_ref)

        @pl.when(jnp.logical_not(has_next))
        def _():
            kn_ref[...] = jnp.zeros_like(kn_ref)
            vn_ref[...] = jnp.zeros_like(vn_ref)

    start = jnp.clip(QTILES * group - 2, 0, TCOLS - KCOLS) * TILE
    key_refs = (kp_ref, k_ref, kn_ref)
    value_refs = (vp_ref, v_ref, vn_ref)
    q = q_ref[...]
    bases = []
    for seg in range(SEGS):
        df, dr = divmod(seg, 3)
        key_row = jnp.clip(row + dr - 1, 0, TROWS - 1)
        base = pl.multiple_of(key_row * (TCOLS * TILE) + start, TILE)
        bases.append(base)
        k = key_refs[df][pl.ds(base, SEG_K), :]
        s_ref[:, seg * SEG_K:(seg + 1) * SEG_K] = lax.dot_general(
            q, k, (((1,), (1,)), ((), ())), preferred_element_type=jnp.float32
        )
    scale = 1.0 / math.sqrt(HEAD_DIM)
    for a in range(QTILES):
        rows = slice(a * TILE, (a + 1) * TILE)
        scores = s_ref[rows, :] * scale + bias_ref[0, a:a + 1, :]
        peak = jnp.max(scores, axis=1, keepdims=True)
        expos = jnp.exp(scores - peak)
        total = jnp.sum(expos, axis=1, keepdims=True)
        p_ref[rows, :] = (expos * (1.0 / total)).astype(jnp.bfloat16)
    acc = jnp.zeros((BLOCK_Q, HEAD_DIM), jnp.float32)
    for seg in range(SEGS):
        df, dr = divmod(seg, 3)
        v = value_refs[df][pl.ds(bases[seg], SEG_K), :]
        acc += jnp.dot(p_ref[:, seg * SEG_K:(seg + 1) * SEG_K], v,
                       preferred_element_type=jnp.float32)
    att_ref[pl.ds(pl.multiple_of((row * GROUPS + group) * BLOCK_Q, BLOCK_Q), BLOCK_Q), :] = (
        acc.astype(att_ref.dtype))

    @pl.when((row == TROWS - 1) & (group == GROUPS - 1))
    def _():
        chunk = got_ref.shape[1] // 2
        copies = []
        for i in range(1, peers):
            peer = lax.rem(me + i, peers)
            for part in range(2):
                src = pl.multiple_of((part * peers + peer) * chunk, chunk)
                copy = pltpu.make_async_remote_copy(
                    src_ref=att_ref.at[pl.ds(src, chunk)],
                    dst_ref=got_ref.at[me, pl.ds(part * chunk, chunk)],
                    send_sem=out_send.at[2 * i + part],
                    recv_sem=out_recv.at[2 * i + part],
                    device_id=(frame, side, peer),
                    device_id_type=mesh,
                )
                copy.start()
                copies.append(copy)
        for i in range(peers):
            peer = lax.rem(me + i, peers)
            for part in range(2):
                src = pl.multiple_of((part * peers + peer) * chunk, chunk)
                copy = pltpu.make_async_remote_copy(
                    src_ref=att_ref.at[pl.ds(src, chunk)],
                    dst_ref=their_ref.at[me, pl.ds(part * chunk, chunk)],
                    send_sem=pair_send.at[2 * i + part],
                    recv_sem=pair_recv.at[2 * i + part],
                    device_id=(partner, side, peer),
                    device_id_type=mesh,
                )
                copy.start()
                copies.append(copy)
        for part in range(2):
            src = pl.multiple_of((part * peers + me) * chunk, chunk)
            got_ref[me, pl.ds(part * chunk, chunk), :] = att_ref[pl.ds(src, chunk), :]
        for copy in copies:
            copy.wait()
        o_ref[...] = got_ref[...]
        o2_ref[...] = their_ref[...]


def attend(q, k, v, bias):
    tokens = q.shape[0]
    full = pl.BlockSpec((tokens, HEAD_DIM), lambda r, g: (0, 0))
    frame_kv = pltpu.VMEM((tokens, HEAD_DIM), jnp.bfloat16)
    peers = lax.axis_size("hz")
    got_shape = (peers, tokens // peers, HEAD_DIM)
    got = pltpu.VMEM(got_shape, jnp.bfloat16)
    return pl.pallas_call(
        attention_kernel,
        grid=(TROWS, GROUPS),
        in_specs=[pl.BlockSpec((BLOCK_Q, HEAD_DIM), lambda r, g: (r * GROUPS + g, 0))]
        + [full] * 2
        + [pl.BlockSpec((1, QTILES, ROW_K), lambda r, g: (r * GROUPS + g, 0, 0))],
        out_specs=[pl.BlockSpec(got_shape, lambda r, g: (0, 0, 0))] * 2,
        out_shape=[jax.ShapeDtypeStruct(got_shape, jnp.bfloat16)] * 2,
        scratch_shapes=[frame_kv] * 4 + [
            pltpu.VMEM((BLOCK_Q, ROW_K), jnp.float32),
            pltpu.VMEM((BLOCK_Q, ROW_K), jnp.bfloat16),
            frame_kv,
            got,
            got,
            pltpu.SemaphoreType.DMA((4,)),
            pltpu.SemaphoreType.DMA((4,)),
            pltpu.SemaphoreType.DMA((2 * peers,)),
            pltpu.SemaphoreType.DMA((2 * peers,)),
            pltpu.SemaphoreType.DMA((2 * peers,)),
            pltpu.SemaphoreType.DMA((2 * peers,)),
        ],
        compiler_params=pltpu.CompilerParams(collective_id=1, has_side_effects=True),
    )(q, k, v, bias)


def on_device(queries, keys, values, block_mask, out_weight):
    tok_dev = queries.shape[0]
    frames_here = tok_dev // (TROWS * TCOLS * TILE)
    assert frames_here == 1 and queries.shape[1] == HEAD_DIM
    count = lax.axis_size("frame")
    frames_total = frames_here * count
    frame = lax.axis_index("frame") * frames_here
    mask_rows = block_mask.reshape(TROWS * TCOLS, WIN)
    bias = window_bias(mask_rows, frame, frames_total)
    got, got_theirs = attend(queries, keys, values, bias)
    core = lax.axis_index("frame") % 2
    side = lax.axis_index("hy")
    sides = lax.axis_size("hy")
    half = out_weight.shape[1] // 2
    partners = [(i, i ^ 1) for i in range(count)]
    weight_half = lax.dynamic_slice_in_dim(out_weight, core * half, half, axis=1)
    weight_half = lax.all_gather(weight_half, "hz", axis=0, tiled=True)
    peers = lax.axis_size("hz")
    mine = got.transpose(1, 0, 2).reshape(tok_dev // peers, peers * HEAD_DIM)
    block = mine.shape[0] // sides

    def project(x, which):
        rows = lax.dynamic_slice_in_dim(x, which * block, block, axis=0)
        return jnp.dot(rows, weight_half, preferred_element_type=jnp.float32)

    flip = [(0, 1), (1, 0)]
    partial_mine = project(mine, 1 - side).astype(jnp.bfloat16)
    partial_mine, mine = lax.optimization_barrier((partial_mine, mine))
    sent_mine = lax.ppermute(partial_mine, "hy", flip)
    theirs = got_theirs.transpose(1, 0, 2).reshape(tok_dev // peers, peers * HEAD_DIM)
    sent_theirs = lax.ppermute(project(theirs, 1 - side).astype(jnp.bfloat16), "hy", flip)
    own_mine = lax.optimization_barrier(project(mine, side))
    own_theirs = lax.optimization_barrier(project(theirs, side))
    other = (own_theirs + sent_theirs.astype(jnp.float32)).astype(jnp.bfloat16)
    other_half = lax.ppermute(other, "frame", partners)
    own_half = (own_mine + sent_mine.astype(jnp.float32)).astype(jnp.bfloat16)
    return jnp.where(
        core == 0,
        jnp.concatenate([own_half, other_half], axis=1),
        jnp.concatenate([other_half, own_half], axis=1),
    )


def solution(mesh):
    frames, heads = mesh.devices.shape
    grid = mesh.devices.reshape(frames, 2, heads // 2)
    split = jax.sharding.Mesh(grid, ("frame", "hy", "hz"))
    head = ("hy", "hz")
    return jax.shard_map(
        on_device,
        mesh=split,
        in_specs=(
            P("frame", head),
            P("frame", head),
            P("frame", head),
            P(head, "frame", None, None),
            P(head, None),
        ),
        out_specs=P(("frame",) + head, None),
        check_vma=False,
    )
```

```python
import math

import numpy as np
import jax
import jax.numpy as jnp
from jax import lax
from jax.experimental import pallas as pl
from jax.experimental.pallas import tpu as pltpu
from jax.sharding import PartitionSpec as P

HEAD_DIM = 128
TROWS = 4
TCOLS = 8
WIN = 45
TILE = 64
QTILES = 2
KCOLS = 6
SEGS = 9
BLOCK_Q = QTILES * TILE
SEG_K = KCOLS * TILE
ROW_K = SEGS * SEG_K
GROUPS = TCOLS // QTILES


def window_tables():
    shape = (TROWS * GROUPS, QTILES, SEGS, KCOLS)
    qtile = np.zeros(shape, np.int32)
    offset = np.zeros(shape, np.int32)
    static_ok = np.zeros(shape, bool)
    centre = np.zeros(shape, bool)
    frame_step = np.zeros(shape, np.int32)
    for row in range(TROWS):
        for group in range(GROUPS):
            start = min(max(QTILES * group - 2, 0), TCOLS - KCOLS)
            for a in range(QTILES):
                col = QTILES * group + a
                for seg in range(SEGS):
                    df, dr = divmod(seg, 3)
                    for j in range(KCOLS):
                        dc = start + j - col
                        b = row * GROUPS + group
                        qtile[b, a, seg, j] = row * TCOLS + col
                        ok = abs(dc) <= 2 and 0 <= row + dr - 1 < TROWS
                        static_ok[b, a, seg, j] = ok
                        offset[b, a, seg, j] = 15 * df + 5 * dr + dc + 2 if ok else 0
                        centre[b, a, seg, j] = df == 1 and dr == 1 and dc == 0
                        frame_step[b, a, seg, j] = df - 1
    return qtile, offset, static_ok, centre, frame_step


def window_picks():
    picks = np.zeros((TCOLS, WIN, SEGS, KCOLS), np.float32)
    for col in range(TCOLS):
        start = min(max(QTILES * (col // QTILES) - 2, 0), TCOLS - KCOLS)
        for seg in range(SEGS):
            df, dr = divmod(seg, 3)
            for j in range(KCOLS):
                dc = start + j - col
                if abs(dc) <= 2:
                    picks[col, 15 * df + 5 * dr + dc + 2, seg, j] = 1.0
    return picks


def window_bias(mask_rows, frame, frames_total):
    qtile, offset, static_ok, centre, frame_step = window_tables()
    grid = mask_rows.astype(jnp.float32).reshape(TROWS, TCOLS, WIN)
    chosen = jnp.einsum("rcw,cwk->rck", grid, window_picks().reshape(TCOLS, WIN, SEGS * KCOLS))
    chosen = chosen.reshape(static_ok.shape) > 0.5
    key_frame = frame + frame_step
    inside = (key_frame >= 0) & (key_frame < frames_total)
    allowed = (chosen | centre) & static_ok & inside
    bias = jnp.where(allowed, 0.0, -jnp.inf).astype(jnp.float32)
    bias = jnp.broadcast_to(bias[..., None], bias.shape + (TILE,))
    return bias.reshape(TROWS * GROUPS, QTILES, ROW_K)


def attention_kernel(q_ref, k_ref, v_ref, bias_ref, o_ref,
                     kp_ref, kn_ref, vp_ref, vn_ref, s_ref, p_ref, att_ref, got_ref,
                     send_sem, recv_sem, out_send, out_recv):
    row = pl.program_id(0)
    group = pl.program_id(1)
    frame = lax.axis_index("frame")
    side = lax.axis_index("hy")
    me = lax.axis_index("hz")
    peers = lax.axis_size("hz")
    mesh = pl.DeviceIdType.MESH

    @pl.when((row == 0) & (group == 0))
    def _():
        count = lax.axis_size("frame")
        peer = me
        has_prev = frame > 0
        has_next = frame < count - 1
        prev_dev = (frame - 1, side, peer)
        next_dev = (frame + 1, side, peer)
        barrier = pltpu.get_barrier_semaphore()

        @pl.when(has_prev)
        def _():
            pl.semaphore_signal(barrier, inc=1, device_id=prev_dev, device_id_type=mesh)

        @pl.when(has_next)
        def _():
            pl.semaphore_signal(barrier, inc=1, device_id=next_dev, device_id_type=mesh)

        for i in range(1, peers):
            other = (frame, side, lax.rem(me + i, peers))
            pl.semaphore_signal(barrier, inc=1, device_id=other, device_id_type=mesh)

        @pl.when(has_prev & has_next)
        def _():
            pl.semaphore_wait(barrier, peers + 1)

        @pl.when(has_prev != has_next)
        def _():
            pl.semaphore_wait(barrier, peers)

        def push(src, dst, slot, device):
            return pltpu.make_async_remote_copy(
                src_ref=src, dst_ref=dst, send_sem=send_sem.at[slot], recv_sem=recv_sem.at[slot],
                device_id=device, device_id_type=mesh,
            )

        to_next = [push(k_ref, kp_ref, 0, next_dev), push(v_ref, vp_ref, 1, next_dev)]
        to_prev = [push(k_ref, kn_ref, 2, prev_dev), push(v_ref, vn_ref, 3, prev_dev)]

        @pl.when(has_next)
        def _():
            for copy in to_next:
                copy.start()

        @pl.when(has_prev)
        def _():
            for copy in to_prev:
                copy.start()

        @pl.when(has_prev)
        def _():
            for copy in to_prev:
                copy.wait_send()
            for copy in to_next:
                copy.wait_recv()

        @pl.when(has_next)
        def _():
            for copy in to_next:
                copy.wait_send()
            for copy in to_prev:
                copy.wait_recv()

        @pl.when(jnp.logical_not(has_prev))
        def _():
            kp_ref[...] = jnp.zeros_like(kp_ref)
            vp_ref[...] = jnp.zeros_like(vp_ref)

        @pl.when(jnp.logical_not(has_next))
        def _():
            kn_ref[...] = jnp.zeros_like(kn_ref)
            vn_ref[...] = jnp.zeros_like(vn_ref)

    start = jnp.clip(QTILES * group - 2, 0, TCOLS - KCOLS) * TILE
    key_refs = (kp_ref, k_ref, kn_ref)
    value_refs = (vp_ref, v_ref, vn_ref)
    q = q_ref[...]
    bases = []
    for seg in range(SEGS):
        df, dr = divmod(seg, 3)
        key_row = jnp.clip(row + dr - 1, 0, TROWS - 1)
        base = pl.multiple_of(key_row * (TCOLS * TILE) + start, TILE)
        bases.append(base)
        k = key_refs[df][pl.ds(base, SEG_K), :]
        s_ref[:, seg * SEG_K:(seg + 1) * SEG_K] = lax.dot_general(
            q, k, (((1,), (1,)), ((), ())), preferred_element_type=jnp.float32
        )
    scale = 1.0 / math.sqrt(HEAD_DIM)
    for a in range(QTILES):
        rows = slice(a * TILE, (a + 1) * TILE)
        scores = s_ref[rows, :] * scale + bias_ref[0, a:a + 1, :]
        peak = jnp.max(scores, axis=1, keepdims=True)
        expos = jnp.exp(scores - peak)
        total = jnp.sum(expos, axis=1, keepdims=True)
        p_ref[rows, :] = (expos * (1.0 / total)).astype(jnp.bfloat16)
    acc = jnp.zeros((BLOCK_Q, HEAD_DIM), jnp.float32)
    for seg in range(SEGS):
        df, dr = divmod(seg, 3)
        v = value_refs[df][pl.ds(bases[seg], SEG_K), :]
        acc += jnp.dot(p_ref[:, seg * SEG_K:(seg + 1) * SEG_K], v,
                       preferred_element_type=jnp.float32)
    att_ref[pl.ds(pl.multiple_of((row * GROUPS + group) * BLOCK_Q, BLOCK_Q), BLOCK_Q), :] = (
        acc.astype(att_ref.dtype))

    @pl.when((row == TROWS - 1) & (group == GROUPS - 1))
    def _():
        chunk = got_ref.shape[1] // 2
        copies = []
        for i in range(1, peers):
            peer = lax.rem(me + i, peers)
            for part in range(2):
                src = pl.multiple_of((part * peers + peer) * chunk, chunk)
                copy = pltpu.make_async_remote_copy(
                    src_ref=att_ref.at[pl.ds(src, chunk)],
                    dst_ref=got_ref.at[me, pl.ds(part * chunk, chunk)],
                    send_sem=out_send.at[2 * i + part],
                    recv_sem=out_recv.at[2 * i + part],
                    device_id=(frame, side, peer),
                    device_id_type=mesh,
                )
                copy.start()
                copies.append(copy)
        for part in range(2):
            src = pl.multiple_of((part * peers + me) * chunk, chunk)
            got_ref[me, pl.ds(part * chunk, chunk), :] = att_ref[pl.ds(src, chunk), :]
        for copy in copies:
            copy.wait()
        o_ref[...] = got_ref[...]


def attend(q, k, v, bias):
    tokens = q.shape[0]
    full = pl.BlockSpec((tokens, HEAD_DIM), lambda r, g: (0, 0))
    frame_kv = pltpu.VMEM((tokens, HEAD_DIM), jnp.bfloat16)
    peers = lax.axis_size("hz")
    got_shape = (peers, tokens // peers, HEAD_DIM)
    got = pltpu.VMEM(got_shape, jnp.bfloat16)
    return pl.pallas_call(
        attention_kernel,
        grid=(TROWS, GROUPS),
        in_specs=[pl.BlockSpec((BLOCK_Q, HEAD_DIM), lambda r, g: (r * GROUPS + g, 0))]
        + [full] * 2
        + [pl.BlockSpec((1, QTILES, ROW_K), lambda r, g: (r * GROUPS + g, 0, 0))],
        out_specs=pl.BlockSpec(got_shape, lambda r, g: (0, 0, 0)),
        out_shape=jax.ShapeDtypeStruct(got_shape, jnp.bfloat16),
        scratch_shapes=[frame_kv] * 4 + [
            pltpu.VMEM((BLOCK_Q, ROW_K), jnp.float32),
            pltpu.VMEM((BLOCK_Q, ROW_K), jnp.bfloat16),
            frame_kv,
            got,
            pltpu.SemaphoreType.DMA((4,)),
            pltpu.SemaphoreType.DMA((4,)),
            pltpu.SemaphoreType.DMA((2 * peers,)),
            pltpu.SemaphoreType.DMA((2 * peers,)),
        ],
        compiler_params=pltpu.CompilerParams(collective_id=1, has_side_effects=True),
    )(q, k, v, bias)


def on_device(queries, keys, values, block_mask, out_weight):
    tok_dev = queries.shape[0]
    frames_here = tok_dev // (TROWS * TCOLS * TILE)
    assert frames_here == 1 and queries.shape[1] == HEAD_DIM
    count = lax.axis_size("frame")
    frames_total = frames_here * count
    frame = lax.axis_index("frame") * frames_here
    mask_rows = block_mask.reshape(TROWS * TCOLS, WIN)
    bias = window_bias(mask_rows, frame, frames_total)
    got = attend(queries, keys, values, bias)
    core = lax.axis_index("frame") % 2
    side = lax.axis_index("hy")
    sides = lax.axis_size("hy")
    half = out_weight.shape[1] // 2
    partners = [(i, i ^ 1) for i in range(count)]
    weight_half = lax.dynamic_slice_in_dim(out_weight, core * half, half, axis=1)
    weight_half = lax.all_gather(weight_half, "hz", axis=0, tiled=True)
    peers = lax.axis_size("hz")
    mine = got.transpose(1, 0, 2).reshape(tok_dev // peers, peers * HEAD_DIM)
    block = mine.shape[0] // sides

    def project(x, which):
        rows = lax.dynamic_slice_in_dim(x, which * block, block, axis=0)
        return jnp.dot(rows, weight_half, preferred_element_type=jnp.float32)

    flip = [(0, 1), (1, 0)]
    theirs = lax.ppermute(mine, "frame", partners)
    partials = jnp.stack([project(mine, 1 - side), project(theirs, 1 - side)]).astype(jnp.bfloat16)
    sent_mine, sent_theirs = lax.ppermute(partials, "hy", flip)
    own_mine = lax.optimization_barrier(project(mine, side))
    own_theirs = lax.optimization_barrier(project(theirs, side))
    other = (own_theirs + sent_theirs.astype(jnp.float32)).astype(jnp.bfloat16)
    other_half = lax.ppermute(other, "frame", partners)
    own_half = (own_mine + sent_mine.astype(jnp.float32)).astype(jnp.bfloat16)
    return jnp.where(
        core == 0,
        jnp.concatenate([own_half, other_half], axis=1),
        jnp.concatenate([other_half, own_half], axis=1),
    )


def solution(mesh):
    frames, heads = mesh.devices.shape
    grid = mesh.devices.reshape(frames, 2, heads // 2)
    split = jax.sharding.Mesh(grid, ("frame", "hy", "hz"))
    head = ("hy", "hz")
    return jax.shard_map(
        on_device,
        mesh=split,
        in_specs=(
            P("frame", head),
            P("frame", head),
            P("frame", head),
            P(head, "frame", None, None),
            P(head, None),
        ),
        out_specs=P(("frame",) + head, None),
        check_vma=False,
    )
```

```python
import math

import numpy as np
import jax
import jax.numpy as jnp
from jax import lax
from jax.experimental import pallas as pl
from jax.experimental.pallas import tpu as pltpu
from jax.sharding import PartitionSpec as P

HEAD_DIM = 128
TROWS = 4
TCOLS = 8
WIN = 45
TILE = 64
QTILES = 2
KCOLS = 6
SEGS = 9
BLOCK_Q = QTILES * TILE
SEG_K = KCOLS * TILE
ROW_K = SEGS * SEG_K
GROUPS = TCOLS // QTILES


def window_tables():
    shape = (TROWS * GROUPS, QTILES, SEGS, KCOLS)
    qtile = np.zeros(shape, np.int32)
    offset = np.zeros(shape, np.int32)
    static_ok = np.zeros(shape, bool)
    centre = np.zeros(shape, bool)
    frame_step = np.zeros(shape, np.int32)
    for row in range(TROWS):
        for group in range(GROUPS):
            start = min(max(QTILES * group - 2, 0), TCOLS - KCOLS)
            for a in range(QTILES):
                col = QTILES * group + a
                for seg in range(SEGS):
                    df, dr = divmod(seg, 3)
                    for j in range(KCOLS):
                        dc = start + j - col
                        b = row * GROUPS + group
                        qtile[b, a, seg, j] = row * TCOLS + col
                        ok = abs(dc) <= 2 and 0 <= row + dr - 1 < TROWS
                        static_ok[b, a, seg, j] = ok
                        offset[b, a, seg, j] = 15 * df + 5 * dr + dc + 2 if ok else 0
                        centre[b, a, seg, j] = df == 1 and dr == 1 and dc == 0
                        frame_step[b, a, seg, j] = df - 1
    return qtile, offset, static_ok, centre, frame_step


def window_picks():
    picks = np.zeros((TCOLS, WIN, SEGS, KCOLS), np.float32)
    for col in range(TCOLS):
        start = min(max(QTILES * (col // QTILES) - 2, 0), TCOLS - KCOLS)
        for seg in range(SEGS):
            df, dr = divmod(seg, 3)
            for j in range(KCOLS):
                dc = start + j - col
                if abs(dc) <= 2:
                    picks[col, 15 * df + 5 * dr + dc + 2, seg, j] = 1.0
    return picks


def window_bias(mask_rows, frame, frames_total):
    qtile, offset, static_ok, centre, frame_step = window_tables()
    grid = mask_rows.astype(jnp.float32).reshape(TROWS, TCOLS, WIN)
    chosen = jnp.einsum("rcw,cwk->rck", grid, window_picks().reshape(TCOLS, WIN, SEGS * KCOLS))
    chosen = chosen.reshape(static_ok.shape) > 0.5
    key_frame = frame + frame_step
    inside = (key_frame >= 0) & (key_frame < frames_total)
    allowed = (chosen | centre) & static_ok & inside
    bias = jnp.where(allowed, 0.0, -jnp.inf).astype(jnp.float32)
    bias = jnp.broadcast_to(bias[..., None], bias.shape + (TILE,))
    return bias.reshape(TROWS * GROUPS, QTILES, ROW_K)


def attention_kernel(q_ref, k_ref, v_ref, bias_ref, o_ref,
                     kp_ref, kn_ref, vp_ref, vn_ref, s_ref, p_ref, att_ref, got_ref,
                     send_sem, recv_sem, out_send, out_recv):
    row = pl.program_id(0)
    group = pl.program_id(1)
    frame = lax.axis_index("frame")
    side = lax.axis_index("hy")
    me = lax.axis_index("hz")
    peers = lax.axis_size("hz")
    mesh = pl.DeviceIdType.MESH

    @pl.when((row == 0) & (group == 0))
    def _():
        count = lax.axis_size("frame")
        peer = me
        has_prev = frame > 0
        has_next = frame < count - 1
        prev_dev = (frame - 1, side, peer)
        next_dev = (frame + 1, side, peer)
        barrier = pltpu.get_barrier_semaphore()

        @pl.when(has_prev)
        def _():
            pl.semaphore_signal(barrier, inc=1, device_id=prev_dev, device_id_type=mesh)

        @pl.when(has_next)
        def _():
            pl.semaphore_signal(barrier, inc=1, device_id=next_dev, device_id_type=mesh)

        for i in range(1, peers):
            other = (frame, side, lax.rem(me + i, peers))
            pl.semaphore_signal(barrier, inc=1, device_id=other, device_id_type=mesh)

        @pl.when(has_prev & has_next)
        def _():
            pl.semaphore_wait(barrier, peers + 1)

        @pl.when(has_prev != has_next)
        def _():
            pl.semaphore_wait(barrier, peers)

        def push(src, dst, slot, device):
            return pltpu.make_async_remote_copy(
                src_ref=src, dst_ref=dst, send_sem=send_sem.at[slot], recv_sem=recv_sem.at[slot],
                device_id=device, device_id_type=mesh,
            )

        to_next = [push(k_ref, kp_ref, 0, next_dev), push(v_ref, vp_ref, 1, next_dev)]
        to_prev = [push(k_ref, kn_ref, 2, prev_dev), push(v_ref, vn_ref, 3, prev_dev)]

        @pl.when(has_next)
        def _():
            for copy in to_next:
                copy.start()

        @pl.when(has_prev)
        def _():
            for copy in to_prev:
                copy.start()

        @pl.when(has_prev)
        def _():
            for copy in to_prev:
                copy.wait_send()
            for copy in to_next:
                copy.wait_recv()

        @pl.when(has_next)
        def _():
            for copy in to_next:
                copy.wait_send()
            for copy in to_prev:
                copy.wait_recv()

        @pl.when(jnp.logical_not(has_prev))
        def _():
            kp_ref[...] = jnp.zeros_like(kp_ref)
            vp_ref[...] = jnp.zeros_like(vp_ref)

        @pl.when(jnp.logical_not(has_next))
        def _():
            kn_ref[...] = jnp.zeros_like(kn_ref)
            vn_ref[...] = jnp.zeros_like(vn_ref)

    start = jnp.clip(QTILES * group - 2, 0, TCOLS - KCOLS) * TILE
    key_refs = (kp_ref, k_ref, kn_ref)
    value_refs = (vp_ref, v_ref, vn_ref)
    q = q_ref[...]
    bases = []
    for seg in range(SEGS):
        df, dr = divmod(seg, 3)
        key_row = jnp.clip(row + dr - 1, 0, TROWS - 1)
        base = pl.multiple_of(key_row * (TCOLS * TILE) + start, TILE)
        bases.append(base)
        k = key_refs[df][pl.ds(base, SEG_K), :]
        s_ref[:, seg * SEG_K:(seg + 1) * SEG_K] = lax.dot_general(
            q, k, (((1,), (1,)), ((), ())), preferred_element_type=jnp.float32
        )
    scale = 1.0 / math.sqrt(HEAD_DIM)
    inverse = []
    for a in range(QTILES):
        rows = slice(a * TILE, (a + 1) * TILE)
        scores = s_ref[rows, :] + bias_ref[0, a:a + 1, :]
        peak = jnp.max(scores, axis=1, keepdims=True)
        expos = jnp.exp((scores - peak) * scale)
        inverse.append(1.0 / jnp.sum(expos, axis=1, keepdims=True))
        p_ref[rows, :] = expos.astype(jnp.bfloat16)
    acc = jnp.zeros((BLOCK_Q, HEAD_DIM), jnp.float32)
    for seg in range(SEGS):
        df, dr = divmod(seg, 3)
        v = value_refs[df][pl.ds(bases[seg], SEG_K), :]
        acc += jnp.dot(p_ref[:, seg * SEG_K:(seg + 1) * SEG_K], v,
                       preferred_element_type=jnp.float32)
    acc = acc * jnp.concatenate(inverse, axis=0)
    att_ref[pl.ds(pl.multiple_of((row * GROUPS + group) * BLOCK_Q, BLOCK_Q), BLOCK_Q), :] = (
        acc.astype(att_ref.dtype))

    @pl.when((row == TROWS - 1) & (group == GROUPS - 1))
    def _():
        chunk = got_ref.shape[1] // 2
        copies = []
        for i in range(1, peers):
            peer = lax.rem(me + i, peers)
            for part in range(2):
                src = pl.multiple_of((part * peers + peer) * chunk, chunk)
                copy = pltpu.make_async_remote_copy(
                    src_ref=att_ref.at[pl.ds(src, chunk)],
                    dst_ref=got_ref.at[me, pl.ds(part * chunk, chunk)],
                    send_sem=out_send.at[2 * i + part],
                    recv_sem=out_recv.at[2 * i + part],
                    device_id=(frame, side, peer),
                    device_id_type=mesh,
                )
                copy.start()
                copies.append(copy)
        for part in range(2):
            src = pl.multiple_of((part * peers + me) * chunk, chunk)
            got_ref[me, pl.ds(part * chunk, chunk), :] = att_ref[pl.ds(src, chunk), :]
        for copy in copies:
            copy.wait()
        o_ref[...] = got_ref[...]


def attend(q, k, v, bias):
    tokens = q.shape[0]
    full = pl.BlockSpec((tokens, HEAD_DIM), lambda r, g: (0, 0))
    frame_kv = pltpu.VMEM((tokens, HEAD_DIM), jnp.bfloat16)
    peers = lax.axis_size("hz")
    got_shape = (peers, tokens // peers, HEAD_DIM)
    got = pltpu.VMEM(got_shape, jnp.bfloat16)
    return pl.pallas_call(
        attention_kernel,
        grid=(TROWS, GROUPS),
        in_specs=[pl.BlockSpec((BLOCK_Q, HEAD_DIM), lambda r, g: (r * GROUPS + g, 0))]
        + [full] * 2
        + [pl.BlockSpec((1, QTILES, ROW_K), lambda r, g: (r * GROUPS + g, 0, 0))],
        out_specs=pl.BlockSpec(got_shape, lambda r, g: (0, 0, 0)),
        out_shape=jax.ShapeDtypeStruct(got_shape, jnp.bfloat16),
        scratch_shapes=[frame_kv] * 4 + [
            pltpu.VMEM((BLOCK_Q, ROW_K), jnp.float32),
            pltpu.VMEM((BLOCK_Q, ROW_K), jnp.bfloat16),
            frame_kv,
            got,
            pltpu.SemaphoreType.DMA((4,)),
            pltpu.SemaphoreType.DMA((4,)),
            pltpu.SemaphoreType.DMA((2 * peers,)),
            pltpu.SemaphoreType.DMA((2 * peers,)),
        ],
        compiler_params=pltpu.CompilerParams(collective_id=1, has_side_effects=True),
    )(q, k, v, bias)


def on_device(queries, keys, values, block_mask, out_weight):
    tok_dev = queries.shape[0]
    frames_here = tok_dev // (TROWS * TCOLS * TILE)
    assert frames_here == 1 and queries.shape[1] == HEAD_DIM
    count = lax.axis_size("frame")
    frames_total = frames_here * count
    frame = lax.axis_index("frame") * frames_here
    mask_rows = block_mask.reshape(TROWS * TCOLS, WIN)
    bias = window_bias(mask_rows, frame, frames_total)
    got = attend(queries, keys, values, bias)
    core = lax.axis_index("frame") % 2
    side = lax.axis_index("hy")
    sides = lax.axis_size("hy")
    half = out_weight.shape[1] // 2
    partners = [(i, i ^ 1) for i in range(count)]
    weight_half = lax.dynamic_slice_in_dim(out_weight, core * half, half, axis=1)
    weight_half = lax.all_gather(weight_half, "hz", axis=0, tiled=True)
    peers = lax.axis_size("hz")
    mine = got.transpose(1, 0, 2).reshape(tok_dev // peers, peers * HEAD_DIM)
    block = mine.shape[0] // sides

    def project(x, which):
        rows = lax.dynamic_slice_in_dim(x, which * block, block, axis=0)
        return jnp.dot(rows, weight_half, preferred_element_type=jnp.float32)

    flip = [(0, 1), (1, 0)]
    theirs = lax.ppermute(mine, "frame", partners)
    partials = jnp.stack([project(mine, 1 - side), project(theirs, 1 - side)]).astype(jnp.bfloat16)
    sent_mine, sent_theirs = lax.ppermute(partials, "hy", flip)
    own_mine = lax.optimization_barrier(project(mine, side))
    own_theirs = lax.optimization_barrier(project(theirs, side))
    other = (own_theirs + sent_theirs.astype(jnp.float32)).astype(jnp.bfloat16)
    other_half = lax.ppermute(other, "frame", partners)
    own_half = (own_mine + sent_mine.astype(jnp.float32)).astype(jnp.bfloat16)
    return jnp.where(
        core == 0,
        jnp.concatenate([own_half, other_half], axis=1),
        jnp.concatenate([other_half, own_half], axis=1),
    )


def solution(mesh):
    frames, heads = mesh.devices.shape
    grid = mesh.devices.reshape(frames, 2, heads // 2)
    split = jax.sharding.Mesh(grid, ("frame", "hy", "hz"))
    head = ("hy", "hz")
    return jax.shard_map(
        on_device,
        mesh=split,
        in_specs=(
            P("frame", head),
            P("frame", head),
            P("frame", head),
            P(head, "frame", None, None),
            P(head, None),
        ),
        out_specs=P(("frame",) + head, None),
        check_vma=False,
    )
```

```python
import math

import numpy as np
import jax
import jax.numpy as jnp
from jax import lax
from jax.experimental import pallas as pl
from jax.experimental.pallas import tpu as pltpu
from jax.sharding import PartitionSpec as P

HEAD_DIM = 128
TROWS = 4
TCOLS = 8
WIN = 45
TILE = 64
QTILES = 2
KCOLS = 6
SEGS = 9
BLOCK_Q = QTILES * TILE
SEG_K = KCOLS * TILE
ROW_K = SEGS * SEG_K
GROUPS = TCOLS // QTILES


def window_tables():
    shape = (TROWS * GROUPS, QTILES, SEGS, KCOLS)
    qtile = np.zeros(shape, np.int32)
    offset = np.zeros(shape, np.int32)
    static_ok = np.zeros(shape, bool)
    centre = np.zeros(shape, bool)
    frame_step = np.zeros(shape, np.int32)
    for row in range(TROWS):
        for group in range(GROUPS):
            start = min(max(QTILES * group - 2, 0), TCOLS - KCOLS)
            for a in range(QTILES):
                col = QTILES * group + a
                for seg in range(SEGS):
                    df, dr = divmod(seg, 3)
                    for j in range(KCOLS):
                        dc = start + j - col
                        b = row * GROUPS + group
                        qtile[b, a, seg, j] = row * TCOLS + col
                        ok = abs(dc) <= 2 and 0 <= row + dr - 1 < TROWS
                        static_ok[b, a, seg, j] = ok
                        offset[b, a, seg, j] = 15 * df + 5 * dr + dc + 2 if ok else 0
                        centre[b, a, seg, j] = df == 1 and dr == 1 and dc == 0
                        frame_step[b, a, seg, j] = df - 1
    return qtile, offset, static_ok, centre, frame_step


def window_picks():
    picks = np.zeros((TCOLS, WIN, SEGS, KCOLS), np.float32)
    for col in range(TCOLS):
        start = min(max(QTILES * (col // QTILES) - 2, 0), TCOLS - KCOLS)
        for seg in range(SEGS):
            df, dr = divmod(seg, 3)
            for j in range(KCOLS):
                dc = start + j - col
                if abs(dc) <= 2:
                    picks[col, 15 * df + 5 * dr + dc + 2, seg, j] = 1.0
    return picks


def window_bias(mask_rows, frame, frames_total):
    qtile, offset, static_ok, centre, frame_step = window_tables()
    grid = mask_rows.astype(jnp.float32).reshape(TROWS, TCOLS, WIN)
    chosen = jnp.einsum("rcw,cwk->rck", grid, window_picks().reshape(TCOLS, WIN, SEGS * KCOLS))
    chosen = chosen.reshape(static_ok.shape) > 0.5
    key_frame = frame + frame_step
    inside = (key_frame >= 0) & (key_frame < frames_total)
    allowed = (chosen | centre) & static_ok & inside
    bias = jnp.where(allowed, 0.0, -jnp.inf).astype(jnp.float32)
    bias = jnp.broadcast_to(bias[..., None], bias.shape + (TILE,))
    return bias.reshape(TROWS * GROUPS, QTILES, ROW_K)


def attention_kernel(q_ref, k_ref, v_ref, bias_ref, o_ref,
                     kp_ref, kn_ref, vp_ref, vn_ref, s_ref, p_ref, att_ref, got_ref,
                     send_sem, recv_sem, out_send, out_recv):
    row = pl.program_id(0)
    group = pl.program_id(1)
    frame = lax.axis_index("frame")
    side = lax.axis_index("hy")
    me = lax.axis_index("hz")
    peers = lax.axis_size("hz")
    mesh = pl.DeviceIdType.MESH

    @pl.when((row == 0) & (group == 0))
    def _():
        count = lax.axis_size("frame")
        peer = me
        has_prev = frame > 0
        has_next = frame < count - 1
        prev_dev = (frame - 1, side, peer)
        next_dev = (frame + 1, side, peer)
        barrier = pltpu.get_barrier_semaphore()

        @pl.when(has_prev)
        def _():
            pl.semaphore_signal(barrier, inc=1, device_id=prev_dev, device_id_type=mesh)

        @pl.when(has_next)
        def _():
            pl.semaphore_signal(barrier, inc=1, device_id=next_dev, device_id_type=mesh)

        for i in range(1, peers):
            other = (frame, side, lax.rem(me + i, peers))
            pl.semaphore_signal(barrier, inc=1, device_id=other, device_id_type=mesh)

        @pl.when(has_prev & has_next)
        def _():
            pl.semaphore_wait(barrier, peers + 1)

        @pl.when(has_prev != has_next)
        def _():
            pl.semaphore_wait(barrier, peers)

        def push(src, dst, slot, device):
            return pltpu.make_async_remote_copy(
                src_ref=src, dst_ref=dst, send_sem=send_sem.at[slot], recv_sem=recv_sem.at[slot],
                device_id=device, device_id_type=mesh,
            )

        to_next = [push(k_ref, kp_ref, 0, next_dev), push(v_ref, vp_ref, 1, next_dev)]
        to_prev = [push(k_ref, kn_ref, 2, prev_dev), push(v_ref, vn_ref, 3, prev_dev)]

        @pl.when(has_next)
        def _():
            for copy in to_next:
                copy.start()

        @pl.when(has_prev)
        def _():
            for copy in to_prev:
                copy.start()

        @pl.when(has_prev)
        def _():
            for copy in to_prev:
                copy.wait_send()
            for copy in to_next:
                copy.wait_recv()

        @pl.when(has_next)
        def _():
            for copy in to_next:
                copy.wait_send()
            for copy in to_prev:
                copy.wait_recv()

        @pl.when(jnp.logical_not(has_prev))
        def _():
            kp_ref[...] = jnp.zeros_like(kp_ref)
            vp_ref[...] = jnp.zeros_like(vp_ref)

        @pl.when(jnp.logical_not(has_next))
        def _():
            kn_ref[...] = jnp.zeros_like(kn_ref)
            vn_ref[...] = jnp.zeros_like(vn_ref)

    start = jnp.clip(QTILES * group - 2, 0, TCOLS - KCOLS) * TILE
    key_refs = (kp_ref, k_ref, kn_ref)
    value_refs = (vp_ref, v_ref, vn_ref)
    q = q_ref[...]
    bases = []
    for seg in range(SEGS):
        df, dr = divmod(seg, 3)
        key_row = jnp.clip(row + dr - 1, 0, TROWS - 1)
        base = pl.multiple_of(key_row * (TCOLS * TILE) + start, TILE)
        bases.append(base)
        k = key_refs[df][pl.ds(base, SEG_K), :]
        s_ref[:, seg * SEG_K:(seg + 1) * SEG_K] = lax.dot_general(
            q, k, (((1,), (1,)), ((), ())), preferred_element_type=jnp.float32
        )
    scale = 1.0 / math.sqrt(HEAD_DIM)
    inverse = []
    for a in range(QTILES):
        rows = slice(a * TILE, (a + 1) * TILE)
        scores = s_ref[rows, :] + bias_ref[0, a:a + 1, :]
        peak = jnp.max(scores, axis=1, keepdims=True)
        expos = jnp.exp((scores - peak) * scale)
        inverse.append(1.0 / jnp.sum(expos, axis=1, keepdims=True))
        p_ref[rows, :] = expos.astype(jnp.bfloat16)
    acc = jnp.zeros((BLOCK_Q, HEAD_DIM), jnp.float32)
    for seg in range(SEGS):
        df, dr = divmod(seg, 3)
        v = value_refs[df][pl.ds(bases[seg], SEG_K), :]
        acc += jnp.dot(p_ref[:, seg * SEG_K:(seg + 1) * SEG_K], v,
                       preferred_element_type=jnp.float32)
    acc = acc * jnp.concatenate(inverse, axis=0)
    block = row * GROUPS + group
    att_ref[pl.ds(pl.multiple_of(block * BLOCK_Q, BLOCK_Q), BLOCK_Q), :] = (
        acc.astype(att_ref.dtype))
    chunk = got_ref.shape[1] // 2
    assert chunk == BLOCK_Q
    part = block // peers
    owner = block % peers
    distance = (owner - me + peers) % peers
    src = att_ref.at[pl.ds(pl.multiple_of(block * BLOCK_Q, BLOCK_Q), chunk)]

    def send(i, which, peer, source):
        return pltpu.make_async_remote_copy(
            src_ref=source,
            dst_ref=got_ref.at[me, pl.ds(pl.multiple_of(which * chunk, chunk), chunk)],
            send_sem=out_send.at[2 * i + which],
            recv_sem=out_recv.at[2 * i + which],
            device_id=(frame, side, peer),
            device_id_type=mesh,
        )

    @pl.when(distance == 0)
    def _():
        got_ref[me, pl.ds(pl.multiple_of(part * chunk, chunk), chunk), :] = src[...]

    @pl.when(distance != 0)
    def _():
        send(distance, part, owner, src).start()

    @pl.when((row == TROWS - 1) & (group == GROUPS - 1))
    def _():
        for i in range(1, peers):
            peer = lax.rem(me + i, peers)
            for which in range(2):
                send(i, which, peer, src).wait()
        o_ref[...] = got_ref[...]


def attend(q, k, v, bias):
    tokens = q.shape[0]
    full = pl.BlockSpec((tokens, HEAD_DIM), lambda r, g: (0, 0))
    frame_kv = pltpu.VMEM((tokens, HEAD_DIM), jnp.bfloat16)
    peers = lax.axis_size("hz")
    got_shape = (peers, tokens // peers, HEAD_DIM)
    got = pltpu.VMEM(got_shape, jnp.bfloat16)
    return pl.pallas_call(
        attention_kernel,
        grid=(TROWS, GROUPS),
        in_specs=[pl.BlockSpec((BLOCK_Q, HEAD_DIM), lambda r, g: (r * GROUPS + g, 0))]
        + [full] * 2
        + [pl.BlockSpec((1, QTILES, ROW_K), lambda r, g: (r * GROUPS + g, 0, 0))],
        out_specs=pl.BlockSpec(got_shape, lambda r, g: (0, 0, 0)),
        out_shape=jax.ShapeDtypeStruct(got_shape, jnp.bfloat16),
        scratch_shapes=[frame_kv] * 4 + [
            pltpu.VMEM((BLOCK_Q, ROW_K), jnp.float32),
            pltpu.VMEM((BLOCK_Q, ROW_K), jnp.bfloat16),
            frame_kv,
            got,
            pltpu.SemaphoreType.DMA((4,)),
            pltpu.SemaphoreType.DMA((4,)),
            pltpu.SemaphoreType.DMA((2 * peers,)),
            pltpu.SemaphoreType.DMA((2 * peers,)),
        ],
        compiler_params=pltpu.CompilerParams(collective_id=1, has_side_effects=True),
    )(q, k, v, bias)


def on_device(queries, keys, values, block_mask, out_weight):
    tok_dev = queries.shape[0]
    frames_here = tok_dev // (TROWS * TCOLS * TILE)
    assert frames_here == 1 and queries.shape[1] == HEAD_DIM
    count = lax.axis_size("frame")
    frames_total = frames_here * count
    frame = lax.axis_index("frame") * frames_here
    mask_rows = block_mask.reshape(TROWS * TCOLS, WIN)
    bias = window_bias(mask_rows, frame, frames_total)
    got = attend(queries, keys, values, bias)
    core = lax.axis_index("frame") % 2
    side = lax.axis_index("hy")
    sides = lax.axis_size("hy")
    half = out_weight.shape[1] // 2
    partners = [(i, i ^ 1) for i in range(count)]
    weight_half = lax.dynamic_slice_in_dim(out_weight, core * half, half, axis=1)
    weight_half = lax.all_gather(weight_half, "hz", axis=0, tiled=True)
    peers = lax.axis_size("hz")
    mine = got.transpose(1, 0, 2).reshape(tok_dev // peers, peers * HEAD_DIM)
    block = mine.shape[0] // sides

    def project(x, which):
        rows = lax.dynamic_slice_in_dim(x, which * block, block, axis=0)
        return jnp.dot(rows, weight_half, preferred_element_type=jnp.float32)

    flip = [(0, 1), (1, 0)]
    theirs = lax.ppermute(mine, "frame", partners)
    partials = jnp.stack([project(mine, 1 - side), project(theirs, 1 - side)]).astype(jnp.bfloat16)
    sent_mine, sent_theirs = lax.ppermute(partials, "hy", flip)
    own_mine = lax.optimization_barrier(project(mine, side))
    own_theirs = lax.optimization_barrier(project(theirs, side))
    other = (own_theirs + sent_theirs.astype(jnp.float32)).astype(jnp.bfloat16)
    other_half = lax.ppermute(other, "frame", partners)
    own_half = (own_mine + sent_mine.astype(jnp.float32)).astype(jnp.bfloat16)
    return jnp.where(
        core == 0,
        jnp.concatenate([own_half, other_half], axis=1),
        jnp.concatenate([other_half, own_half], axis=1),
    )


def solution(mesh):
    frames, heads = mesh.devices.shape
    grid = mesh.devices.reshape(frames, 2, heads // 2)
    split = jax.sharding.Mesh(grid, ("frame", "hy", "hz"))
    head = ("hy", "hz")
    return jax.shard_map(
        on_device,
        mesh=split,
        in_specs=(
            P("frame", head),
            P("frame", head),
            P("frame", head),
            P(head, "frame", None, None),
            P(head, None),
        ),
        out_specs=P(("frame",) + head, None),
        check_vma=False,
    )
```

```python
import math

import numpy as np
import jax
import jax.numpy as jnp
from jax import lax
from jax.experimental import pallas as pl
from jax.experimental.pallas import tpu as pltpu
from jax.sharding import PartitionSpec as P

HEAD_DIM = 128
TROWS = 4
TCOLS = 8
WIN = 45
TILE = 64
QTILES = 2
KCOLS = 6
SEGS = 9
BLOCK_Q = QTILES * TILE
SEG_K = KCOLS * TILE
ROW_K = SEGS * SEG_K
GROUPS = TCOLS // QTILES


def window_tables():
    shape = (TROWS * GROUPS, QTILES, SEGS, KCOLS)
    qtile = np.zeros(shape, np.int32)
    offset = np.zeros(shape, np.int32)
    static_ok = np.zeros(shape, bool)
    centre = np.zeros(shape, bool)
    frame_step = np.zeros(shape, np.int32)
    for row in range(TROWS):
        for group in range(GROUPS):
            start = min(max(QTILES * group - 2, 0), TCOLS - KCOLS)
            for a in range(QTILES):
                col = QTILES * group + a
                for seg in range(SEGS):
                    df, dr = divmod(seg, 3)
                    for j in range(KCOLS):
                        dc = start + j - col
                        b = row * GROUPS + group
                        qtile[b, a, seg, j] = row * TCOLS + col
                        ok = abs(dc) <= 2 and 0 <= row + dr - 1 < TROWS
                        static_ok[b, a, seg, j] = ok
                        offset[b, a, seg, j] = 15 * df + 5 * dr + dc + 2 if ok else 0
                        centre[b, a, seg, j] = df == 1 and dr == 1 and dc == 0
                        frame_step[b, a, seg, j] = df - 1
    return qtile, offset, static_ok, centre, frame_step


def window_picks():
    picks = np.zeros((TCOLS, WIN, SEGS, KCOLS), np.float32)
    for col in range(TCOLS):
        start = min(max(QTILES * (col // QTILES) - 2, 0), TCOLS - KCOLS)
        for seg in range(SEGS):
            df, dr = divmod(seg, 3)
            for j in range(KCOLS):
                dc = start + j - col
                if abs(dc) <= 2:
                    picks[col, 15 * df + 5 * dr + dc + 2, seg, j] = 1.0
    return picks


def window_bias(mask_rows, frame, frames_total):
    qtile, offset, static_ok, centre, frame_step = window_tables()
    grid = mask_rows.astype(jnp.float32).reshape(TROWS, TCOLS, WIN)
    chosen = jnp.einsum("rcw,cwk->rck", grid, window_picks().reshape(TCOLS, WIN, SEGS * KCOLS))
    chosen = chosen.reshape(static_ok.shape) > 0.5
    key_frame = frame + frame_step
    inside = (key_frame >= 0) & (key_frame < frames_total)
    allowed = (chosen | centre) & static_ok & inside
    bias = jnp.where(allowed, 0.0, -jnp.inf).astype(jnp.float32)
    bias = jnp.broadcast_to(bias[..., None], bias.shape + (TILE,))
    return bias.reshape(TROWS * GROUPS, QTILES, ROW_K)


def attention_kernel(q_ref, k_ref, v_ref, bias_ref, o_ref,
                     kp_ref, kn_ref, vp_ref, vn_ref, s_ref, p_ref, att_ref, got_ref,
                     send_sem, recv_sem, out_send, out_recv):
    row = pl.program_id(0)
    group = pl.program_id(1)
    frame = lax.axis_index("frame")
    side = lax.axis_index("hy")
    me = lax.axis_index("hz")
    peers = lax.axis_size("hz")
    mesh = pl.DeviceIdType.MESH

    @pl.when((row == 0) & (group == 0))
    def _():
        count = lax.axis_size("frame")
        peer = me
        has_prev = frame > 0
        has_next = frame < count - 1
        prev_dev = (frame - 1, side, peer)
        next_dev = (frame + 1, side, peer)
        barrier = pltpu.get_barrier_semaphore()

        @pl.when(has_prev)
        def _():
            pl.semaphore_signal(barrier, inc=1, device_id=prev_dev, device_id_type=mesh)

        @pl.when(has_next)
        def _():
            pl.semaphore_signal(barrier, inc=1, device_id=next_dev, device_id_type=mesh)

        for i in range(1, peers):
            other = (frame, side, lax.rem(me + i, peers))
            pl.semaphore_signal(barrier, inc=1, device_id=other, device_id_type=mesh)

        @pl.when(has_prev & has_next)
        def _():
            pl.semaphore_wait(barrier, peers + 1)

        @pl.when(has_prev != has_next)
        def _():
            pl.semaphore_wait(barrier, peers)

        def push(src, dst, slot, device):
            return pltpu.make_async_remote_copy(
                src_ref=src, dst_ref=dst, send_sem=send_sem.at[slot], recv_sem=recv_sem.at[slot],
                device_id=device, device_id_type=mesh,
            )

        to_next = [push(k_ref, kp_ref, 0, next_dev), push(v_ref, vp_ref, 1, next_dev)]
        to_prev = [push(k_ref, kn_ref, 2, prev_dev), push(v_ref, vn_ref, 3, prev_dev)]

        @pl.when(has_next)
        def _():
            for copy in to_next:
                copy.start()

        @pl.when(has_prev)
        def _():
            for copy in to_prev:
                copy.start()

        @pl.when(has_prev)
        def _():
            for copy in to_prev:
                copy.wait_send()
            for copy in to_next:
                copy.wait_recv()

        @pl.when(has_next)
        def _():
            for copy in to_next:
                copy.wait_send()
            for copy in to_prev:
                copy.wait_recv()

        @pl.when(jnp.logical_not(has_prev))
        def _():
            kp_ref[...] = jnp.zeros_like(kp_ref)
            vp_ref[...] = jnp.zeros_like(vp_ref)

        @pl.when(jnp.logical_not(has_next))
        def _():
            kn_ref[...] = jnp.zeros_like(kn_ref)
            vn_ref[...] = jnp.zeros_like(vn_ref)

    start = jnp.clip(QTILES * group - 2, 0, TCOLS - KCOLS) * TILE
    key_refs = (kp_ref, k_ref, kn_ref)
    value_refs = (vp_ref, v_ref, vn_ref)
    q = q_ref[...]
    bases = []
    for seg in range(SEGS):
        df, dr = divmod(seg, 3)
        key_row = jnp.clip(row + dr - 1, 0, TROWS - 1)
        base = pl.multiple_of(key_row * (TCOLS * TILE) + start, TILE)
        bases.append(base)
        k = key_refs[df][pl.ds(base, SEG_K), :]
        s_ref[:, seg * SEG_K:(seg + 1) * SEG_K] = lax.dot_general(
            q, k, (((1,), (1,)), ((), ())), preferred_element_type=jnp.float32
        )
    scale = 1.0 / math.sqrt(HEAD_DIM)
    inverse = []
    for a in range(QTILES):
        rows = slice(a * TILE, (a + 1) * TILE)
        scores = s_ref[rows, :] + bias_ref[0, a:a + 1, :]
        peak = jnp.max(scores, axis=1, keepdims=True)
        expos = jnp.exp((scores - peak) * scale)
        inverse.append(1.0 / jnp.sum(expos, axis=1, keepdims=True))
        p_ref[rows, :] = expos.astype(jnp.bfloat16)
    acc = jnp.zeros((BLOCK_Q, HEAD_DIM), jnp.float32)
    for seg in range(SEGS):
        df, dr = divmod(seg, 3)
        v = value_refs[df][pl.ds(bases[seg], SEG_K), :]
        acc += jnp.dot(p_ref[:, seg * SEG_K:(seg + 1) * SEG_K], v,
                       preferred_element_type=jnp.float32)
    acc = acc * jnp.concatenate(inverse, axis=0)
    block = row * GROUPS + group
    att_ref[pl.ds(pl.multiple_of(block * BLOCK_Q, BLOCK_Q), BLOCK_Q), :] = (
        acc.astype(att_ref.dtype))
    chunk = got_ref.shape[1] // 2
    assert chunk == BLOCK_Q
    part = block // peers
    owner = block % peers
    distance = (owner - me + peers) % peers
    src = att_ref.at[pl.ds(pl.multiple_of(block * BLOCK_Q, BLOCK_Q), chunk)]

    def send(i, which, peer, source):
        return pltpu.make_async_remote_copy(
            src_ref=source,
            dst_ref=got_ref.at[me, pl.ds(pl.multiple_of(which * chunk, chunk), chunk)],
            send_sem=out_send.at[2 * i + which],
            recv_sem=out_recv.at[2 * i + which],
            device_id=(frame, side, peer),
            device_id_type=mesh,
        )

    @pl.when(distance == 0)
    def _():
        got_ref[me, pl.ds(pl.multiple_of(part * chunk, chunk), chunk), :] = src[...]

    @pl.when(distance != 0)
    def _():
        send(distance, part, owner, src).start()

    @pl.when((row == TROWS - 1) & (group == GROUPS - 1))
    def _():
        for i in range(1, peers):
            peer = lax.rem(me + i, peers)
            for which in range(2):
                send(i, which, peer, src).wait()
        o_ref[...] = got_ref[...]


def attend(q, k, v, bias):
    tokens = q.shape[0]
    full = pl.BlockSpec((tokens, HEAD_DIM), lambda r, g: (0, 0))
    frame_kv = pltpu.VMEM((tokens, HEAD_DIM), jnp.bfloat16)
    peers = lax.axis_size("hz")
    got_shape = (peers, tokens // peers, HEAD_DIM)
    got = pltpu.VMEM(got_shape, jnp.bfloat16)
    return pl.pallas_call(
        attention_kernel,
        grid=(TROWS, GROUPS),
        in_specs=[pl.BlockSpec((BLOCK_Q, HEAD_DIM), lambda r, g: (r * GROUPS + g, 0))]
        + [full] * 2
        + [pl.BlockSpec((1, QTILES, ROW_K), lambda r, g: (r * GROUPS + g, 0, 0))],
        out_specs=pl.BlockSpec(got_shape, lambda r, g: (0, 0, 0)),
        out_shape=jax.ShapeDtypeStruct(got_shape, jnp.bfloat16),
        scratch_shapes=[frame_kv] * 4 + [
            pltpu.VMEM((BLOCK_Q, ROW_K), jnp.float32),
            pltpu.VMEM((BLOCK_Q, ROW_K), jnp.bfloat16),
            frame_kv,
            got,
            pltpu.SemaphoreType.DMA((4,)),
            pltpu.SemaphoreType.DMA((4,)),
            pltpu.SemaphoreType.DMA((2 * peers,)),
            pltpu.SemaphoreType.DMA((2 * peers,)),
        ],
        compiler_params=pltpu.CompilerParams(collective_id=1, has_side_effects=True),
    )(q, k, v, bias)


def on_device(queries, keys, values, block_mask, out_weight):
    tok_dev = queries.shape[0]
    frames_here = tok_dev // (TROWS * TCOLS * TILE)
    assert frames_here == 1 and queries.shape[1] == HEAD_DIM
    count = lax.axis_size("frame")
    frames_total = frames_here * count
    frame = lax.axis_index("frame") * frames_here
    mask_rows = block_mask.reshape(TROWS * TCOLS, WIN)
    bias = window_bias(mask_rows, frame, frames_total)
    got = attend(queries, keys, values, bias)
    core = lax.axis_index("frame") % 2
    side = lax.axis_index("hy")
    sides = lax.axis_size("hy")
    half = out_weight.shape[1] // 2
    partners = [(i, i ^ 1) for i in range(count)]
    quarter = half // 2
    weights = [
        lax.all_gather(
            lax.dynamic_slice_in_dim(out_weight, core * half + k * quarter, quarter, axis=1),
            "hz", axis=0, tiled=True)
        for k in range(2)
    ]
    peers = lax.axis_size("hz")
    mine = got.transpose(1, 0, 2).reshape(tok_dev // peers, peers * HEAD_DIM)
    block = mine.shape[0] // sides

    def project(x, which, weight):
        rows = lax.dynamic_slice_in_dim(x, which * block, block, axis=0)
        return jnp.dot(rows, weight, preferred_element_type=jnp.float32)

    flip = [(0, 1), (1, 0)]
    theirs = lax.ppermute(mine, "frame", partners)
    own_parts, other_parts = [], []
    for weight in weights:
        partials = jnp.stack([project(mine, 1 - side, weight), project(theirs, 1 - side, weight)])
        sent_mine, sent_theirs = lax.ppermute(partials.astype(jnp.bfloat16), "hy", flip)
        own_mine = lax.optimization_barrier(project(mine, side, weight))
        own_theirs = lax.optimization_barrier(project(theirs, side, weight))
        other_parts.append((own_theirs + sent_theirs.astype(jnp.float32)).astype(jnp.bfloat16))
        own_parts.append((own_mine + sent_mine.astype(jnp.float32)).astype(jnp.bfloat16))
    other_half = lax.ppermute(jnp.concatenate(other_parts, axis=1), "frame", partners)
    own_half = jnp.concatenate(own_parts, axis=1)
    return jnp.where(
        core == 0,
        jnp.concatenate([own_half, other_half], axis=1),
        jnp.concatenate([other_half, own_half], axis=1),
    )


def solution(mesh):
    frames, heads = mesh.devices.shape
    grid = mesh.devices.reshape(frames, 2, heads // 2)
    split = jax.sharding.Mesh(grid, ("frame", "hy", "hz"))
    head = ("hy", "hz")
    return jax.shard_map(
        on_device,
        mesh=split,
        in_specs=(
            P("frame", head),
            P("frame", head),
            P("frame", head),
            P(head, "frame", None, None),
            P(head, None),
        ),
        out_specs=P(("frame",) + head, None),
        check_vma=False,
    )
```

```python
import math

import numpy as np
import jax
import jax.numpy as jnp
from jax import lax
from jax.experimental import pallas as pl
from jax.experimental.pallas import tpu as pltpu
from jax.sharding import PartitionSpec as P

HEAD_DIM = 128
TROWS = 4
TCOLS = 8
WIN = 45
TILE = 64
QTILES = 2
KCOLS = 6
SEGS = 9
BLOCK_Q = QTILES * TILE
SEG_K = KCOLS * TILE
ROW_K = SEGS * SEG_K
GROUPS = TCOLS // QTILES


def window_tables():
    shape = (TROWS * GROUPS, QTILES, SEGS, KCOLS)
    qtile = np.zeros(shape, np.int32)
    offset = np.zeros(shape, np.int32)
    static_ok = np.zeros(shape, bool)
    centre = np.zeros(shape, bool)
    frame_step = np.zeros(shape, np.int32)
    for row in range(TROWS):
        for group in range(GROUPS):
            start = min(max(QTILES * group - 2, 0), TCOLS - KCOLS)
            for a in range(QTILES):
                col = QTILES * group + a
                for seg in range(SEGS):
                    df, dr = divmod(seg, 3)
                    for j in range(KCOLS):
                        dc = start + j - col
                        b = row * GROUPS + group
                        qtile[b, a, seg, j] = row * TCOLS + col
                        ok = abs(dc) <= 2 and 0 <= row + dr - 1 < TROWS
                        static_ok[b, a, seg, j] = ok
                        offset[b, a, seg, j] = 15 * df + 5 * dr + dc + 2 if ok else 0
                        centre[b, a, seg, j] = df == 1 and dr == 1 and dc == 0
                        frame_step[b, a, seg, j] = df - 1
    return qtile, offset, static_ok, centre, frame_step


def window_picks():
    picks = np.zeros((TCOLS, WIN, SEGS, KCOLS), np.float32)
    for col in range(TCOLS):
        start = min(max(QTILES * (col // QTILES) - 2, 0), TCOLS - KCOLS)
        for seg in range(SEGS):
            df, dr = divmod(seg, 3)
            for j in range(KCOLS):
                dc = start + j - col
                if abs(dc) <= 2:
                    picks[col, 15 * df + 5 * dr + dc + 2, seg, j] = 1.0
    return picks


def window_bias(mask_rows, frame, frames_total):
    qtile, offset, static_ok, centre, frame_step = window_tables()
    grid = mask_rows.astype(jnp.float32).reshape(TROWS, TCOLS, WIN)
    chosen = jnp.einsum("rcw,cwk->rck", grid, window_picks().reshape(TCOLS, WIN, SEGS * KCOLS))
    chosen = chosen.reshape(static_ok.shape) > 0.5
    key_frame = frame + frame_step
    inside = (key_frame >= 0) & (key_frame < frames_total)
    allowed = (chosen | centre) & static_ok & inside
    bias = jnp.where(allowed, 0.0, -jnp.inf).astype(jnp.float32)
    bias = jnp.broadcast_to(bias[..., None], bias.shape + (TILE,))
    return bias.reshape(TROWS * GROUPS, QTILES, ROW_K)


def attention_kernel(q_ref, k_ref, v_ref, bias_ref, w_ref, o_ref, ow_ref,
                     kp_ref, kn_ref, vp_ref, vn_ref, s_ref, p_ref, att_ref, got_ref, wall_ref,
                     send_sem, recv_sem, out_send, out_recv, w_send, w_recv):
    row = pl.program_id(0)
    group = pl.program_id(1)
    frame = lax.axis_index("frame")
    side = lax.axis_index("hy")
    me = lax.axis_index("hz")
    peers = lax.axis_size("hz")
    mesh = pl.DeviceIdType.MESH

    def weight_copy(i):
        return pltpu.make_async_remote_copy(
            src_ref=w_ref, dst_ref=wall_ref.at[me], send_sem=w_send.at[i], recv_sem=w_recv.at[i],
            device_id=(frame, side, lax.rem(me + i, peers)), device_id_type=mesh,
        )

    @pl.when((row == 0) & (group == 0))
    def _():
        count = lax.axis_size("frame")
        peer = me
        has_prev = frame > 0
        has_next = frame < count - 1
        prev_dev = (frame - 1, side, peer)
        next_dev = (frame + 1, side, peer)
        barrier = pltpu.get_barrier_semaphore()

        @pl.when(has_prev)
        def _():
            pl.semaphore_signal(barrier, inc=1, device_id=prev_dev, device_id_type=mesh)

        @pl.when(has_next)
        def _():
            pl.semaphore_signal(barrier, inc=1, device_id=next_dev, device_id_type=mesh)

        for i in range(1, peers):
            other = (frame, side, lax.rem(me + i, peers))
            pl.semaphore_signal(barrier, inc=1, device_id=other, device_id_type=mesh)

        @pl.when(has_prev & has_next)
        def _():
            pl.semaphore_wait(barrier, peers + 1)

        @pl.when(has_prev != has_next)
        def _():
            pl.semaphore_wait(barrier, peers)

        def push(src, dst, slot, device):
            return pltpu.make_async_remote_copy(
                src_ref=src, dst_ref=dst, send_sem=send_sem.at[slot], recv_sem=recv_sem.at[slot],
                device_id=device, device_id_type=mesh,
            )

        to_next = [push(k_ref, kp_ref, 0, next_dev), push(v_ref, vp_ref, 1, next_dev)]
        to_prev = [push(k_ref, kn_ref, 2, prev_dev), push(v_ref, vn_ref, 3, prev_dev)]

        @pl.when(has_next)
        def _():
            for copy in to_next:
                copy.start()

        @pl.when(has_prev)
        def _():
            for copy in to_prev:
                copy.start()

        @pl.when(has_prev)
        def _():
            for copy in to_prev:
                copy.wait_send()
            for copy in to_next:
                copy.wait_recv()

        @pl.when(has_next)
        def _():
            for copy in to_next:
                copy.wait_send()
            for copy in to_prev:
                copy.wait_recv()

        for i in range(1, peers):
            weight_copy(i).start()
        wall_ref[me] = w_ref[...]

        @pl.when(jnp.logical_not(has_prev))
        def _():
            kp_ref[...] = jnp.zeros_like(kp_ref)
            vp_ref[...] = jnp.zeros_like(vp_ref)

        @pl.when(jnp.logical_not(has_next))
        def _():
            kn_ref[...] = jnp.zeros_like(kn_ref)
            vn_ref[...] = jnp.zeros_like(vn_ref)

    start = jnp.clip(QTILES * group - 2, 0, TCOLS - KCOLS) * TILE
    key_refs = (kp_ref, k_ref, kn_ref)
    value_refs = (vp_ref, v_ref, vn_ref)
    q = q_ref[...]
    bases = []
    for seg in range(SEGS):
        df, dr = divmod(seg, 3)
        key_row = jnp.clip(row + dr - 1, 0, TROWS - 1)
        base = pl.multiple_of(key_row * (TCOLS * TILE) + start, TILE)
        bases.append(base)
        k = key_refs[df][pl.ds(base, SEG_K), :]
        s_ref[:, seg * SEG_K:(seg + 1) * SEG_K] = lax.dot_general(
            q, k, (((1,), (1,)), ((), ())), preferred_element_type=jnp.float32
        )
    scale = 1.0 / math.sqrt(HEAD_DIM)
    inverse = []
    for a in range(QTILES):
        rows = slice(a * TILE, (a + 1) * TILE)
        scores = s_ref[rows, :] + bias_ref[0, a:a + 1, :]
        peak = jnp.max(scores, axis=1, keepdims=True)
        expos = jnp.exp((scores - peak) * scale)
        inverse.append(1.0 / jnp.sum(expos, axis=1, keepdims=True))
        p_ref[rows, :] = expos.astype(jnp.bfloat16)
    acc = jnp.zeros((BLOCK_Q, HEAD_DIM), jnp.float32)
    for seg in range(SEGS):
        df, dr = divmod(seg, 3)
        v = value_refs[df][pl.ds(bases[seg], SEG_K), :]
        acc += jnp.dot(p_ref[:, seg * SEG_K:(seg + 1) * SEG_K], v,
                       preferred_element_type=jnp.float32)
    acc = acc * jnp.concatenate(inverse, axis=0)
    block = row * GROUPS + group
    att_ref[pl.ds(pl.multiple_of(block * BLOCK_Q, BLOCK_Q), BLOCK_Q), :] = (
        acc.astype(att_ref.dtype))
    chunk = got_ref.shape[1] // 2
    assert chunk == BLOCK_Q
    part = block // peers
    owner = block % peers
    distance = (owner - me + peers) % peers
    src = att_ref.at[pl.ds(pl.multiple_of(block * BLOCK_Q, BLOCK_Q), chunk)]

    def send(i, which, peer, source):
        return pltpu.make_async_remote_copy(
            src_ref=source,
            dst_ref=got_ref.at[me, pl.ds(pl.multiple_of(which * chunk, chunk), chunk)],
            send_sem=out_send.at[2 * i + which],
            recv_sem=out_recv.at[2 * i + which],
            device_id=(frame, side, peer),
            device_id_type=mesh,
        )

    @pl.when(distance == 0)
    def _():
        got_ref[me, pl.ds(pl.multiple_of(part * chunk, chunk), chunk), :] = src[...]

    @pl.when(distance != 0)
    def _():
        send(distance, part, owner, src).start()

    @pl.when((row == TROWS - 1) & (group == GROUPS - 1))
    def _():
        for i in range(1, peers):
            peer = lax.rem(me + i, peers)
            for which in range(2):
                send(i, which, peer, src).wait()
        for i in range(1, peers):
            weight_copy(i).wait()
        o_ref[...] = got_ref[...]
        ow_ref[...] = wall_ref[...]


def attend(q, k, v, bias, weight):
    tokens = q.shape[0]
    full = pl.BlockSpec((tokens, HEAD_DIM), lambda r, g: (0, 0))
    frame_kv = pltpu.VMEM((tokens, HEAD_DIM), jnp.bfloat16)
    peers = lax.axis_size("hz")
    got_shape = (peers, tokens // peers, HEAD_DIM)
    got = pltpu.VMEM(got_shape, jnp.bfloat16)
    wall_shape = (peers,) + weight.shape
    return pl.pallas_call(
        attention_kernel,
        grid=(TROWS, GROUPS),
        in_specs=[pl.BlockSpec((BLOCK_Q, HEAD_DIM), lambda r, g: (r * GROUPS + g, 0))]
        + [full] * 2
        + [pl.BlockSpec((1, QTILES, ROW_K), lambda r, g: (r * GROUPS + g, 0, 0)),
           pl.BlockSpec(weight.shape, lambda r, g: (0, 0))],
        out_specs=[pl.BlockSpec(got_shape, lambda r, g: (0, 0, 0)),
                   pl.BlockSpec(wall_shape, lambda r, g: (0, 0, 0))],
        out_shape=[jax.ShapeDtypeStruct(got_shape, jnp.bfloat16),
                   jax.ShapeDtypeStruct(wall_shape, weight.dtype)],
        scratch_shapes=[frame_kv] * 4 + [
            pltpu.VMEM((BLOCK_Q, ROW_K), jnp.float32),
            pltpu.VMEM((BLOCK_Q, ROW_K), jnp.bfloat16),
            frame_kv,
            got,
            pltpu.VMEM(wall_shape, weight.dtype),
            pltpu.SemaphoreType.DMA((4,)),
            pltpu.SemaphoreType.DMA((4,)),
            pltpu.SemaphoreType.DMA((2 * peers,)),
            pltpu.SemaphoreType.DMA((2 * peers,)),
            pltpu.SemaphoreType.DMA((peers,)),
            pltpu.SemaphoreType.DMA((peers,)),
        ],
        compiler_params=pltpu.CompilerParams(collective_id=1, has_side_effects=True),
    )(q, k, v, bias, weight)


def on_device(queries, keys, values, block_mask, out_weight):
    tok_dev = queries.shape[0]
    frames_here = tok_dev // (TROWS * TCOLS * TILE)
    assert frames_here == 1 and queries.shape[1] == HEAD_DIM
    count = lax.axis_size("frame")
    frames_total = frames_here * count
    frame = lax.axis_index("frame") * frames_here
    mask_rows = block_mask.reshape(TROWS * TCOLS, WIN)
    bias = window_bias(mask_rows, frame, frames_total)
    core = lax.axis_index("frame") % 2
    half = out_weight.shape[1] // 2
    weight_rows = lax.dynamic_slice_in_dim(out_weight, core * half, half, axis=1)
    got, weight_all = attend(queries, keys, values, bias, weight_rows)
    core = lax.axis_index("frame") % 2
    side = lax.axis_index("hy")
    sides = lax.axis_size("hy")
    half = out_weight.shape[1] // 2
    partners = [(i, i ^ 1) for i in range(count)]
    weight_half = weight_all.reshape(-1, half)
    peers = lax.axis_size("hz")
    mine = got.transpose(1, 0, 2).reshape(tok_dev // peers, peers * HEAD_DIM)
    block = mine.shape[0] // sides

    def project(x, which):
        rows = lax.dynamic_slice_in_dim(x, which * block, block, axis=0)
        return jnp.dot(rows, weight_half, preferred_element_type=jnp.float32)

    flip = [(0, 1), (1, 0)]
    theirs = lax.ppermute(mine, "frame", partners)
    partials = jnp.stack([project(mine, 1 - side), project(theirs, 1 - side)]).astype(jnp.bfloat16)
    sent_mine, sent_theirs = lax.ppermute(partials, "hy", flip)
    own_mine = lax.optimization_barrier(project(mine, side))
    own_theirs = lax.optimization_barrier(project(theirs, side))
    other = (own_theirs + sent_theirs.astype(jnp.float32)).astype(jnp.bfloat16)
    other_half = lax.ppermute(other, "frame", partners)
    own_half = (own_mine + sent_mine.astype(jnp.float32)).astype(jnp.bfloat16)
    return jnp.where(
        core == 0,
        jnp.concatenate([own_half, other_half], axis=1),
        jnp.concatenate([other_half, own_half], axis=1),
    )


def solution(mesh):
    frames, heads = mesh.devices.shape
    grid = mesh.devices.reshape(frames, 2, heads // 2)
    split = jax.sharding.Mesh(grid, ("frame", "hy", "hz"))
    head = ("hy", "hz")
    return jax.shard_map(
        on_device,
        mesh=split,
        in_specs=(
            P("frame", head),
            P("frame", head),
            P("frame", head),
            P(head, "frame", None, None),
            P(head, None),
        ),
        out_specs=P(("frame",) + head, None),
        check_vma=False,
    )
```

```python
import math

import numpy as np
import jax
import jax.numpy as jnp
from jax import lax
from jax.experimental import pallas as pl
from jax.experimental.pallas import tpu as pltpu
from jax.sharding import PartitionSpec as P

HEAD_DIM = 128
TROWS = 4
TCOLS = 8
WIN = 45
TILE = 64
QTILES = 2
KCOLS = 6
SEGS = 9
BLOCK_Q = QTILES * TILE
SEG_K = KCOLS * TILE
ROW_K = SEGS * SEG_K
GROUPS = TCOLS // QTILES


def window_tables():
    shape = (TROWS * GROUPS, QTILES, SEGS, KCOLS)
    qtile = np.zeros(shape, np.int32)
    offset = np.zeros(shape, np.int32)
    static_ok = np.zeros(shape, bool)
    centre = np.zeros(shape, bool)
    frame_step = np.zeros(shape, np.int32)
    for row in range(TROWS):
        for group in range(GROUPS):
            start = min(max(QTILES * group - 2, 0), TCOLS - KCOLS)
            for a in range(QTILES):
                col = QTILES * group + a
                for seg in range(SEGS):
                    df, dr = divmod(seg, 3)
                    for j in range(KCOLS):
                        dc = start + j - col
                        b = row * GROUPS + group
                        qtile[b, a, seg, j] = row * TCOLS + col
                        ok = abs(dc) <= 2 and 0 <= row + dr - 1 < TROWS
                        static_ok[b, a, seg, j] = ok
                        offset[b, a, seg, j] = 15 * df + 5 * dr + dc + 2 if ok else 0
                        centre[b, a, seg, j] = df == 1 and dr == 1 and dc == 0
                        frame_step[b, a, seg, j] = df - 1
    return qtile, offset, static_ok, centre, frame_step


def window_picks():
    picks = np.zeros((TCOLS, WIN, SEGS, KCOLS), np.float32)
    for col in range(TCOLS):
        start = min(max(QTILES * (col // QTILES) - 2, 0), TCOLS - KCOLS)
        for seg in range(SEGS):
            df, dr = divmod(seg, 3)
            for j in range(KCOLS):
                dc = start + j - col
                if abs(dc) <= 2:
                    picks[col, 15 * df + 5 * dr + dc + 2, seg, j] = 1.0
    return picks


def window_bias(mask_rows, frame, frames_total):
    qtile, offset, static_ok, centre, frame_step = window_tables()
    grid = mask_rows.astype(jnp.float32).reshape(TROWS, TCOLS, WIN)
    chosen = jnp.einsum("rcw,cwk->rck", grid, window_picks().reshape(TCOLS, WIN, SEGS * KCOLS))
    chosen = chosen.reshape(static_ok.shape) > 0.5
    key_frame = frame + frame_step
    inside = (key_frame >= 0) & (key_frame < frames_total)
    allowed = (chosen | centre) & static_ok & inside
    bias = jnp.where(allowed, 0.0, -jnp.inf).astype(jnp.float32)
    bias = jnp.broadcast_to(bias[..., None], bias.shape + (TILE,))
    return bias.reshape(TROWS * GROUPS, QTILES, ROW_K)


def attention_kernel(q_ref, k_ref, v_ref, bias_ref, o_ref,
                     kp_ref, kn_ref, vp_ref, vn_ref, s_ref, p_ref, att_ref, got_ref,
                     send_sem, recv_sem, out_send, out_recv):
    row = pl.program_id(0)
    group = pl.program_id(1)
    frame = lax.axis_index("frame")
    side = lax.axis_index("hy")
    me = lax.axis_index("hz")
    peers = lax.axis_size("hz")
    mesh = pl.DeviceIdType.MESH

    @pl.when((row == 0) & (group == 0))
    def _():
        count = lax.axis_size("frame")
        peer = me
        has_prev = frame > 0
        has_next = frame < count - 1
        prev_dev = (frame - 1, side, peer)
        next_dev = (frame + 1, side, peer)
        barrier = pltpu.get_barrier_semaphore()

        @pl.when(has_prev)
        def _():
            pl.semaphore_signal(barrier, inc=1, device_id=prev_dev, device_id_type=mesh)

        @pl.when(has_next)
        def _():
            pl.semaphore_signal(barrier, inc=1, device_id=next_dev, device_id_type=mesh)

        for i in range(1, peers):
            other = (frame, side, lax.rem(me + i, peers))
            pl.semaphore_signal(barrier, inc=1, device_id=other, device_id_type=mesh)

        @pl.when(has_prev & has_next)
        def _():
            pl.semaphore_wait(barrier, peers + 1)

        @pl.when(has_prev != has_next)
        def _():
            pl.semaphore_wait(barrier, peers)

        def push(src, dst, slot, device):
            return pltpu.make_async_remote_copy(
                src_ref=src, dst_ref=dst, send_sem=send_sem.at[slot], recv_sem=recv_sem.at[slot],
                device_id=device, device_id_type=mesh,
            )

        to_next = [push(k_ref, kp_ref, 0, next_dev), push(v_ref, vp_ref, 1, next_dev)]
        to_prev = [push(k_ref, kn_ref, 2, prev_dev), push(v_ref, vn_ref, 3, prev_dev)]

        @pl.when(has_next)
        def _():
            for copy in to_next:
                copy.start()

        @pl.when(has_prev)
        def _():
            for copy in to_prev:
                copy.start()

        @pl.when(has_prev)
        def _():
            for copy in to_prev:
                copy.wait_send()
            for copy in to_next:
                copy.wait_recv()

        @pl.when(has_next)
        def _():
            for copy in to_next:
                copy.wait_send()
            for copy in to_prev:
                copy.wait_recv()

        @pl.when(jnp.logical_not(has_prev))
        def _():
            kp_ref[...] = jnp.zeros_like(kp_ref)
            vp_ref[...] = jnp.zeros_like(vp_ref)

        @pl.when(jnp.logical_not(has_next))
        def _():
            kn_ref[...] = jnp.zeros_like(kn_ref)
            vn_ref[...] = jnp.zeros_like(vn_ref)

    start = jnp.clip(QTILES * group - 2, 0, TCOLS - KCOLS) * TILE
    key_refs = (kp_ref, k_ref, kn_ref)
    value_refs = (vp_ref, v_ref, vn_ref)
    q = q_ref[...]
    bases = []
    for seg in range(SEGS):
        df, dr = divmod(seg, 3)
        key_row = jnp.clip(row + dr - 1, 0, TROWS - 1)
        base = pl.multiple_of(key_row * (TCOLS * TILE) + start, TILE)
        bases.append(base)
        k = key_refs[df][pl.ds(base, SEG_K), :]
        s_ref[:, seg * SEG_K:(seg + 1) * SEG_K] = lax.dot_general(
            q, k, (((1,), (1,)), ((), ())), preferred_element_type=jnp.float32
        )
    scale = 1.0 / math.sqrt(HEAD_DIM)
    inverse = []
    for a in range(QTILES):
        rows = slice(a * TILE, (a + 1) * TILE)
        scores = s_ref[rows, :] + bias_ref[0, a:a + 1, :]
        peak = jnp.max(scores, axis=1, keepdims=True)
        expos = jnp.exp((scores - peak) * scale)
        inverse.append(1.0 / jnp.sum(expos, axis=1, keepdims=True))
        p_ref[rows, :] = expos.astype(jnp.bfloat16)
    acc = jnp.zeros((BLOCK_Q, HEAD_DIM), jnp.float32)
    for seg in range(SEGS):
        df, dr = divmod(seg, 3)
        v = value_refs[df][pl.ds(bases[seg], SEG_K), :]
        acc += jnp.dot(p_ref[:, seg * SEG_K:(seg + 1) * SEG_K], v,
                       preferred_element_type=jnp.float32)
    acc = acc * jnp.concatenate(inverse, axis=0)
    block = row * GROUPS + group
    att_ref[pl.ds(pl.multiple_of(block * BLOCK_Q, BLOCK_Q), BLOCK_Q), :] = (
        acc.astype(att_ref.dtype))
    chunk = got_ref.shape[1] // 2
    assert chunk == BLOCK_Q
    part = block // peers
    owner = block % peers
    distance = (owner - me + peers) % peers
    src = att_ref.at[pl.ds(pl.multiple_of(block * BLOCK_Q, BLOCK_Q), chunk)]

    def send(i, which, peer, source):
        return pltpu.make_async_remote_copy(
            src_ref=source,
            dst_ref=got_ref.at[me, pl.ds(pl.multiple_of(which * chunk, chunk), chunk)],
            send_sem=out_send.at[2 * i + which],
            recv_sem=out_recv.at[2 * i + which],
            device_id=(frame, side, peer),
            device_id_type=mesh,
        )

    @pl.when(distance == 0)
    def _():
        got_ref[me, pl.ds(pl.multiple_of(part * chunk, chunk), chunk), :] = src[...]

    @pl.when(distance != 0)
    def _():
        send(distance, part, owner, src).start()

    @pl.when((row == TROWS - 1) & (group == GROUPS - 1))
    def _():
        for i in range(1, peers):
            peer = lax.rem(me + i, peers)
            for which in range(2):
                send(i, which, peer, src).wait()
        o_ref[...] = got_ref[...]


def attend(q, k, v, bias):
    tokens = q.shape[0]
    full = pl.BlockSpec((tokens, HEAD_DIM), lambda r, g: (0, 0))
    frame_kv = pltpu.VMEM((tokens, HEAD_DIM), jnp.bfloat16)
    peers = lax.axis_size("hz")
    got_shape = (peers, tokens // peers, HEAD_DIM)
    got = pltpu.VMEM(got_shape, jnp.bfloat16)
    return pl.pallas_call(
        attention_kernel,
        grid=(TROWS, GROUPS),
        in_specs=[pl.BlockSpec((BLOCK_Q, HEAD_DIM), lambda r, g: (r * GROUPS + g, 0))]
        + [full] * 2
        + [pl.BlockSpec((1, QTILES, ROW_K), lambda r, g: (r * GROUPS + g, 0, 0))],
        out_specs=pl.BlockSpec(got_shape, lambda r, g: (0, 0, 0)),
        out_shape=jax.ShapeDtypeStruct(got_shape, jnp.bfloat16),
        scratch_shapes=[frame_kv] * 4 + [
            pltpu.VMEM((BLOCK_Q, ROW_K), jnp.float32),
            pltpu.VMEM((BLOCK_Q, ROW_K), jnp.bfloat16),
            frame_kv,
            got,
            pltpu.SemaphoreType.DMA((4,)),
            pltpu.SemaphoreType.DMA((4,)),
            pltpu.SemaphoreType.DMA((2 * peers,)),
            pltpu.SemaphoreType.DMA((2 * peers,)),
        ],
        compiler_params=pltpu.CompilerParams(collective_id=1, has_side_effects=True),
    )(q, k, v, bias)


def on_device(queries, keys, values, block_mask, out_weight):
    tok_dev = queries.shape[0]
    frames_here = tok_dev // (TROWS * TCOLS * TILE)
    assert frames_here == 1 and queries.shape[1] == HEAD_DIM
    count = lax.axis_size("frame")
    frames_total = frames_here * count
    frame = lax.axis_index("frame") * frames_here
    mask_rows = block_mask.reshape(TROWS * TCOLS, WIN)
    bias = window_bias(mask_rows, frame, frames_total)
    got = attend(queries, keys, values, bias)
    core = lax.axis_index("frame") % 2
    side = lax.axis_index("hy")
    sides = lax.axis_size("hy")
    half = out_weight.shape[1] // 2
    partners = [(i, i ^ 1) for i in range(count)]
    weight_half = lax.dynamic_slice_in_dim(out_weight, core * half, half, axis=1)
    weight_half = lax.all_gather(weight_half, "hz", axis=0, tiled=True)
    peers = lax.axis_size("hz")
    mine = got.transpose(1, 0, 2).reshape(tok_dev // peers, peers * HEAD_DIM)
    block = mine.shape[0] // sides

    def project(x, which):
        rows = lax.dynamic_slice_in_dim(x, which * block, block, axis=0)
        return jnp.dot(rows, weight_half, preferred_element_type=jnp.float32)

    flip = [(0, 1), (1, 0)]
    theirs = lax.ppermute(mine, "frame", partners)
    sent_mine = lax.ppermute(project(mine, 1 - side).astype(jnp.bfloat16), "hy", flip)
    diagonal = [(f * sides + h, (f ^ 1) * sides + (sides - 1 - h)) for f in range(count) for h in range(sides)]
    sent_cross = lax.ppermute(project(theirs, 1 - side).astype(jnp.bfloat16), ("frame", "hy"), diagonal)
    own_mine = lax.optimization_barrier(project(mine, side))
    from_partner = lax.ppermute(project(theirs, side), "frame", partners)
    other_half = (from_partner + sent_cross.astype(jnp.float32)).astype(jnp.bfloat16)
    own_half = (own_mine + sent_mine.astype(jnp.float32)).astype(jnp.bfloat16)
    return jnp.where(
        core == 0,
        jnp.concatenate([own_half, other_half], axis=1),
        jnp.concatenate([other_half, own_half], axis=1),
    )


def solution(mesh):
    frames, heads = mesh.devices.shape
    grid = mesh.devices.reshape(frames, 2, heads // 2)
    split = jax.sharding.Mesh(grid, ("frame", "hy", "hz"))
    head = ("hy", "hz")
    return jax.shard_map(
        on_device,
        mesh=split,
        in_specs=(
            P("frame", head),
            P("frame", head),
            P("frame", head),
            P(head, "frame", None, None),
            P(head, None),
        ),
        out_specs=P(("frame",) + head, None),
        check_vma=False,
    )
```

```python
import math

import numpy as np
import jax
import jax.numpy as jnp
from jax import lax
from jax.experimental import pallas as pl
from jax.experimental.pallas import tpu as pltpu
from jax.sharding import PartitionSpec as P

HEAD_DIM = 128
TROWS = 4
TCOLS = 8
WIN = 45
TILE = 64
QTILES = 2
KCOLS = 6
SEGS = 9
BLOCK_Q = QTILES * TILE
SEG_K = KCOLS * TILE
ROW_K = SEGS * SEG_K
GROUPS = TCOLS // QTILES


def window_tables():
    shape = (TROWS * GROUPS, QTILES, SEGS, KCOLS)
    qtile = np.zeros(shape, np.int32)
    offset = np.zeros(shape, np.int32)
    static_ok = np.zeros(shape, bool)
    centre = np.zeros(shape, bool)
    frame_step = np.zeros(shape, np.int32)
    for row in range(TROWS):
        for group in range(GROUPS):
            start = min(max(QTILES * group - 2, 0), TCOLS - KCOLS)
            for a in range(QTILES):
                col = QTILES * group + a
                for seg in range(SEGS):
                    df, dr = divmod(seg, 3)
                    for j in range(KCOLS):
                        dc = start + j - col
                        b = row * GROUPS + group
                        qtile[b, a, seg, j] = row * TCOLS + col
                        ok = abs(dc) <= 2 and 0 <= row + dr - 1 < TROWS
                        static_ok[b, a, seg, j] = ok
                        offset[b, a, seg, j] = 15 * df + 5 * dr + dc + 2 if ok else 0
                        centre[b, a, seg, j] = df == 1 and dr == 1 and dc == 0
                        frame_step[b, a, seg, j] = df - 1
    return qtile, offset, static_ok, centre, frame_step


def window_picks():
    picks = np.zeros((TCOLS, WIN, SEGS, KCOLS), np.float32)
    for col in range(TCOLS):
        start = min(max(QTILES * (col // QTILES) - 2, 0), TCOLS - KCOLS)
        for seg in range(SEGS):
            df, dr = divmod(seg, 3)
            for j in range(KCOLS):
                dc = start + j - col
                if abs(dc) <= 2:
                    picks[col, 15 * df + 5 * dr + dc + 2, seg, j] = 1.0
    return picks


def window_bias(mask_rows, frame, frames_total):
    qtile, offset, static_ok, centre, frame_step = window_tables()
    grid = mask_rows.astype(jnp.float32).reshape(TROWS, TCOLS, WIN)
    chosen = jnp.einsum("rcw,cwk->rck", grid, window_picks().reshape(TCOLS, WIN, SEGS * KCOLS))
    chosen = chosen.reshape(static_ok.shape) > 0.5
    key_frame = frame + frame_step
    inside = (key_frame >= 0) & (key_frame < frames_total)
    allowed = (chosen | centre) & static_ok & inside
    bias = jnp.where(allowed, 0.0, -jnp.inf).astype(jnp.float32)
    bias = jnp.broadcast_to(bias[..., None], bias.shape + (TILE,))
    return bias.reshape(TROWS * GROUPS, QTILES, ROW_K)


def attention_kernel(q_ref, k_ref, v_ref, bias_ref, o_ref,
                     kp_ref, kn_ref, vp_ref, vn_ref, s_ref, p_ref, att_ref, got_ref,
                     send_sem, recv_sem, out_send, out_recv):
    row = pl.program_id(0)
    group = pl.program_id(1)
    frame = lax.axis_index("frame")
    side = lax.axis_index("hy")
    me = lax.axis_index("hz")
    peers = lax.axis_size("hz")
    mesh = pl.DeviceIdType.MESH

    @pl.when((row == 0) & (group == 0))
    def _():
        count = lax.axis_size("frame")
        peer = me
        has_prev = frame > 0
        has_next = frame < count - 1
        prev_dev = (frame - 1, side, peer)
        next_dev = (frame + 1, side, peer)
        barrier = pltpu.get_barrier_semaphore()

        @pl.when(has_prev)
        def _():
            pl.semaphore_signal(barrier, inc=1, device_id=prev_dev, device_id_type=mesh)

        @pl.when(has_next)
        def _():
            pl.semaphore_signal(barrier, inc=1, device_id=next_dev, device_id_type=mesh)

        for i in range(1, peers):
            other = (frame, side, lax.rem(me + i, peers))
            pl.semaphore_signal(barrier, inc=1, device_id=other, device_id_type=mesh)

        @pl.when(has_prev & has_next)
        def _():
            pl.semaphore_wait(barrier, peers + 1)

        @pl.when(has_prev != has_next)
        def _():
            pl.semaphore_wait(barrier, peers)

        def push(src, dst, slot, device):
            return pltpu.make_async_remote_copy(
                src_ref=src, dst_ref=dst, send_sem=send_sem.at[slot], recv_sem=recv_sem.at[slot],
                device_id=device, device_id_type=mesh,
            )

        to_next = [push(k_ref, kp_ref, 0, next_dev), push(v_ref, vp_ref, 1, next_dev)]
        to_prev = [push(k_ref, kn_ref, 2, prev_dev), push(v_ref, vn_ref, 3, prev_dev)]

        @pl.when(has_next)
        def _():
            for copy in to_next:
                copy.start()

        @pl.when(has_prev)
        def _():
            for copy in to_prev:
                copy.start()

        @pl.when(has_prev)
        def _():
            for copy in to_prev:
                copy.wait_send()
            for copy in to_next:
                copy.wait_recv()

        @pl.when(has_next)
        def _():
            for copy in to_next:
                copy.wait_send()
            for copy in to_prev:
                copy.wait_recv()

        @pl.when(jnp.logical_not(has_prev))
        def _():
            kp_ref[...] = jnp.zeros_like(kp_ref)
            vp_ref[...] = jnp.zeros_like(vp_ref)

        @pl.when(jnp.logical_not(has_next))
        def _():
            kn_ref[...] = jnp.zeros_like(kn_ref)
            vn_ref[...] = jnp.zeros_like(vn_ref)

    start = jnp.clip(QTILES * group - 2, 0, TCOLS - KCOLS) * TILE
    key_refs = (kp_ref, k_ref, kn_ref)
    value_refs = (vp_ref, v_ref, vn_ref)
    q = q_ref[...]
    bases = []
    for seg in range(SEGS):
        df, dr = divmod(seg, 3)
        key_row = jnp.clip(row + dr - 1, 0, TROWS - 1)
        base = pl.multiple_of(key_row * (TCOLS * TILE) + start, TILE)
        bases.append(base)
        k = key_refs[df][pl.ds(base, SEG_K), :]
        s_ref[:, seg * SEG_K:(seg + 1) * SEG_K] = lax.dot_general(
            q, k, (((1,), (1,)), ((), ())), preferred_element_type=jnp.float32
        )
    scale = 1.0 / math.sqrt(HEAD_DIM)
    inverse = []
    for a in range(QTILES):
        rows = slice(a * TILE, (a + 1) * TILE)
        scores = s_ref[rows, :] + bias_ref[0, a:a + 1, :]
        peak = jnp.max(scores, axis=1, keepdims=True)
        expos = jnp.exp((scores - peak) * scale)
        inverse.append(1.0 / jnp.sum(expos, axis=1, keepdims=True))
        p_ref[rows, :] = expos.astype(jnp.bfloat16)
    acc = jnp.zeros((BLOCK_Q, HEAD_DIM), jnp.float32)
    for seg in range(SEGS):
        df, dr = divmod(seg, 3)
        v = value_refs[df][pl.ds(bases[seg], SEG_K), :]
        acc += jnp.dot(p_ref[:, seg * SEG_K:(seg + 1) * SEG_K], v,
                       preferred_element_type=jnp.float32)
    acc = acc * jnp.concatenate(inverse, axis=0)
    block = row * GROUPS + group
    att_ref[pl.ds(pl.multiple_of(block * BLOCK_Q, BLOCK_Q), BLOCK_Q), :] = (
        acc.astype(att_ref.dtype))
    chunk = got_ref.shape[1] // 2
    assert chunk == BLOCK_Q
    part = block // peers
    owner = block % peers
    distance = (owner - me + peers) % peers
    src = att_ref.at[pl.ds(pl.multiple_of(block * BLOCK_Q, BLOCK_Q), chunk)]

    def send(i, which, peer, source):
        return pltpu.make_async_remote_copy(
            src_ref=source,
            dst_ref=got_ref.at[me, pl.ds(pl.multiple_of(which * chunk, chunk), chunk)],
            send_sem=out_send.at[2 * i + which],
            recv_sem=out_recv.at[2 * i + which],
            device_id=(frame, side, peer),
            device_id_type=mesh,
        )

    @pl.when(distance == 0)
    def _():
        got_ref[me, pl.ds(pl.multiple_of(part * chunk, chunk), chunk), :] = src[...]

    @pl.when(distance != 0)
    def _():
        send(distance, part, owner, src).start()

    @pl.when((row == TROWS - 1) & (group == GROUPS - 1))
    def _():
        for i in range(1, peers):
            peer = lax.rem(me + i, peers)
            for which in range(2):
                send(i, which, peer, src).wait()
        o_ref[...] = got_ref[...]


def attend(q, k, v, bias):
    tokens = q.shape[0]
    full = pl.BlockSpec((tokens, HEAD_DIM), lambda r, g: (0, 0))
    frame_kv = pltpu.VMEM((tokens, HEAD_DIM), jnp.bfloat16)
    peers = lax.axis_size("hz")
    got_shape = (peers, tokens // peers, HEAD_DIM)
    got = pltpu.VMEM(got_shape, jnp.bfloat16)
    return pl.pallas_call(
        attention_kernel,
        grid=(TROWS, GROUPS),
        in_specs=[pl.BlockSpec((BLOCK_Q, HEAD_DIM), lambda r, g: (r * GROUPS + g, 0))]
        + [full] * 2
        + [pl.BlockSpec((1, QTILES, ROW_K), lambda r, g: (r * GROUPS + g, 0, 0))],
        out_specs=pl.BlockSpec(got_shape, lambda r, g: (0, 0, 0)),
        out_shape=jax.ShapeDtypeStruct(got_shape, jnp.bfloat16),
        scratch_shapes=[frame_kv] * 4 + [
            pltpu.VMEM((BLOCK_Q, ROW_K), jnp.float32),
            pltpu.VMEM((BLOCK_Q, ROW_K), jnp.bfloat16),
            frame_kv,
            got,
            pltpu.SemaphoreType.DMA((4,)),
            pltpu.SemaphoreType.DMA((4,)),
            pltpu.SemaphoreType.DMA((2 * peers,)),
            pltpu.SemaphoreType.DMA((2 * peers,)),
        ],
        compiler_params=pltpu.CompilerParams(collective_id=1, has_side_effects=True),
    )(q, k, v, bias)


def half_kernel(w_ref, o_ref, sem):
    core = lax.axis_index("frame") % 2
    half = o_ref.shape[1]
    copy = pltpu.make_async_copy(w_ref.at[:, pl.ds(pl.multiple_of(core * half, 128), half)], o_ref, sem)
    copy.start()
    copy.wait()


def column_half(w):
    return pl.pallas_call(
        half_kernel,
        out_shape=jax.ShapeDtypeStruct((w.shape[0], w.shape[1] // 2), w.dtype),
        in_specs=[pl.BlockSpec(memory_space=pl.ANY)],
        out_specs=pl.BlockSpec(memory_space=pl.ANY),
        scratch_shapes=[pltpu.SemaphoreType.DMA(())],
    )(w)


def on_device(queries, keys, values, block_mask, out_weight):
    tok_dev = queries.shape[0]
    frames_here = tok_dev // (TROWS * TCOLS * TILE)
    assert frames_here == 1 and queries.shape[1] == HEAD_DIM
    count = lax.axis_size("frame")
    frames_total = frames_here * count
    frame = lax.axis_index("frame") * frames_here
    mask_rows = block_mask.reshape(TROWS * TCOLS, WIN)
    bias = window_bias(mask_rows, frame, frames_total)
    got = attend(queries, keys, values, bias)
    core = lax.axis_index("frame") % 2
    side = lax.axis_index("hy")
    sides = lax.axis_size("hy")
    half = out_weight.shape[1] // 2
    partners = [(i, i ^ 1) for i in range(count)]
    weight_half = column_half(out_weight)
    weight_half = lax.all_gather(weight_half, "hz", axis=0, tiled=True)
    peers = lax.axis_size("hz")
    mine = got.transpose(1, 0, 2).reshape(tok_dev // peers, peers * HEAD_DIM)
    block = mine.shape[0] // sides

    def project(x, which):
        rows = lax.dynamic_slice_in_dim(x, which * block, block, axis=0)
        return jnp.dot(rows, weight_half, preferred_element_type=jnp.float32)

    flip = [(0, 1), (1, 0)]
    theirs = lax.ppermute(mine, "frame", partners)
    sent_mine = lax.ppermute(project(mine, 1 - side).astype(jnp.bfloat16), "hy", flip)
    diagonal = [(f * sides + h, (f ^ 1) * sides + (sides - 1 - h)) for f in range(count) for h in range(sides)]
    sent_cross = lax.ppermute(project(theirs, 1 - side).astype(jnp.bfloat16), ("frame", "hy"), diagonal)
    own_mine = lax.optimization_barrier(project(mine, side))
    from_partner = lax.ppermute(project(theirs, side), "frame", partners)
    other_half = (from_partner + sent_cross.astype(jnp.float32)).astype(jnp.bfloat16)
    own_half = (own_mine + sent_mine.astype(jnp.float32)).astype(jnp.bfloat16)
    return jnp.where(
        core == 0,
        jnp.concatenate([own_half, other_half], axis=1),
        jnp.concatenate([other_half, own_half], axis=1),
    )


def solution(mesh):
    frames, heads = mesh.devices.shape
    grid = mesh.devices.reshape(frames, 2, heads // 2)
    split = jax.sharding.Mesh(grid, ("frame", "hy", "hz"))
    head = ("hy", "hz")
    return jax.shard_map(
        on_device,
        mesh=split,
        in_specs=(
            P("frame", head),
            P("frame", head),
            P("frame", head),
            P(head, "frame", None, None),
            P(head, None),
        ),
        out_specs=P(("frame",) + head, None),
        check_vma=False,
    )
```

```python
import math

import numpy as np
import jax
import jax.numpy as jnp
from jax import lax
from jax.experimental import pallas as pl
from jax.experimental.pallas import tpu as pltpu
from jax.sharding import PartitionSpec as P

HEAD_DIM = 128
TROWS = 4
TCOLS = 8
WIN = 45
TILE = 64
QTILES = 2
KCOLS = 6
SEGS = 9
BLOCK_Q = QTILES * TILE
SEG_K = KCOLS * TILE
ROW_K = SEGS * SEG_K
GROUPS = TCOLS // QTILES


def window_tables():
    shape = (TROWS * GROUPS, QTILES, SEGS, KCOLS)
    qtile = np.zeros(shape, np.int32)
    offset = np.zeros(shape, np.int32)
    static_ok = np.zeros(shape, bool)
    centre = np.zeros(shape, bool)
    frame_step = np.zeros(shape, np.int32)
    for row in range(TROWS):
        for group in range(GROUPS):
            start = min(max(QTILES * group - 2, 0), TCOLS - KCOLS)
            for a in range(QTILES):
                col = QTILES * group + a
                for seg in range(SEGS):
                    df, dr = divmod(seg, 3)
                    for j in range(KCOLS):
                        dc = start + j - col
                        b = row * GROUPS + group
                        qtile[b, a, seg, j] = row * TCOLS + col
                        ok = abs(dc) <= 2 and 0 <= row + dr - 1 < TROWS
                        static_ok[b, a, seg, j] = ok
                        offset[b, a, seg, j] = 15 * df + 5 * dr + dc + 2 if ok else 0
                        centre[b, a, seg, j] = df == 1 and dr == 1 and dc == 0
                        frame_step[b, a, seg, j] = df - 1
    return qtile, offset, static_ok, centre, frame_step


def window_picks():
    picks = np.zeros((TCOLS, WIN, SEGS, KCOLS), np.float32)
    for col in range(TCOLS):
        start = min(max(QTILES * (col // QTILES) - 2, 0), TCOLS - KCOLS)
        for seg in range(SEGS):
            df, dr = divmod(seg, 3)
            for j in range(KCOLS):
                dc = start + j - col
                if abs(dc) <= 2:
                    picks[col, 15 * df + 5 * dr + dc + 2, seg, j] = 1.0
    return picks


def window_bias(mask_rows, frame, frames_total):
    qtile, offset, static_ok, centre, frame_step = window_tables()
    grid = mask_rows.astype(jnp.float32).reshape(TROWS, TCOLS, WIN)
    chosen = jnp.einsum("rcw,cwk->rck", grid, window_picks().reshape(TCOLS, WIN, SEGS * KCOLS))
    chosen = chosen.reshape(static_ok.shape) > 0.5
    key_frame = frame + frame_step
    inside = (key_frame >= 0) & (key_frame < frames_total)
    allowed = (chosen | centre) & static_ok & inside
    bias = jnp.where(allowed, 0.0, -jnp.inf).astype(jnp.float32)
    bias = jnp.broadcast_to(bias[..., None], bias.shape + (TILE,))
    return bias.reshape(TROWS * GROUPS, QTILES, ROW_K)


def attention_kernel(q_ref, k_ref, v_ref, bias_ref, o_ref,
                     kp_ref, kn_ref, vp_ref, vn_ref, s_ref, p_ref, att_ref, got_ref,
                     send_sem, recv_sem, out_send, out_recv):
    row = pl.program_id(0)
    group = pl.program_id(1)
    frame = lax.axis_index("frame")
    side = lax.axis_index("hy")
    me = lax.axis_index("hz")
    peers = lax.axis_size("hz")
    mesh = pl.DeviceIdType.MESH

    @pl.when((row == 0) & (group == 0))
    def _():
        count = lax.axis_size("frame")
        peer = me
        has_prev = frame > 0
        has_next = frame < count - 1
        prev_dev = (frame - 1, side, peer)
        next_dev = (frame + 1, side, peer)
        barrier = pltpu.get_barrier_semaphore()

        @pl.when(has_prev)
        def _():
            pl.semaphore_signal(barrier, inc=1, device_id=prev_dev, device_id_type=mesh)

        @pl.when(has_next)
        def _():
            pl.semaphore_signal(barrier, inc=1, device_id=next_dev, device_id_type=mesh)

        for i in range(1, peers):
            other = (frame, side, lax.rem(me + i, peers))
            pl.semaphore_signal(barrier, inc=1, device_id=other, device_id_type=mesh)

        @pl.when(has_prev & has_next)
        def _():
            pl.semaphore_wait(barrier, peers + 1)

        @pl.when(has_prev != has_next)
        def _():
            pl.semaphore_wait(barrier, peers)

        def push(src, dst, slot, device):
            return pltpu.make_async_remote_copy(
                src_ref=src, dst_ref=dst, send_sem=send_sem.at[slot], recv_sem=recv_sem.at[slot],
                device_id=device, device_id_type=mesh,
            )

        to_next = [push(k_ref, kp_ref, 0, next_dev), push(v_ref, vp_ref, 1, next_dev)]
        to_prev = [push(k_ref, kn_ref, 2, prev_dev), push(v_ref, vn_ref, 3, prev_dev)]

        @pl.when(has_next)
        def _():
            for copy in to_next:
                copy.start()

        @pl.when(has_prev)
        def _():
            for copy in to_prev:
                copy.start()

        @pl.when(has_prev)
        def _():
            for copy in to_prev:
                copy.wait_send()
            for copy in to_next:
                copy.wait_recv()

        @pl.when(has_next)
        def _():
            for copy in to_next:
                copy.wait_send()
            for copy in to_prev:
                copy.wait_recv()

        @pl.when(jnp.logical_not(has_prev))
        def _():
            kp_ref[...] = jnp.zeros_like(kp_ref)
            vp_ref[...] = jnp.zeros_like(vp_ref)

        @pl.when(jnp.logical_not(has_next))
        def _():
            kn_ref[...] = jnp.zeros_like(kn_ref)
            vn_ref[...] = jnp.zeros_like(vn_ref)

    start = jnp.clip(QTILES * group - 2, 0, TCOLS - KCOLS) * TILE
    key_refs = (kp_ref, k_ref, kn_ref)
    value_refs = (vp_ref, v_ref, vn_ref)
    q = q_ref[...]
    bases = []
    for seg in range(SEGS):
        df, dr = divmod(seg, 3)
        key_row = jnp.clip(row + dr - 1, 0, TROWS - 1)
        base = pl.multiple_of(key_row * (TCOLS * TILE) + start, TILE)
        bases.append(base)
        k = key_refs[df][pl.ds(base, SEG_K), :]
        s_ref[:, seg * SEG_K:(seg + 1) * SEG_K] = lax.dot_general(
            q, k, (((1,), (1,)), ((), ())), preferred_element_type=jnp.float32
        )
    scale = 1.0 / math.sqrt(HEAD_DIM)
    inverse = []
    for a in range(QTILES):
        rows = slice(a * TILE, (a + 1) * TILE)
        scores = s_ref[rows, :] + bias_ref[0, a:a + 1, :]
        peak = jnp.max(scores, axis=1, keepdims=True)
        expos = jnp.exp((scores - peak) * scale)
        inverse.append(1.0 / jnp.sum(expos, axis=1, keepdims=True))
        p_ref[rows, :] = expos.astype(jnp.bfloat16)
    acc = jnp.zeros((BLOCK_Q, HEAD_DIM), jnp.float32)
    for seg in range(SEGS):
        df, dr = divmod(seg, 3)
        v = value_refs[df][pl.ds(bases[seg], SEG_K), :]
        acc += jnp.dot(p_ref[:, seg * SEG_K:(seg + 1) * SEG_K], v,
                       preferred_element_type=jnp.float32)
    acc = acc * jnp.concatenate(inverse, axis=0)
    block = row * GROUPS + group
    att_ref[pl.ds(pl.multiple_of(block * BLOCK_Q, BLOCK_Q), BLOCK_Q), :] = (
        acc.astype(att_ref.dtype))
    chunk = got_ref.shape[1] // 2
    assert chunk == BLOCK_Q
    part = block // peers
    owner = block % peers
    distance = (owner - me + peers) % peers
    src = att_ref.at[pl.ds(pl.multiple_of(block * BLOCK_Q, BLOCK_Q), chunk)]

    def send(i, which, peer, source):
        return pltpu.make_async_remote_copy(
            src_ref=source,
            dst_ref=got_ref.at[me, pl.ds(pl.multiple_of(which * chunk, chunk), chunk)],
            send_sem=out_send.at[2 * i + which],
            recv_sem=out_recv.at[2 * i + which],
            device_id=(frame, side, peer),
            device_id_type=mesh,
        )

    @pl.when(distance == 0)
    def _():
        got_ref[me, pl.ds(pl.multiple_of(part * chunk, chunk), chunk), :] = src[...]

    @pl.when(distance != 0)
    def _():
        send(distance, part, owner, src).start()

    @pl.when((row == TROWS - 1) & (group == GROUPS - 1))
    def _():
        for i in range(1, peers):
            peer = lax.rem(me + i, peers)
            for which in range(2):
                send(i, which, peer, src).wait()
        o_ref[...] = got_ref[...]


def attend(q, k, v, bias):
    tokens = q.shape[0]
    full = pl.BlockSpec((tokens, HEAD_DIM), lambda r, g: (0, 0))
    frame_kv = pltpu.VMEM((tokens, HEAD_DIM), jnp.bfloat16)
    peers = lax.axis_size("hz")
    got_shape = (peers, tokens // peers, HEAD_DIM)
    got = pltpu.VMEM(got_shape, jnp.bfloat16)
    return pl.pallas_call(
        attention_kernel,
        grid=(TROWS, GROUPS),
        in_specs=[pl.BlockSpec((BLOCK_Q, HEAD_DIM), lambda r, g: (r * GROUPS + g, 0))]
        + [full] * 2
        + [pl.BlockSpec((1, QTILES, ROW_K), lambda r, g: (r * GROUPS + g, 0, 0))],
        out_specs=pl.BlockSpec(got_shape, lambda r, g: (0, 0, 0)),
        out_shape=jax.ShapeDtypeStruct(got_shape, jnp.bfloat16),
        scratch_shapes=[frame_kv] * 4 + [
            pltpu.VMEM((BLOCK_Q, ROW_K), jnp.float32),
            pltpu.VMEM((BLOCK_Q, ROW_K), jnp.bfloat16),
            frame_kv,
            got,
            pltpu.SemaphoreType.DMA((4,)),
            pltpu.SemaphoreType.DMA((4,)),
            pltpu.SemaphoreType.DMA((2 * peers,)),
            pltpu.SemaphoreType.DMA((2 * peers,)),
        ],
        compiler_params=pltpu.CompilerParams(collective_id=1, has_side_effects=True),
    )(q, k, v, bias)


def on_device(queries, keys, values, block_mask, out_weight):
    tok_dev = queries.shape[0]
    frames_here = tok_dev // (TROWS * TCOLS * TILE)
    assert frames_here == 1 and queries.shape[1] == HEAD_DIM
    count = lax.axis_size("frame")
    frames_total = frames_here * count
    frame = lax.axis_index("frame") * frames_here
    mask_rows = block_mask.reshape(TROWS * TCOLS, WIN)
    bias = window_bias(mask_rows, frame, frames_total)
    got = attend(queries, keys, values, bias)
    core = lax.axis_index("frame") % 2
    side = lax.axis_index("hy")
    sides = lax.axis_size("hy")
    half = out_weight.shape[1] // 2
    partners = [(i, i ^ 1) for i in range(count)]
    weight_half = lax.dynamic_slice_in_dim(out_weight, core * half, half, axis=1)
    weight_half = lax.all_gather(weight_half, "hz", axis=0, tiled=True)
    peers = lax.axis_size("hz")
    mine = got.transpose(1, 0, 2).reshape(tok_dev // peers, peers * HEAD_DIM)
    block = mine.shape[0] // sides

    def project(x, which):
        rows = lax.dynamic_slice_in_dim(x, which * block, block, axis=0)
        return jnp.dot(rows, weight_half, preferred_element_type=jnp.float32)

    flip = [(0, 1), (1, 0)]
    theirs = lax.ppermute(mine, "frame", partners)
    away = lambda x: lax.dynamic_slice_in_dim(x, (1 - side) * block, block, axis=0)
    both = jnp.dot(jnp.concatenate([away(mine), away(theirs)]), weight_half,
                   preferred_element_type=jnp.float32).astype(jnp.bfloat16)
    sent_mine = lax.ppermute(both[:block], "hy", flip)
    diagonal = [(f * sides + h, (f ^ 1) * sides + (sides - 1 - h)) for f in range(count) for h in range(sides)]
    sent_cross = lax.ppermute(both[block:], ("frame", "hy"), diagonal)
    own_mine = lax.optimization_barrier(project(mine, side))
    from_partner = lax.ppermute(project(theirs, side), "frame", partners)
    other_half = (from_partner + sent_cross.astype(jnp.float32)).astype(jnp.bfloat16)
    own_half = (own_mine + sent_mine.astype(jnp.float32)).astype(jnp.bfloat16)
    return jnp.where(
        core == 0,
        jnp.concatenate([own_half, other_half], axis=1),
        jnp.concatenate([other_half, own_half], axis=1),
    )


def solution(mesh):
    frames, heads = mesh.devices.shape
    grid = mesh.devices.reshape(frames, 2, heads // 2)
    split = jax.sharding.Mesh(grid, ("frame", "hy", "hz"))
    head = ("hy", "hz")
    return jax.shard_map(
        on_device,
        mesh=split,
        in_specs=(
            P("frame", head),
            P("frame", head),
            P("frame", head),
            P(head, "frame", None, None),
            P(head, None),
        ),
        out_specs=P(("frame",) + head, None),
        check_vma=False,
    )
```
